512 devices in a mesh: grp: 8 (over y, core), tile: 64 (over x, z).
Axes of the slice: x: 4, y: 4, z: 16, core: 2. Of those that a mesh axis runs over, the one named last changes fastest.
Arguments:
- level_set: float32 [2560, 40960], P('grp', 'tile'), may hold values from -8 to 8
- fuel: int32 [2560, 40960], P('grp', 'tile'), may hold values from 0 to 12
- wind: float32 [2, 128, 2048], P(None, 'grp', 'tile'), may hold values from -6 to 6
- owner: int32 [8, 64], P('grp'), may hold values from 0 to 63, each once within a row
- active: int32 [4, 8, 64], P(None, 'grp', 'tile'), may hold values 0 or 1
- fuel_rate: float32 [13], replicated, may hold values from 0.05 to 0.3
- fuel_wind: float32 [13], replicated, may hold values from 0.01 to 0.05
- fuel_heat: float32 [13], replicated, may hold values from 0.5 to 4
Outputs:
- level_out: float32 [2560, 40960], P('grp', 'tile')
- wind_out: float32 [2, 128, 2048], P(None, 'grp', 'tile')
The draws below stay inside these ranges and needn't reach their ends.
Inputs may be any that keep to these rules, and one draw needn't show every extreme that they name: Each row of owner is a permutation of the 64 tiles of a group.
All inputs are finite; a program needn't handle non-finite values. No bound on the sum of `active` on one device may be relied on, other than what follows from the above.
Results may differ from the reference program's by a relative error of at most 0.0003.
Values sent between devices are 32-bit elements; how exact they have to be, the bound alone decides.
No kernel may reach another device: no remote copies, remote signals or barrier semaphores. Data moves between devices by JAX's collectives and lax.ppermute only.
A program may use at most 64 MiB of HBM per device.

```python
import math
import jax
import jax.numpy as jnp

R = 20
NFUEL = 13
AY = 16
AX = 32
STEPS = 2
SUBSTEPS = 2
SUBS = 4
FY = 320
FX = 640
NAY = 128
NAX = 2048
NFY = 2560
NFX = 40960
N_GRP = 8
N_TILE = 64


def plant(values, rng, low, largest):
    index_at = [jax.random.randint(jax.random.fold_in(rng, axis), (), 0, length) for axis, length in enumerate(values.shape)]
    widest = values.shape.index(max(values.shape))
    neighbour = index_at[:widest] + [(index_at[widest] + 1) % values.shape[widest]] + index_at[widest + 1:]
    return values.at[tuple(index_at)].set(low).at[tuple(neighbour)].set(largest)


def block_levels(own_key, extent, split, smallest, high):
    gain, own = 1.0, jax.random.fold_in(own_key, 6)
    for position, shards_of in split:
        heights = jnp.exp(jax.random.uniform(jax.random.fold_in(own, position), (shards_of,), jnp.float32, smallest / len(split), high / len(split)))
        gain = gain * jnp.repeat(heights, extent[position] // shards_of).reshape([-1 if axis == position else 1 for axis in range(len(extent))])
    return gain


def gaussian(own_key, dims, deviation, most, split=(), dtype=jnp.bfloat16):
    entries = jax.random.normal(own_key, dims, jnp.float32) * deviation
    if len(split) > 0:
        entries = block_levels(own_key, dims, split, -0.22, 0.18) * entries
    return jnp.clip(entries, min=-most, max=most).astype(dtype)


def setup_inputs(seed: int = 0) -> dict:
    seeds = jax.random.split(jax.random.key(seed), 9)
    return {
        "level_set": gaussian(seeds[0], (NFY, NFX), 2.0, 8.0, ((0, 8), (1, 64)), jnp.float32),
        "fuel": plant(jax.random.randint(seeds[1], (NFY, NFX), 0, NFUEL), jax.random.fold_in(seeds[1], 1), 0, NFUEL - 1).astype(jnp.int32),
        "wind": gaussian(seeds[2], (2, NAY, NAX), 2.0, 6.0, ((1, 8), (2, 64)), jnp.float32),
        "owner": jax.vmap(lambda own: jax.random.permutation(own, N_TILE))(jax.random.split(seeds[3], N_GRP)).reshape((N_GRP, N_TILE)).astype(jnp.int32),
        "active": plant((jax.random.randint(seeds[4], (SUBS, N_GRP, N_TILE), 0, 3) < 2).astype(jnp.int32), jax.random.fold_in(seeds[4], 1), 0, 1),
        "fuel_rate": jnp.clip(jnp.exp(jax.random.uniform(seeds[5], (NFUEL,), jnp.float32, math.log(0.05), math.log(0.3))), 0.05, 0.3),
        "fuel_wind": jnp.clip(jnp.exp(jax.random.uniform(seeds[6], (NFUEL,), jnp.float32, math.log(0.01), math.log(0.05))), 0.01, 0.05),
        "fuel_heat": jnp.clip(jnp.exp(jax.random.uniform(seeds[7], (NFUEL,), jnp.float32, math.log(0.5), math.log(4.0))), 0.5, 4.0),
    }


def lookup(fuel, table):
    total = jnp.zeros(fuel.shape, jnp.float32)
    for category in range(NFUEL):
        total = total + jnp.where(fuel == category, table[category], jnp.float32(0.0))
    return total

def burnt(level):
    return 0.5 * (1.0 - jnp.tanh(level))

def reference(level_set, fuel, wind, owner, active, fuel_rate, fuel_wind, fuel_heat):
    groups = N_GRP
    tiles = N_TILE
    rate = lookup(fuel, fuel_rate)
    drift = lookup(fuel, fuel_wind)
    heat = lookup(fuel, fuel_heat)
    level = level_set
    inverse = jnp.argsort(owner, axis=1).astype(jnp.int32)
    counter = 0
    for atmos_step in range(STEPS):
        blocks = wind.reshape(2, groups, AY, tiles, AX)
        index = jnp.broadcast_to(owner[None, :, None, :, None], blocks.shape)
        readers = jnp.take_along_axis(blocks, index, axis=3).reshape(2, NAY, NAX)
        east = jnp.repeat(jnp.repeat(readers[0], R, axis=0), R, axis=1)
        north = jnp.repeat(jnp.repeat(readers[1], R, axis=0), R, axis=1)
        fine_flux = jnp.zeros(level.shape, jnp.float32)
        for substep in range(SUBSTEPS):
            padded = jnp.pad(level, 1, mode='edge')
            back_x = level - padded[1:-1, :-2]
            ahead_x = padded[1:-1, 2:] - level
            back_y = level - padded[:-2, 1:-1]
            ahead_y = padded[2:, 1:-1] - level
            slope = jnp.sqrt(jnp.maximum(back_x, 0.0) ** 2 + jnp.minimum(ahead_x, 0.0) ** 2 + jnp.maximum(back_y, 0.0) ** 2 + jnp.minimum(ahead_y, 0.0) ** 2 + 1e-12)
            carry = jnp.maximum(east, 0.0) * back_x + jnp.minimum(east, 0.0) * ahead_x + jnp.maximum(north, 0.0) * back_y + jnp.minimum(north, 0.0) * ahead_y
            candidate = level - rate * slope - drift * carry
            flags = active[counter] > 0
            gate = flags[:, None, :, None]
            newer = jnp.where(gate, candidate.reshape(groups, FY, tiles, FX), level.reshape(groups, FY, tiles, FX)).reshape(NFY, NFX)
            fine_flux = fine_flux + heat * (burnt(newer) - burnt(level))
            level = newer
            counter += 1
        coarse = fine_flux.reshape(NAY, R, NAX, R).sum(axis=(1, 3)) / float(R * R)
        coarse4 = coarse.reshape(groups, AY, tiles, AX)
        inv_index = jnp.broadcast_to(inverse[:, None, :, None], coarse4.shape)
        owned = jnp.take_along_axis(coarse4, inv_index, axis=2)
        padq = jnp.pad(owned, ((0, 0), (1, 1), (0, 0), (1, 1)), mode='edge')
        grad_x = (padq[:, 1:-1, :, 2:] - padq[:, 1:-1, :, :-2]) * 0.5
        grad_y = (padq[:, 2:, :, 1:-1] - padq[:, :-2, :, 1:-1]) * 0.5
        wind4 = wind.reshape(2, groups, AY, tiles, AX)
        new_east = 0.9 * wind4[0] + 40.0 * grad_x
        new_north = 0.9 * wind4[1] + 40.0 * grad_y
        wind = jnp.stack([new_east, new_north]).reshape(2, NAY, NAX)
    return (level, wind)
```

```python
import jax
import jax.numpy as jnp
from jax import lax
from jax.experimental import pallas as pl
from jax.experimental.pallas import tpu as pltpu
from jax.sharding import PartitionSpec as P

R = 20
AY = 16
AX = 32
FY = 320
FX = 640
STEPS = 2
SUBSTEPS = 2
NZ = 16
NX = 4
HALO = 48
HALF = 64
PAD = 8
TOP = PAD + HALO
ROWS = TOP + FY + HALO + PAD
COLS = FX + 2 * HALF
NL = COLS // 128
RIGHT = 40
LEFT = 51
CR = 24

VM = pl.BlockSpec(memory_space=pltpu.VMEM)
SM = pl.BlockSpec(memory_space=pltpu.SMEM)
PARAMS = pltpu.CompilerParams(vmem_limit_bytes=40 * 1024 * 1024)


def lanes(shape):
    return lax.broadcasted_iota(jnp.int32, shape, 1)


def f32(*shape):
    return jax.ShapeDtypeStruct(shape, jnp.float32)


def thirds(x):
    high = x.astype(jnp.bfloat16)
    rest = x - high.astype(jnp.float32)
    middle = rest.astype(jnp.bfloat16)
    low = (rest - middle.astype(jnp.float32)).astype(jnp.bfloat16)
    return jnp.concatenate([high, middle, low], axis=0)


def exact_dot(x, onehot):
    n = x.shape[0]
    out = jnp.dot(thirds(x), onehot, preferred_element_type=jnp.float32)
    return out[:n] + out[n : 2 * n] + out[2 * n :]


def coarse_lane(fine):
    own = fine // R
    right = RIGHT + (fine - FX) // R
    left = LEFT - (COLS - 1 - fine) // R
    edge = jnp.where(fine < FX + 3 * R, right, jnp.where(fine >= COLS - 3 * R, left, -1))
    return jnp.where(fine < FX, own, edge)


def pack_kernel(level0, level4, fuel0, fuel4, wind, active, to_left, to_right, slots):
    lane = lanes((FY, 128))
    fuel_first = pltpu.roll(fuel0[...].astype(jnp.float32), HALF, 1)
    fuel_last = pltpu.roll(fuel4[...].astype(jnp.float32), HALF, 1)
    to_left[0:FY, :] = jnp.where(lane < HALF, level0[...], fuel_first)
    to_right[0:FY, :] = jnp.where(lane >= HALF, level4[...], fuel_last)
    for k in range(8):
        flag = (active[min(k, 3), 0, 0] > 0).astype(jnp.float32)
        row = jnp.full((1, 128), flag, jnp.float32)
        to_left[FY + k : FY + k + 1, :] = row
        to_right[FY + k : FY + k + 1, :] = row
    parts = [wind[0, 0:8, :], wind[0, 8:16, :], wind[1, 0:8, :], wind[1, 8:16, :]]
    block = jnp.concatenate(parts, axis=1)
    for k in range(NX):
        slots[k] = block


def pack(level, fuel, wind, active):
    edge0 = pl.BlockSpec((FY, 128), lambda i: (0, 0))
    edge4 = pl.BlockSpec((FY, 128), lambda i: (0, FX // 128 - 1))
    whole = lambda *s: pl.BlockSpec(s, lambda i: (0,) * len(s))
    return pl.pallas_call(
        pack_kernel,
        grid=(1,),
        in_specs=[edge0, edge4, edge0, edge4, whole(2, AY, AX), SM],
        out_specs=[whole(FY + 8, 128), whole(FY + 8, 128), whole(NX, 8, 128)],
        out_shape=[f32(FY + 8, 128), f32(FY + 8, 128), f32(NX, 8, 128)],
        name="pack",
    )(level, level, fuel, fuel, wind, active)


def route_kernel(owner, blocks, slots):
    tile = lax.axis_index("tile")
    first = (tile // NZ) * NZ
    inside = lanes((8, 128)) % AX
    for k in range(NZ):
        reader = first + k
        main = blocks[owner[0, reader] // NZ]
        left = blocks[owner[0, jnp.maximum(reader - 1, 0)] // NZ]
        right = blocks[owner[0, jnp.minimum(reader + 1, NX * NZ - 1)] // NZ]
        edges = jnp.where(inside >= AX - 3, left, jnp.where(inside < 3, right, 0.0))
        edges = pltpu.roll(edges, 3, 1)
        small = edges[0:2]
        for b in range(1, 4):
            small = small + pltpu.roll(edges[2 * b : 2 * b + 2], 8 * b, 1)
        for b in range(4):
            slots[5 * k + b] = main[2 * b : 2 * b + 2]
        slots[5 * k + 4] = small


def route(owner, blocks):
    return pl.pallas_call(
        route_kernel, in_specs=[SM, VM], out_specs=VM, out_shape=f32(5 * NZ, 2, 128), name="route"
    )(owner, blocks)


def rows_kernel(level_top, level_bottom, fuel_top, fuel_bottom, from_left, from_right, active, to_up, to_down):
    lane = lanes((HALO, 128))
    for out, level, fuel, start, cut in (
        (to_up, level_top, fuel_top, 0, 0),
        (to_down, level_bottom, fuel_bottom, FY - HALO, 80 - HALO),
    ):
        out[0:HALO, 0:FX] = level[cut : cut + HALO, :]
        out[HALO : 2 * HALO, 0:FX] = fuel[cut : cut + HALO, :].astype(jnp.float32)
        one = from_left[start : start + HALO, :]
        two = from_right[start : start + HALO, :]
        out[0:HALO, FX:COLS] = jnp.where(lane < HALF, two, one)
        out[HALO : 2 * HALO, FX:COLS] = pltpu.roll(jnp.where(lane < HALF, one, two), HALF, 1)
        for k in range(8):
            flag = (active[min(k, 3), 0, 0] > 0).astype(jnp.float32)
            out[2 * HALO + k : 2 * HALO + k + 1, 0:FX] = jnp.full((1, FX), flag, jnp.float32)
        out[2 * HALO : 2 * HALO + 8, FX:COLS] = jnp.where(
            lane[0:8] < HALF, from_right[FY : FY + 8, :], from_left[FY : FY + 8, :]
        )


def rows(level, fuel, from_left, from_right, active):
    top = pl.BlockSpec((80, FX), lambda i: (0, 0))
    bottom = pl.BlockSpec((80, FX), lambda i: (FY // 80 - 1, 0))
    whole = lambda *s: pl.BlockSpec(s, lambda i: (0,) * len(s))
    shape = (2 * HALO + 8, COLS)
    return pl.pallas_call(
        rows_kernel,
        grid=(1,),
        in_specs=[top, bottom, top, bottom, whole(FY + 8, 128), whole(FY + 8, 128), SM],
        out_specs=[whole(*shape), whole(*shape)],
        out_shape=[f32(*shape), f32(*shape)],
        name="rows",
    )(level, level, fuel, fuel, from_left, from_right, active)


def readers_kernel(owner, received, held, to_up, to_down):
    tile = lax.axis_index("tile")
    lane = lanes((8, 128))
    main_at = 5 * (owner[0, tile] % NZ)
    left_at = 5 * (owner[0, jnp.maximum(tile - 1, 0)] % NZ) + 4
    right_at = 5 * (owner[0, jnp.minimum(tile + 1, NX * NZ - 1)] % NZ) + 4
    main = jnp.concatenate([received[main_at + b] for b in range(4)], axis=0)
    left = received[left_at]
    right = received[right_at]
    left = jnp.concatenate([pltpu.roll(left, (128 - 8 * b) % 128, 1) for b in range(4)], axis=0)
    right = jnp.concatenate([pltpu.roll(right, (128 - 8 * b) % 128, 1) for b in range(4)], axis=0)
    for q in range(4):
        own = pltpu.roll(main, (128 - 32 * q) % 128, 1)
        one = pltpu.roll(left, (LEFT - 2 - 32 * (q + 1)) % 128, 1)
        two = pltpu.roll(right, (RIGHT - 3 - 32 * q) % 128, 1)
        is_left = jnp.logical_and(lane >= LEFT - 2, lane <= LEFT)
        is_right = jnp.logical_and(lane >= RIGHT, lane <= RIGHT + 2)
        held[8 * q : 8 * q + 8, :] = jnp.where(
            lane < AX, own, jnp.where(is_left, one, jnp.where(is_right, two, 0.0))
        )
    for out, start in ((to_up, 0), (to_down, AY - 3)):
        out[0:3, :] = held[start : start + 3, :]
        out[3:6, :] = held[AY + start : AY + start + 3, :]
        out[6:8, :] = jnp.zeros((2, 128), jnp.float32)


def readers(owner, received):
    return pl.pallas_call(
        readers_kernel,
        in_specs=[SM, VM],
        out_specs=[VM, VM, VM],
        out_shape=[f32(2 * AY, 128), f32(8, 128), f32(8, 128)],
        name="readers",
    )(owner, received)


def slab_kernel(
    level, fuel, from_left, from_right, from_up, from_down, held, wind_up, wind_down,
    active, fuel_rate, fuel_wind, fuel_heat,
    level_out, slots,
    phi_a, phi_b, phi_c, rate, drift, heat, east, north, winds, gates, sums, spread, gather,
):
    group = lax.axis_index("grp")
    tile = lax.axis_index("tile")
    first_row = group == 0
    last_row = group == lax.axis_size("grp") - 1
    first_col = tile == 0
    last_col = tile == lax.axis_size("tile") - 1
    lane8 = lanes((8, 128))
    sub8 = lax.broadcasted_iota(jnp.int32, (8, COLS), 0)

    def table(values):
        row = jnp.zeros((8, 128), jnp.float32)
        for c in range(values.shape[0]):
            row = jnp.where(lane8 == c, values[c], row)
        return row

    tables = [(table(fuel_rate), rate), (table(fuel_wind), drift), (table(fuel_heat), heat)]

    def look(kinds, at, col):
        for row, out in tables:
            out[pl.ds(at, 8), col : col + 128] = jnp.take_along_axis(
                row, kinds, axis=1, mode="promise_in_bounds"
            )

    zero = jnp.zeros((PAD, COLS), jnp.float32)
    for buf in (phi_a, phi_b, phi_c, rate, drift, heat):
        buf[0:PAD, :] = zero
        buf[ROWS - PAD : ROWS, :] = zero
    phi_a[TOP - HALO : TOP, :] = from_up[0:HALO, :]
    phi_a[TOP + FY : TOP + FY + HALO, :] = from_down[0:HALO, :]

    def own_rows(i, _):
        at = pl.multiple_of(i * 8, 8)
        to = pl.multiple_of(i * 8 + TOP, 8)
        phi_a[pl.ds(to, 8), 0:FX] = level[pl.ds(at, 8), :]
        one = from_left[pl.ds(at, 8), :]
        two = from_right[pl.ds(at, 8), :]
        phi_a[pl.ds(to, 8), FX:COLS] = jnp.where(lane8 < HALF, two, one)
        beside = pltpu.roll(jnp.where(lane8 < HALF, one, two), HALF, 1).astype(jnp.int32)
        for c in range(FX // 128):
            look(fuel[pl.ds(at, 8), 128 * c : 128 * c + 128], to, 128 * c)
        look(beside, to, FX)
        return 0

    lax.fori_loop(0, FY // 8, own_rows, 0)

    def halo_rows(i, _):
        at = pl.multiple_of(i * 8 + HALO, 8)
        for source, start in ((from_up, TOP - HALO), (from_down, TOP + FY)):
            to = pl.multiple_of(i * 8 + start, 8)
            for c in range(NL):
                look(source[pl.ds(at, 8), 128 * c : 128 * c + 128].astype(jnp.int32), to, 128 * c)
        return 0

    lax.fori_loop(0, HALO // 8, halo_rows, 0)

    gates[0:8, :] = from_up[2 * HALO : 2 * HALO + 8, :]
    gates[16:24, :] = from_down[2 * HALO : 2 * HALO + 8, :]
    for k in range(STEPS * SUBSTEPS):
        flag = (active[k, 0, 0] > 0).astype(jnp.float32)
        gates[8 + k : 9 + k, 0:FX] = jnp.full((1, FX), flag, jnp.float32)
    gates[8:16, FX:COLS] = jnp.where(
        lane8 < HALF, from_right[FY : FY + 8, :], from_left[FY : FY + 8, :]
    )

    for comp in range(2):
        base = comp * CR
        winds[base : base + 3, :] = wind_up[3 * comp : 3 * comp + 3, :]
        winds[base + 3 : base + 3 + AY, :] = held[AY * comp : AY * comp + AY, :]
        winds[base + 3 + AY : base + 6 + AY, :] = wind_down[3 * comp : 3 * comp + 3, :]
        winds[base + 6 + AY : base + CR, :] = jnp.zeros((CR - 6 - AY, 128), jnp.float32)

    spread[...] = (
        coarse_lane(lanes((128, COLS))) == lax.broadcasted_iota(jnp.int32, (128, COLS), 0)
    ).astype(jnp.bfloat16)
    gather[...] = (
        coarse_lane(lax.broadcasted_iota(jnp.int32, (COLS, 128), 0)) == lanes((COLS, 128))
    ).astype(jnp.bfloat16)

    def expand():
        wide = exact_dot(winds[...], spread[...])
        east[...] = wide[0:CR]
        north[...] = wide[CR : 2 * CR]

    def edges(phi):
        @pl.when(first_row)
        def _():
            phi[TOP - 1 : TOP, :] = phi[TOP : TOP + 1, :]

        @pl.when(last_row)
        def _():
            phi[TOP + FY : TOP + FY + 1, :] = phi[TOP + FY - 1 : TOP + FY, :]

        @pl.when(first_col)
        def _():
            old = phi[:, COLS - 128 : COLS]
            new = jnp.broadcast_to(phi[:, 0:1], (ROWS, 128))
            phi[:, COLS - 128 : COLS] = jnp.where(lanes((ROWS, 128)) == 127, new, old)

        @pl.when(last_col)
        def _():
            old = phi[:, FX : FX + 128]
            new = jnp.broadcast_to(phi[:, FX - 1 : FX], (ROWS, 128))
            phi[:, FX : FX + 128] = jnp.where(lanes((ROWS, 128)) == 0, new, old)

    def update(phi, at, e, n, gate):
        before = phi[pl.ds(pl.multiple_of(at - 8, 8), 8), :]
        now = phi[pl.ds(at, 8), :]
        after = phi[pl.ds(pl.multiple_of(at + 8, 8), 8), :]
        south = jnp.where(sub8 == 0, pltpu.roll(before, 1, 0), pltpu.roll(now, 1, 0))
        above = jnp.where(sub8 == 7, pltpu.roll(after, 7, 0), pltpu.roll(now, 7, 0))
        west = pltpu.roll(now, 1, 1)
        east_cell = pltpu.roll(now, COLS - 1, 1)
        back_x = now - west
        ahead_x = east_cell - now
        back_y = now - south
        ahead_y = above - now
        bx = jnp.maximum(back_x, 0.0)
        ax = jnp.minimum(ahead_x, 0.0)
        by = jnp.maximum(back_y, 0.0)
        ay = jnp.minimum(ahead_y, 0.0)
        slope = jnp.sqrt(bx * bx + ax * ax + by * by + ay * ay + 1e-12)
        carry = e[0] * back_x + e[1] * ahead_x + n[0] * back_y + n[1] * ahead_y
        change = rate[pl.ds(at, 8), :] * slope + drift[pl.ds(at, 8), :] * carry
        return now - gate * change

    def signed(row):
        return (jnp.maximum(row, 0.0), jnp.minimum(row, 0.0))

    def wind_row(ref, row):
        return jnp.broadcast_to(ref[pl.ds(row, 1), :], (8, COLS))

    def band(phi, m, k, which, finish):
        at = pl.multiple_of(2 * PAD + 40 * m, 8)
        region = (m > 0).astype(jnp.int32) + (m > 8).astype(jnp.int32)
        gate = jnp.broadcast_to(gates[pl.ds(region * 8 + k, 1), :], (8, COLS))
        row = 2 * m + 1
        low = (wind_row(east, row), wind_row(north, row))
        high = (wind_row(east, row + 1), wind_row(north, row + 1))
        mixed = tuple(jnp.where(sub8 < 4, a, b) for a, b in zip(low, high))
        for t in which:
            e, n = (low, low, mixed, high, high)[t]
            here = pl.multiple_of(at + 8 * t, 8)
            finish(t, here, update(phi, here, signed(e), signed(n), gate))

    def tile_rows(phi, at, row, region, k):
        gate = jnp.broadcast_to(gates[region * 8 + k : region * 8 + k + 1, :], (8, COLS))
        return update(phi, at, signed(wind_row(east, row)), signed(wind_row(north, row)), gate)

    def store_to(out):
        def finish(t, here, new):
            out[pl.ds(here, 8), :] = new

        return finish

    def flux_bands(before, phi, out, k, first, last):
        def body(m, _):
            parts = []

            def finish(t, here, new):
                if out is not None:
                    out[pl.ds(here, 8), :] = new
                else:
                    level_out[pl.ds(pl.multiple_of(here - TOP, 8), 8), :] = new[:, 0:FX]
                old = before[pl.ds(here, 8), :]
                parts.append(heat[pl.ds(here, 8), :] * (jnp.tanh(old) - jnp.tanh(new)))

            band(phi, m, k, range(5), finish)
            low = parts[0] + parts[1] + jnp.where(sub8 < 4, parts[2], 0.0)
            high = parts[3] + parts[4] + jnp.where(sub8 >= 4, parts[2], 0.0)
            sums[pl.ds(2 * m + 1, 1), :] = jnp.sum(low, axis=0, keepdims=True)
            sums[pl.ds(2 * m + 2, 1), :] = jnp.sum(high, axis=0, keepdims=True)
            return 0

        lax.fori_loop(first, last, body, 0)

    def pooled():
        return exact_dot(sums[...], gather[...]) * (0.5 / (R * R))

    lane_c = lanes((CR, 128))
    row_c = lax.broadcasted_iota(jnp.int32, (CR, 128), 0)
    sums[...] = jnp.zeros((CR, COLS), jnp.float32)

    expand()
    edges(phi_a)
    phi_b[PAD : PAD + 8, :] = tile_rows(phi_a, PAD, 0, 0, 0)
    phi_b[ROWS - 2 * PAD : ROWS - PAD, :] = tile_rows(phi_a, ROWS - 2 * PAD, AY + 5, 2, 0)

    def first_substep(m, _):
        band(phi_a, m, 0, range(5), store_to(phi_b))
        return 0

    lax.fori_loop(0, 10, first_substep, 0)
    edges(phi_b)
    flux_bands(phi_a, phi_b, phi_c, 1, 0, 10)
    edges(phi_c)

    flux0 = pooled()
    ahead = jnp.where(jnp.logical_or(lane_c == AX - 1, lane_c == LEFT), flux0, pltpu.roll(flux0, 127, 1))
    back = jnp.where(jnp.logical_or(lane_c == 0, lane_c == RIGHT), flux0, pltpu.roll(flux0, 1, 1))
    last_rows = jnp.logical_or(row_c == 2, row_c == AY + 2)
    first_rows = jnp.logical_or(row_c == 3, row_c == AY + 3)
    below = jnp.where(last_rows, flux0, pltpu.roll(flux0, CR - 1, 0))
    upper = jnp.where(first_rows, flux0, pltpu.roll(flux0, 1, 0))
    winds[0:CR, :] = 0.9 * winds[0:CR, :] + 20.0 * (ahead - back)
    winds[CR : 2 * CR, :] = 0.9 * winds[CR : 2 * CR, :] + 20.0 * (below - upper)
    expand()

    top = TOP - 8
    bottom = TOP + FY
    phi_b[top : top + 8, :] = tile_rows(phi_c, top, 2, 0, 2)
    phi_b[bottom : bottom + 8, :] = tile_rows(phi_c, bottom, AY + 3, 2, 2)

    def third_substep(m, _):
        band(phi_c, m, 2, range(5), store_to(phi_b))
        return 0

    lax.fori_loop(1, 9, third_substep, 0)
    edges(phi_b)
    flux_bands(phi_c, phi_b, None, 3, 1, 9)
    total = 0.9 * flux0 + pooled()

    packed = jnp.zeros((4, 128), jnp.float32)
    lane4 = lanes((4, 128))
    for q in range(4):
        moved = pltpu.roll(total, 32 * q, 1)[3 + 4 * q : 7 + 4 * q]
        packed = jnp.where(lane4 // AX == q, moved, packed)
    for k in range(NX * NZ):
        slots[k] = packed


def slab(*args):
    big = pltpu.VMEM((ROWS, COLS), jnp.float32)
    return pl.pallas_call(
        slab_kernel,
        in_specs=[VM] * 9 + [SM] * 4,
        out_specs=[VM, VM],
        out_shape=[f32(FY, FX), f32(NX * NZ, 4, 128)],
        scratch_shapes=[big] * 6
        + [
            pltpu.VMEM((CR, COLS), jnp.float32),
            pltpu.VMEM((CR, COLS), jnp.float32),
            pltpu.VMEM((2 * CR, 128), jnp.float32),
            pltpu.VMEM((CR, COLS), jnp.float32),
            pltpu.VMEM((CR, COLS), jnp.float32),
            pltpu.VMEM((128, COLS), jnp.bfloat16),
            pltpu.VMEM((COLS, 128), jnp.bfloat16),
        ],
        compiler_params=PARAMS,
        name="slab",
    )(*args)


def final_kernel(owner, received, wind, wind_out):
    tile = lax.axis_index("tile")
    source = jnp.int32(0)
    for t in range(NX * NZ):
        source = jnp.where(owner[0, t] == tile, t, source)
    block = received[source]
    flux = jnp.concatenate([pltpu.roll(block, (128 - 32 * q) % 128, 1) for q in range(4)], axis=0)
    lane = lanes((AY, 128))
    row = lax.broadcasted_iota(jnp.int32, (AY, 128), 0)
    ahead = jnp.where(lane == AX - 1, flux, pltpu.roll(flux, 127, 1))
    back = jnp.where(lane == 0, flux, pltpu.roll(flux, 1, 1))
    below = jnp.where(row == AY - 1, flux, pltpu.roll(flux, AY - 1, 0))
    upper = jnp.where(row == 0, flux, pltpu.roll(flux, 1, 0))
    wind_out[0] = 0.81 * wind[0] + 20.0 * (ahead - back)[:, 0:AX]
    wind_out[1] = 0.81 * wind[1] + 20.0 * (below - upper)[:, 0:AX]


def final(owner, received, wind):
    return pl.pallas_call(
        final_kernel, in_specs=[SM, VM, VM], out_specs=VM, out_shape=f32(2, AY, AX), name="final"
    )(owner, received, wind)


def shift(value, axis, step):
    size = lax.axis_size(axis)
    pairs = [(i, i + step) for i in range(size) if 0 <= i + step < size]
    return lax.ppermute(value, axis, pairs)


def shards(level, fuel, wind, owner, active, fuel_rate, fuel_wind, fuel_heat):
    along_x = [[x * NZ + z for x in range(NX)] for z in range(NZ)]
    along_z = [[x * NZ + z for z in range(NZ)] for x in range(NX)]
    to_left, to_right, blocks = pack(level, fuel, wind, active)
    from_right = shift(to_left, "tile", -1)
    from_left = shift(to_right, "tile", 1)
    blocks = lax.all_to_all(blocks, "tile", 0, 0, tiled=True, axis_index_groups=along_x)
    slots = route(owner, blocks)
    to_up, to_down = rows(level, fuel, from_left, from_right, active)
    from_down = shift(to_up, "grp", -1)
    from_up = shift(to_down, "grp", 1)
    received = lax.all_to_all(slots, "tile", 0, 0, tiled=True, axis_index_groups=along_z)
    held, wind_to_up, wind_to_down = readers(owner, received)
    wind_down = shift(wind_to_up, "grp", -1)
    wind_up = shift(wind_to_down, "grp", 1)
    level_out, flux = slab(
        level, fuel, from_left, from_right, from_up, from_down, held, wind_up, wind_down,
        active, fuel_rate, fuel_wind, fuel_heat,
    )
    flux = lax.all_to_all(flux, "tile", 0, 0, tiled=True)
    return (level_out, final(owner, flux, wind))


def solution(mesh):
    in_specs = (
        P("grp", "tile"),
        P("grp", "tile"),
        P(None, "grp", "tile"),
        P("grp", None),
        P(None, "grp", "tile"),
        P(),
        P(),
        P(),
    )
    out_specs = (P("grp", "tile"), P(None, "grp", "tile"))
    return jax.shard_map(shards, mesh=mesh, in_specs=in_specs, out_specs=out_specs, check_vma=False)
```

```python
import jax
import jax.numpy as jnp
from jax import lax
from jax.experimental import pallas as pl
from jax.experimental.pallas import tpu as pltpu
from jax.sharding import PartitionSpec as P

R = 20
AY = 16
AX = 32
FY = 320
FX = 640
STEPS = 2
SUBSTEPS = 2
NZ = 16
NX = 4
HALO = 48
HALF = 64
PAD = 8
TOP = PAD + HALO
ROWS = TOP + FY + HALO + PAD
COLS = FX + 2 * HALF
NL = COLS // 128
RIGHT = 40
LEFT = 51
CR = 24

VM = pl.BlockSpec(memory_space=pltpu.VMEM)
SM = pl.BlockSpec(memory_space=pltpu.SMEM)
PARAMS = pltpu.CompilerParams(vmem_limit_bytes=40 * 1024 * 1024)


def lanes(shape):
    return lax.broadcasted_iota(jnp.int32, shape, 1)


def f32(*shape):
    return jax.ShapeDtypeStruct(shape, jnp.float32)


def thirds(x):
    high = x.astype(jnp.bfloat16)
    rest = x - high.astype(jnp.float32)
    middle = rest.astype(jnp.bfloat16)
    low = (rest - middle.astype(jnp.float32)).astype(jnp.bfloat16)
    return jnp.concatenate([high, middle, low], axis=0)


def exact_dot(x, onehot):
    n = x.shape[0]
    out = jnp.dot(thirds(x), onehot, preferred_element_type=jnp.float32)
    return out[:n] + out[n : 2 * n] + out[2 * n :]


def coarse_lane(fine):
    own = fine // R
    right = RIGHT + (fine - FX) // R
    left = LEFT - (COLS - 1 - fine) // R
    edge = jnp.where(fine < FX + 3 * R, right, jnp.where(fine >= COLS - 3 * R, left, -1))
    return jnp.where(fine < FX, own, edge)


def pack_kernel(level0, level4, fuel0, fuel4, wind, active, to_left, to_right, slots):
    lane = lanes((FY, 128))
    fuel_first = pltpu.roll(fuel0[...].astype(jnp.float32), HALF, 1)
    fuel_last = pltpu.roll(fuel4[...].astype(jnp.float32), HALF, 1)
    to_left[0:FY, :] = jnp.where(lane < HALF, level0[...], fuel_first)
    to_right[0:FY, :] = jnp.where(lane >= HALF, level4[...], fuel_last)
    for k in range(8):
        row = jnp.full((1, 128), flag_of(active, k), jnp.float32)
        to_left[FY + k : FY + k + 1, :] = row
        to_right[FY + k : FY + k + 1, :] = row
    parts = [wind[0, 0:8, :], wind[0, 8:16, :], wind[1, 0:8, :], wind[1, 8:16, :]]
    block = jnp.concatenate(parts, axis=1)
    for k in range(NX * NZ):
        slots[k] = block


def flag_of(active, k):
    return (active[0, 0, min(k, STEPS * SUBSTEPS - 1)] > 0).astype(jnp.float32)


def whole(*s):
    return pl.BlockSpec(s, lambda i: (0,) * len(s))


def pack(level, fuel, wind, active):
    edge0 = pl.BlockSpec((FY, 128), lambda i: (0, 0))
    edge4 = pl.BlockSpec((FY, 128), lambda i: (0, FX // 128 - 1))
    return pl.pallas_call(
        pack_kernel,
        grid=(1,),
        in_specs=[edge0, edge4, edge0, edge4, whole(2, AY, AX), SM],
        out_specs=[whole(FY + 8, 128), whole(FY + 8, 128), whole(NX * NZ, 8, 128)],
        out_shape=[f32(FY + 8, 128), f32(FY + 8, 128), f32(NX * NZ, 8, 128)],
        name="pack",
    )(level, level, fuel, fuel, wind, active)


def rows_kernel(
    level_top, level_bottom, fuel_top, fuel_bottom, from_left, from_right, blocks, owner, active,
    held, to_up, to_down,
):
    tile = lax.axis_index("tile")
    lane = lanes((HALO, 128))
    lane8 = lanes((8, 128))
    main = blocks[owner[0, tile]]
    left = blocks[owner[0, jnp.maximum(tile - 1, 0)]]
    right = blocks[owner[0, jnp.minimum(tile + 1, NX * NZ - 1)]]
    is_left = jnp.logical_and(lane8 >= LEFT - 2, lane8 <= LEFT)
    is_right = jnp.logical_and(lane8 >= RIGHT, lane8 <= RIGHT + 2)
    for q in range(4):
        own = pltpu.roll(main, (128 - 32 * q) % 128, 1)
        one = pltpu.roll(left, (LEFT - 31 - 32 * q) % 128, 1)
        two = pltpu.roll(right, (RIGHT - 32 * q) % 128, 1)
        held[8 * q : 8 * q + 8, :] = jnp.where(
            lane8 < AX, own, jnp.where(is_left, one, jnp.where(is_right, two, 0.0))
        )
    for out, level, fuel, start, cut, coarse in (
        (to_up, level_top, fuel_top, 0, 0, 0),
        (to_down, level_bottom, fuel_bottom, FY - HALO, 80 - HALO, AY - 3),
    ):
        out[0:HALO, 0:FX] = level[cut : cut + HALO, :]
        out[HALO : 2 * HALO, 0:FX] = fuel[cut : cut + HALO, :].astype(jnp.float32)
        one = from_left[start : start + HALO, :]
        two = from_right[start : start + HALO, :]
        out[0:HALO, FX:COLS] = jnp.where(lane < HALF, two, one)
        out[HALO : 2 * HALO, FX:COLS] = pltpu.roll(jnp.where(lane < HALF, one, two), HALF, 1)
        for k in range(4):
            row = 2 * HALO + k
            out[row : row + 1, 0:FX] = jnp.full((1, FX), flag_of(active, k), jnp.float32)
            out[row : row + 1, FX:COLS] = jnp.where(
                lane[0:1] < HALF, from_right[FY + k : FY + k + 1, :], from_left[FY + k : FY + k + 1, :]
            )
        row = 2 * HALO + 4
        for c in range(6):
            at = (c // 3) * AY + coarse + c % 3
            out[row : row + 1, 128 * c : 128 * c + 128] = held[at : at + 1, :]
        out[row + 1 : row + 4, :] = jnp.zeros((3, COLS), jnp.float32)


def rows(level, fuel, from_left, from_right, blocks, owner, active):
    top = pl.BlockSpec((80, FX), lambda i: (0, 0))
    bottom = pl.BlockSpec((80, FX), lambda i: (FY // 80 - 1, 0))
    shape = (2 * HALO + 8, COLS)
    return pl.pallas_call(
        rows_kernel,
        grid=(1,),
        in_specs=[top, bottom, top, bottom, whole(FY + 8, 128), whole(FY + 8, 128),
                  whole(NX * NZ, 8, 128), SM, SM],
        out_specs=[whole(2 * AY, 128), whole(*shape), whole(*shape)],
        out_shape=[f32(2 * AY, 128), f32(*shape), f32(*shape)],
        name="rows",
    )(level, level, fuel, fuel, from_left, from_right, blocks, owner, active)


def table(values):
    lane = lanes((8, 128))
    row = jnp.zeros((8, 128), jnp.float32)
    for c in range(values.shape[0]):
        row = jnp.where(lane == c, values[c], row)
    return row


def look(row, kinds):
    return jnp.take_along_axis(row, kinds, axis=1, mode="promise_in_bounds")


def values_kernel(fuel, from_left, from_right, after, fuel_rate, fuel_wind, fuel_heat, rate, drift, heat):
    lane8 = lanes((8, 128))
    tables = [(table(fuel_rate), rate), (table(fuel_wind), drift), (table(fuel_heat), heat)]

    def own_rows(i, _):
        at = pl.multiple_of(i * 8, 8)
        one = from_left[pl.ds(at, 8), :]
        two = from_right[pl.ds(at, 8), :]
        beside = pltpu.roll(jnp.where(lane8 < HALF, one, two), HALF, 1).astype(jnp.int32)
        for c in range(NL):
            kinds = beside if c == NL - 1 else fuel[pl.ds(at, 8), 128 * c : 128 * c + 128]
            for row, out in tables:
                out[pl.ds(at, 8), 128 * c : 128 * c + 128] = look(row, kinds)
        return 0

    lax.fori_loop(0, FY // 8, own_rows, 0, unroll=4)


def values(fuel, from_left, from_right, after, *names):
    return pl.pallas_call(
        values_kernel,
        in_specs=[VM, VM, VM, pl.BlockSpec(memory_space=pl.ANY), SM, SM, SM],
        out_specs=[VM, VM, VM],
        out_shape=[f32(FY, COLS)] * 3,
        compiler_params=PARAMS,
        name="values",
    )(fuel, from_left, from_right, after, *names)


def slab_kernel(
    level, from_left, from_right, from_up, from_down, held, rate, drift, heat,
    active, fuel_rate, fuel_wind, fuel_heat,
    level_out, slots,
    phi_a, phi_b, phi_c, edge_rate, edge_drift, edge_heat, east, north, winds, gates, sums, spread, gather,
):
    group = lax.axis_index("grp")
    tile = lax.axis_index("tile")
    first_row = group == 0
    last_row = group == lax.axis_size("grp") - 1
    first_col = tile == 0
    last_col = tile == lax.axis_size("tile") - 1
    lane8 = lanes((8, 128))
    sub8 = lax.broadcasted_iota(jnp.int32, (8, COLS), 0)

    zero = jnp.zeros((PAD, COLS), jnp.float32)
    phi_a[0:PAD, :] = zero
    phi_a[ROWS - PAD : ROWS, :] = zero
    phi_a[TOP - HALO : TOP, :] = from_up[0:HALO, :]
    phi_a[TOP + FY : TOP + FY + HALO, :] = from_down[0:HALO, :]

    def own_rows(i, _):
        at = pl.multiple_of(i * 8, 8)
        to = pl.multiple_of(i * 8 + TOP, 8)
        phi_a[pl.ds(to, 8), 0:FX] = level[pl.ds(at, 8), :]
        one = from_left[pl.ds(at, 8), :]
        two = from_right[pl.ds(at, 8), :]
        phi_a[pl.ds(to, 8), FX:COLS] = jnp.where(lane8 < HALF, two, one)
        return 0

    lax.fori_loop(0, FY // 8, own_rows, 0, unroll=4)
    tables = [(table(fuel_rate), edge_rate), (table(fuel_wind), edge_drift), (table(fuel_heat), edge_heat)]

    def halo_rows(i, _):
        at = pl.multiple_of(i * 8, 8)
        for source, start in ((from_up, 0), (from_down, HALO)):
            to = pl.multiple_of(at + start, 8)
            for c in range(NL):
                kinds = source[pl.ds(pl.multiple_of(at + HALO, 8), 8), 128 * c : 128 * c + 128]
                kinds = kinds.astype(jnp.int32)
                for row, out in tables:
                    out[pl.ds(to, 8), 128 * c : 128 * c + 128] = look(row, kinds)
        return 0

    lax.fori_loop(0, HALO // 8, halo_rows, 0, unroll=3)

    gates[0:8, :] = from_up[2 * HALO : 2 * HALO + 8, :]
    gates[16:24, :] = from_down[2 * HALO : 2 * HALO + 8, :]
    for k in range(STEPS * SUBSTEPS):
        gates[8 + k : 9 + k, 0:FX] = jnp.full((1, FX), flag_of(active, k), jnp.float32)
    gates[8:16, FX:COLS] = jnp.where(
        lane8 < HALF, from_right[FY : FY + 8, :], from_left[FY : FY + 8, :]
    )

    row = 2 * HALO + 4
    for comp in range(2):
        base = comp * CR
        for c in range(3):
            at = 128 * (3 * comp + c)
            winds[base + c : base + c + 1, :] = from_up[row : row + 1, at : at + 128]
            below = base + 3 + AY + c
            winds[below : below + 1, :] = from_down[row : row + 1, at : at + 128]
        winds[base + 3 : base + 3 + AY, :] = held[AY * comp : AY * comp + AY, :]
        winds[base + 6 + AY : base + CR, :] = jnp.zeros((CR - 6 - AY, 128), jnp.float32)

    spread[...] = (
        coarse_lane(lanes((128, COLS))) == lax.broadcasted_iota(jnp.int32, (128, COLS), 0)
    ).astype(jnp.bfloat16)
    gather[...] = (
        coarse_lane(lax.broadcasted_iota(jnp.int32, (COLS, 128), 0)) == lanes((COLS, 128))
    ).astype(jnp.bfloat16)

    def expand():
        wide = exact_dot(winds[...], spread[...])
        for comp, out in ((0, east), (1, north)):
            part = wide[comp * CR : comp * CR + CR]
            out[0:CR, :] = jnp.maximum(part, 0.0)
            out[CR : 2 * CR, :] = jnp.minimum(part, 0.0)

    def edges(phi):
        @pl.when(first_row)
        def _():
            phi[TOP - 1 : TOP, :] = phi[TOP : TOP + 1, :]

        @pl.when(last_row)
        def _():
            phi[TOP + FY : TOP + FY + 1, :] = phi[TOP + FY - 1 : TOP + FY, :]

        @pl.when(first_col)
        def _():
            old = phi[:, COLS - 128 : COLS]
            new = jnp.broadcast_to(phi[:, 0:1], (ROWS, 128))
            phi[:, COLS - 128 : COLS] = jnp.where(lanes((ROWS, 128)) == 127, new, old)

        @pl.when(last_col)
        def _():
            old = phi[:, FX : FX + 128]
            new = jnp.broadcast_to(phi[:, FX - 1 : FX], (ROWS, 128))
            phi[:, FX : FX + 128] = jnp.where(lanes((ROWS, 128)) == 0, new, old)

    own = (rate, drift, heat, TOP)
    upper_edge = (edge_rate, edge_drift, edge_heat, TOP - HALO)
    lower_edge = (edge_rate, edge_drift, edge_heat, TOP + FY - HALO)

    def update(phi, at, e, n, gate, fuels):
        before = phi[pl.ds(pl.multiple_of(at - 8, 8), 8), :]
        now = phi[pl.ds(at, 8), :]
        after = phi[pl.ds(pl.multiple_of(at + 8, 8), 8), :]
        south = jnp.where(sub8 == 0, pltpu.roll(before, 1, 0), pltpu.roll(now, 1, 0))
        above = jnp.where(sub8 == 7, pltpu.roll(after, 7, 0), pltpu.roll(now, 7, 0))
        west = pltpu.roll(now, 1, 1)
        east_cell = pltpu.roll(now, COLS - 1, 1)
        back_x = now - west
        ahead_x = east_cell - now
        back_y = now - south
        ahead_y = above - now
        bx = jnp.maximum(back_x, 0.0)
        ax = jnp.minimum(ahead_x, 0.0)
        by = jnp.maximum(back_y, 0.0)
        ay = jnp.minimum(ahead_y, 0.0)
        square = bx * bx + ax * ax + by * by + ay * ay + 1e-12
        slope = square * lax.rsqrt(square)
        carry = e[0] * back_x + e[1] * ahead_x + n[0] * back_y + n[1] * ahead_y
        there = pl.multiple_of(at - fuels[3], 8)
        change = fuels[0][pl.ds(there, 8), :] * slope + fuels[1][pl.ds(there, 8), :] * carry
        return now - gate * change

    def wind_row(ref, row):
        return tuple(jnp.broadcast_to(ref[pl.ds(row + part, 1), :], (8, COLS)) for part in (0, CR))

    def mix(a, b):
        return tuple(jnp.where(sub8 < 4, one, two) for one, two in zip(a, b))

    def band(phi, m, k, region, fuels, finish):
        at = pl.multiple_of(2 * PAD + 40 * m, 8)
        gate = jnp.broadcast_to(gates[region * 8 + k : region * 8 + k + 1, :], (8, COLS))
        row = 2 * m + 1
        for t in range(5):
            if t == 2:
                e = mix(wind_row(east, row), wind_row(east, row + 1))
                n = mix(wind_row(north, row), wind_row(north, row + 1))
            else:
                e, n = (wind_row(ref, row + t // 3) for ref in (east, north))
            here = pl.multiple_of(at + 8 * t, 8)
            finish(here, update(phi, here, e, n, gate, fuels), fuels)

    def tile_rows(phi, at, row, region, k, fuels):
        gate = jnp.broadcast_to(gates[region * 8 + k : region * 8 + k + 1, :], (8, COLS))
        return update(phi, at, wind_row(east, row), wind_row(north, row), gate, fuels)

    def own_bands(body):
        def step(m, _):
            body(m, 1, own)
            return 0

        lax.fori_loop(1, 9, step, 0)

    def store_to(out):
        def finish(here, new, fuels):
            out[pl.ds(here, 8), :] = new

        return finish

    def flux_band(before, phi, out, k):
        def body(m, region, fuels):
            parts = []

            def finish(here, new, fuels):
                if out is not None:
                    out[pl.ds(here, 8), :] = new
                else:
                    level_out[pl.ds(pl.multiple_of(here - TOP, 8), 8), :] = new[:, 0:FX]
                old = before[pl.ds(here, 8), :]
                there = pl.multiple_of(here - fuels[3], 8)
                parts.append(fuels[2][pl.ds(there, 8), :] * (jnp.tanh(old) - jnp.tanh(new)))

            band(phi, m, k, region, fuels, finish)
            low = parts[0] + parts[1] + jnp.where(sub8 < 4, parts[2], 0.0)
            high = parts[3] + parts[4] + jnp.where(sub8 >= 4, parts[2], 0.0)
            sums[pl.ds(2 * m + 1, 1), :] = jnp.sum(low, axis=0, keepdims=True)
            sums[pl.ds(2 * m + 2, 1), :] = jnp.sum(high, axis=0, keepdims=True)

        return body

    def pooled():
        return exact_dot(sums[...], gather[...]) * (0.5 / (R * R))

    lane_c = lanes((CR, 128))
    row_c = lax.broadcasted_iota(jnp.int32, (CR, 128), 0)
    sums[...] = jnp.zeros((CR, COLS), jnp.float32)

    expand()
    edges(phi_a)
    phi_b[PAD : PAD + 8, :] = tile_rows(phi_a, PAD, 0, 0, 0, upper_edge)
    phi_b[ROWS - 2 * PAD : ROWS - PAD, :] = tile_rows(phi_a, ROWS - 2 * PAD, AY + 5, 2, 0, lower_edge)
    band(phi_a, 0, 0, 0, upper_edge, store_to(phi_b))
    band(phi_a, 9, 0, 2, lower_edge, store_to(phi_b))
    own_bands(lambda m, region, fuels: band(phi_a, m, 0, region, fuels, store_to(phi_b)))
    edges(phi_b)
    second = flux_band(phi_a, phi_b, phi_c, 1)
    second(0, 0, upper_edge)
    second(9, 2, lower_edge)
    own_bands(second)
    edges(phi_c)

    flux0 = pooled()
    ahead = jnp.where(jnp.logical_or(lane_c == AX - 1, lane_c == LEFT), flux0, pltpu.roll(flux0, 127, 1))
    back = jnp.where(jnp.logical_or(lane_c == 0, lane_c == RIGHT), flux0, pltpu.roll(flux0, 1, 1))
    last_rows = jnp.logical_or(row_c == 2, row_c == AY + 2)
    first_rows = jnp.logical_or(row_c == 3, row_c == AY + 3)
    below = jnp.where(last_rows, flux0, pltpu.roll(flux0, CR - 1, 0))
    upper = jnp.where(first_rows, flux0, pltpu.roll(flux0, 1, 0))
    winds[0:CR, :] = 0.9 * winds[0:CR, :] + 20.0 * (ahead - back)
    winds[CR : 2 * CR, :] = 0.9 * winds[CR : 2 * CR, :] + 20.0 * (below - upper)
    expand()

    top = TOP - 8
    bottom = TOP + FY
    phi_b[top : top + 8, :] = tile_rows(phi_c, top, 2, 0, 2, upper_edge)
    phi_b[bottom : bottom + 8, :] = tile_rows(phi_c, bottom, AY + 3, 2, 2, lower_edge)
    own_bands(lambda m, region, fuels: band(phi_c, m, 2, region, fuels, store_to(phi_b)))
    edges(phi_b)
    own_bands(flux_band(phi_c, phi_b, None, 3))
    total = 0.9 * flux0 + pooled()

    packed = jnp.zeros((4, 128), jnp.float32)
    lane4 = lanes((4, 128))
    for q in range(4):
        moved = pltpu.roll(total, 32 * q, 1)[3 + 4 * q : 7 + 4 * q]
        packed = jnp.where(lane4 // AX == q, moved, packed)
    for k in range(NX * NZ):
        slots[k] = packed


def slab(*args):
    big = pltpu.VMEM((ROWS, COLS), jnp.float32)
    edge = pltpu.VMEM((2 * HALO, COLS), jnp.float32)
    return pl.pallas_call(
        slab_kernel,
        in_specs=[VM] * 9 + [SM] * 4,
        out_specs=[VM, VM],
        out_shape=[f32(FY, FX), f32(NX * NZ, 4, 128)],
        scratch_shapes=[big] * 3
        + [edge] * 3
        + [
            pltpu.VMEM((2 * CR, COLS), jnp.float32),
            pltpu.VMEM((2 * CR, COLS), jnp.float32),
            pltpu.VMEM((2 * CR, 128), jnp.float32),
            pltpu.VMEM((CR, COLS), jnp.float32),
            pltpu.VMEM((CR, COLS), jnp.float32),
            pltpu.VMEM((128, COLS), jnp.bfloat16),
            pltpu.VMEM((COLS, 128), jnp.bfloat16),
        ],
        compiler_params=PARAMS,
        name="slab",
    )(*args)


def final_kernel(owner, received, wind, wind_out):
    tile = lax.axis_index("tile")
    source = jnp.int32(0)
    for t in range(NX * NZ):
        source = jnp.where(owner[0, t] == tile, t, source)
    block = received[source]
    flux = jnp.concatenate([pltpu.roll(block, (128 - 32 * q) % 128, 1) for q in range(4)], axis=0)
    lane = lanes((AY, 128))
    row = lax.broadcasted_iota(jnp.int32, (AY, 128), 0)
    ahead = jnp.where(lane == AX - 1, flux, pltpu.roll(flux, 127, 1))
    back = jnp.where(lane == 0, flux, pltpu.roll(flux, 1, 1))
    below = jnp.where(row == AY - 1, flux, pltpu.roll(flux, AY - 1, 0))
    upper = jnp.where(row == 0, flux, pltpu.roll(flux, 1, 0))
    wind_out[0] = 0.81 * wind[0] + 20.0 * (ahead - back)[:, 0:AX]
    wind_out[1] = 0.81 * wind[1] + 20.0 * (below - upper)[:, 0:AX]


def final(owner, received, wind):
    return pl.pallas_call(
        final_kernel, in_specs=[SM, VM, VM], out_specs=VM, out_shape=f32(2, AY, AX), name="final"
    )(owner, received, wind)


def shift(value, axis, step):
    size = lax.axis_size(axis)
    pairs = [(i, i + step) for i in range(size) if 0 <= i + step < size]
    return lax.ppermute(value, axis, pairs)


def shards(level, fuel, wind, owner, active, fuel_rate, fuel_wind, fuel_heat):
    active = jnp.transpose(active, (1, 2, 0))
    tables = (fuel_rate, fuel_wind, fuel_heat)
    to_left, to_right, blocks = pack(level, fuel, wind, active)
    from_right = shift(to_left, "tile", -1)
    from_left = shift(to_right, "tile", 1)
    blocks = lax.all_to_all(blocks, "tile", 0, 0, tiled=True)
    held, to_up, to_down = rows(level, fuel, from_left, from_right, blocks, owner, active)
    from_down = shift(to_up, "grp", -1)
    from_up = shift(to_down, "grp", 1)
    rate, drift, heat = values(fuel, from_left, from_right, held, *tables)
    level_out, flux = slab(
        level, from_left, from_right, from_up, from_down, held, rate, drift, heat, active, *tables
    )
    flux = lax.all_to_all(flux, "tile", 0, 0, tiled=True)
    return (level_out, final(owner, flux, wind))


def solution(mesh):
    in_specs = (
        P("grp", "tile"),
        P("grp", "tile"),
        P(None, "grp", "tile"),
        P("grp", None),
        P(None, "grp", "tile"),
        P(),
        P(),
        P(),
    )
    out_specs = (P("grp", "tile"), P(None, "grp", "tile"))
    return jax.shard_map(shards, mesh=mesh, in_specs=in_specs, out_specs=out_specs, check_vma=False)
```

```python
import jax
import jax.numpy as jnp
from jax import lax
from jax.experimental import pallas as pl
from jax.experimental.pallas import tpu as pltpu
from jax.sharding import PartitionSpec as P

R = 20
AY = 16
AX = 32
FY = 320
FX = 640
STEPS = 2
SUBSTEPS = 2
NZ = 16
NX = 4
HALO = 48
HALF = 64
PAD = 8
TOP = PAD + HALO
ROWS = TOP + FY + HALO + PAD
COLS = FX + 2 * HALF
NL = COLS // 128
RIGHT = 40
LEFT = 51
CR = 24

VM = pl.BlockSpec(memory_space=pltpu.VMEM)
SM = pl.BlockSpec(memory_space=pltpu.SMEM)
ANY = pl.BlockSpec(memory_space=pl.ANY)
PARAMS = pltpu.CompilerParams(vmem_limit_bytes=40 * 1024 * 1024)


def lanes(shape):
    return lax.broadcasted_iota(jnp.int32, shape, 1)


def f32(*shape):
    return jax.ShapeDtypeStruct(shape, jnp.float32)


def thirds(x):
    high = x.astype(jnp.bfloat16)
    rest = x - high.astype(jnp.float32)
    middle = rest.astype(jnp.bfloat16)
    low = (rest - middle.astype(jnp.float32)).astype(jnp.bfloat16)
    return jnp.concatenate([high, middle, low], axis=0)


def exact_dot(x, onehot):
    n = x.shape[0]
    out = jnp.dot(thirds(x), onehot, preferred_element_type=jnp.float32)
    return out[:n] + out[n : 2 * n] + out[2 * n :]


def coarse_lane(fine):
    own = fine // R
    right = RIGHT + (fine - FX) // R
    left = LEFT - (COLS - 1 - fine) // R
    edge = jnp.where(fine < FX + 3 * R, right, jnp.where(fine >= COLS - 3 * R, left, -1))
    return jnp.where(fine < FX, own, edge)


def strips_kernel(level, fuel, active, to_left, to_right, left_level, right_level, left_fuel, right_fuel, arrived):
    first, last = pl.ds(0, 128), pl.ds(FX - 128, 128)
    moves = [
        pltpu.make_async_copy(source.at[:, part], buf, arrived.at[i])
        for i, (source, part, buf) in enumerate((
            (level, first, left_level), (fuel, first, left_fuel),
            (level, last, right_level), (fuel, last, right_fuel),
        ))
    ]
    for move in moves:
        move.start()
    for k in range(8):
        row = jnp.full((1, 128), flag_of(active, k), jnp.float32)
        to_left[FY + k : FY + k + 1, :] = row
        to_right[FY + k : FY + k + 1, :] = row
    lane = lanes((FY, 128))
    moves[0].wait()
    moves[1].wait()
    to_left[0:FY, :] = jnp.where(
        lane < HALF, left_level[...], pltpu.roll(left_fuel[...].astype(jnp.float32), HALF, 1)
    )
    moves[2].wait()
    moves[3].wait()
    to_right[0:FY, :] = jnp.where(
        lane >= HALF, right_level[...], pltpu.roll(right_fuel[...].astype(jnp.float32), HALF, 1)
    )


def strips(level, fuel, active):
    strip = pltpu.VMEM((FY, 128), jnp.float32)
    kinds = pltpu.VMEM((FY, 128), jnp.int32)
    return pl.pallas_call(
        strips_kernel,
        in_specs=[ANY, ANY, SM],
        out_specs=[VM, VM],
        out_shape=[f32(FY + 8, 128), f32(FY + 8, 128)],
        scratch_shapes=[strip, strip, kinds, kinds, pltpu.SemaphoreType.DMA((4,))],
        name="strips",
    )(level, fuel, active)


def flag_of(active, k):
    return (active[0, 0, min(k, STEPS * SUBSTEPS - 1)] > 0).astype(jnp.float32)


def blocks_kernel(wind, after, slots):
    parts = [wind[0, 0:8, :], wind[0, 8:16, :], wind[1, 0:8, :], wind[1, 8:16, :]]
    block = jnp.concatenate(parts, axis=1)
    for k in range(NX * NZ):
        slots[k] = block


def blocks_of(wind, after):
    return pl.pallas_call(
        blocks_kernel, in_specs=[VM, ANY], out_specs=VM, out_shape=f32(NX * NZ, 8, 128), name="blocks"
    )(wind, after)


def rows_kernel(
    level, fuel, from_left, from_right, blocks, owner, active, held, to_up, to_down,
):
    tile = lax.axis_index("tile")
    lane = lanes((HALO, 128))
    lane8 = lanes((8, 128))
    main = blocks[owner[0, tile]]
    left = blocks[owner[0, jnp.maximum(tile - 1, 0)]]
    right = blocks[owner[0, jnp.minimum(tile + 1, NX * NZ - 1)]]
    is_left = jnp.logical_and(lane8 >= LEFT - 2, lane8 <= LEFT)
    is_right = jnp.logical_and(lane8 >= RIGHT, lane8 <= RIGHT + 2)
    for q in range(4):
        own = pltpu.roll(main, (128 - 32 * q) % 128, 1)
        one = pltpu.roll(left, (LEFT - 31 - 32 * q) % 128, 1)
        two = pltpu.roll(right, (RIGHT - 32 * q) % 128, 1)
        held[8 * q : 8 * q + 8, :] = jnp.where(
            lane8 < AX, own, jnp.where(is_left, one, jnp.where(is_right, two, 0.0))
        )
    for k in range(8):
        held[2 * AY + k : 2 * AY + k + 1, :] = jnp.full((1, 128), flag_of(active, k), jnp.float32)
    for out, start, coarse in ((to_up, 0, 0), (to_down, FY - HALO, AY - 3)):
        out[0:HALO, 0:FX] = level[start : start + HALO, :]
        out[HALO : 2 * HALO, 0:FX] = fuel[start : start + HALO, :].astype(jnp.float32)
        one = from_left[start : start + HALO, :]
        two = from_right[start : start + HALO, :]
        out[0:HALO, FX:COLS] = jnp.where(lane < HALF, two, one)
        out[HALO : 2 * HALO, FX:COLS] = pltpu.roll(jnp.where(lane < HALF, one, two), HALF, 1)
        for k in range(4):
            row = 2 * HALO + k
            out[row : row + 1, 0:FX] = jnp.full((1, FX), flag_of(active, k), jnp.float32)
            out[row : row + 1, FX:COLS] = jnp.where(
                lane[0:1] < HALF, from_right[FY + k : FY + k + 1, :], from_left[FY + k : FY + k + 1, :]
            )
        row = 2 * HALO + 4
        for c in range(6):
            at = (c // 3) * AY + coarse + c % 3
            out[row : row + 1, 128 * c : 128 * c + 128] = held[at : at + 1, :]
        out[row + 1 : row + 4, :] = jnp.zeros((3, COLS), jnp.float32)


def rows(level, fuel, from_left, from_right, blocks, owner, active):
    shape = (2 * HALO + 8, COLS)
    return pl.pallas_call(
        rows_kernel,
        in_specs=[VM] * 5 + [SM, SM],
        out_specs=[VM, VM, VM],
        out_shape=[f32(2 * AY + 8, 128), f32(*shape), f32(*shape)],
        compiler_params=PARAMS,
        name="rows",
    )(level, fuel, from_left, from_right, blocks, owner, active)


def table(values):
    lane = lanes((8, 128))
    row = jnp.zeros((8, 128), jnp.float32)
    for c in range(values.shape[0]):
        row = jnp.where(lane == c, values[c], row)
    return row


def look(row, kinds):
    return jnp.take_along_axis(row, kinds, axis=1, mode="promise_in_bounds")


def values_kernel(
    fuel, from_left, from_right, after, fuel_rate, fuel_wind, fuel_heat, rate, drift, heat, three
):
    lane8 = lanes((8, 128))
    tables = [(table(fuel_rate), rate), (table(fuel_wind), drift), (table(fuel_heat), heat)]
    for i in range(3):
        three[8 * i : 8 * i + 8, :] = tables[i][0]

    def own_rows(i, _):
        at = pl.multiple_of(i * 8, 8)
        one = from_left[pl.ds(at, 8), :]
        two = from_right[pl.ds(at, 8), :]
        beside = pltpu.roll(jnp.where(lane8 < HALF, one, two), HALF, 1).astype(jnp.int32)
        for c in range(NL):
            kinds = beside if c == NL - 1 else fuel[pl.ds(at, 8), 128 * c : 128 * c + 128]
            for row, out in tables:
                out[pl.ds(at, 8), 128 * c : 128 * c + 128] = look(row, kinds)
        return 0

    lax.fori_loop(0, FY // 8, own_rows, 0, unroll=4)


def values(fuel, from_left, from_right, after, *names):
    return pl.pallas_call(
        values_kernel,
        in_specs=[VM, VM, VM, ANY, SM, SM, SM],
        out_specs=[VM] * 4,
        out_shape=[f32(FY, COLS)] * 3 + [f32(24, 128)],
        compiler_params=PARAMS,
        name="values",
    )(fuel, from_left, from_right, after, *names)


def slab_kernel(
    level, from_left, from_right, from_up, from_down, held, rate, drift, heat, three,
    level_out, slots,
    phi_a, phi_b, phi_c, edge_rate, edge_drift, edge_heat, east, north, winds, gates, sums, spread, gather,
):
    group = lax.axis_index("grp")
    tile = lax.axis_index("tile")
    first_row = group == 0
    last_row = group == lax.axis_size("grp") - 1
    first_col = tile == 0
    last_col = tile == lax.axis_size("tile") - 1
    lane8 = lanes((8, 128))
    sub8 = lax.broadcasted_iota(jnp.int32, (8, COLS), 0)

    zero = jnp.zeros((PAD, COLS), jnp.float32)
    phi_a[0:PAD, :] = zero
    phi_a[ROWS - PAD : ROWS, :] = zero
    phi_a[TOP - HALO : TOP, :] = from_up[0:HALO, :]
    phi_a[TOP + FY : TOP + FY + HALO, :] = from_down[0:HALO, :]

    def own_rows(i, _):
        at = pl.multiple_of(i * 8, 8)
        to = pl.multiple_of(i * 8 + TOP, 8)
        phi_a[pl.ds(to, 8), 0:FX] = level[pl.ds(at, 8), :]
        one = from_left[pl.ds(at, 8), :]
        two = from_right[pl.ds(at, 8), :]
        phi_a[pl.ds(to, 8), FX:COLS] = jnp.where(lane8 < HALF, two, one)
        return 0

    lax.fori_loop(0, FY // 8, own_rows, 0, unroll=4)
    tables = [
        (three[8 * i : 8 * i + 8, :], out) for i, out in enumerate((edge_rate, edge_drift, edge_heat))
    ]

    def halo_rows(i, _):
        at = pl.multiple_of(i * 8, 8)
        for source, start in ((from_up, 0), (from_down, HALO)):
            to = pl.multiple_of(at + start, 8)
            for c in range(NL):
                kinds = source[pl.ds(pl.multiple_of(at + HALO, 8), 8), 128 * c : 128 * c + 128]
                kinds = kinds.astype(jnp.int32)
                for row, out in tables:
                    out[pl.ds(to, 8), 128 * c : 128 * c + 128] = look(row, kinds)
        return 0

    lax.fori_loop(0, HALO // 8, halo_rows, 0, unroll=3)

    gates[0:8, :] = from_up[2 * HALO : 2 * HALO + 8, :]
    gates[16:24, :] = from_down[2 * HALO : 2 * HALO + 8, :]
    for c in range(FX // 128):
        gates[8:16, 128 * c : 128 * c + 128] = held[2 * AY : 2 * AY + 8, :]
    gates[8:16, FX:COLS] = jnp.where(
        lane8 < HALF, from_right[FY : FY + 8, :], from_left[FY : FY + 8, :]
    )

    row = 2 * HALO + 4
    for comp in range(2):
        base = comp * CR
        for c in range(3):
            at = 128 * (3 * comp + c)
            winds[base + c : base + c + 1, :] = from_up[row : row + 1, at : at + 128]
            below = base + 3 + AY + c
            winds[below : below + 1, :] = from_down[row : row + 1, at : at + 128]
        winds[base + 3 : base + 3 + AY, :] = held[AY * comp : AY * comp + AY, :]
        winds[base + 6 + AY : base + CR, :] = jnp.zeros((CR - 6 - AY, 128), jnp.float32)

    spread[...] = (
        coarse_lane(lanes((128, COLS))) == lax.broadcasted_iota(jnp.int32, (128, COLS), 0)
    ).astype(jnp.bfloat16)
    gather[...] = (
        coarse_lane(lax.broadcasted_iota(jnp.int32, (COLS, 128), 0)) == lanes((COLS, 128))
    ).astype(jnp.bfloat16)

    def expand():
        wide = exact_dot(winds[...], spread[...])
        for comp, out in ((0, east), (1, north)):
            part = wide[comp * CR : comp * CR + CR]
            out[0:CR, :] = jnp.maximum(part, 0.0)
            out[CR : 2 * CR, :] = jnp.minimum(part, 0.0)

    def edges(phi):
        @pl.when(first_row)
        def _():
            phi[TOP - 1 : TOP, :] = phi[TOP : TOP + 1, :]

        @pl.when(last_row)
        def _():
            phi[TOP + FY : TOP + FY + 1, :] = phi[TOP + FY - 1 : TOP + FY, :]

        @pl.when(first_col)
        def _():
            old = phi[:, COLS - 128 : COLS]
            new = jnp.broadcast_to(phi[:, 0:1], (ROWS, 128))
            phi[:, COLS - 128 : COLS] = jnp.where(lanes((ROWS, 128)) == 127, new, old)

        @pl.when(last_col)
        def _():
            old = phi[:, FX : FX + 128]
            new = jnp.broadcast_to(phi[:, FX - 1 : FX], (ROWS, 128))
            phi[:, FX : FX + 128] = jnp.where(lanes((ROWS, 128)) == 0, new, old)

    own = (rate, drift, heat, TOP)
    upper_edge = (edge_rate, edge_drift, edge_heat, TOP - HALO)
    lower_edge = (edge_rate, edge_drift, edge_heat, TOP + FY - HALO)

    def update(phi, at, e, n, gate, fuels):
        before = phi[pl.ds(pl.multiple_of(at - 8, 8), 8), :]
        now = phi[pl.ds(at, 8), :]
        after = phi[pl.ds(pl.multiple_of(at + 8, 8), 8), :]
        south = jnp.where(sub8 == 0, pltpu.roll(before, 1, 0), pltpu.roll(now, 1, 0))
        above = jnp.where(sub8 == 7, pltpu.roll(after, 7, 0), pltpu.roll(now, 7, 0))
        west = pltpu.roll(now, 1, 1)
        east_cell = pltpu.roll(now, COLS - 1, 1)
        back_x = now - west
        ahead_x = east_cell - now
        back_y = now - south
        ahead_y = above - now
        bx = jnp.maximum(back_x, 0.0)
        ax = jnp.minimum(ahead_x, 0.0)
        by = jnp.maximum(back_y, 0.0)
        ay = jnp.minimum(ahead_y, 0.0)
        square = bx * bx + ax * ax + by * by + ay * ay + 1e-12
        slope = square * lax.rsqrt(square)
        carry = e[0] * back_x + e[1] * ahead_x + n[0] * back_y + n[1] * ahead_y
        there = pl.multiple_of(at - fuels[3], 8)
        change = fuels[0][pl.ds(there, 8), :] * slope + fuels[1][pl.ds(there, 8), :] * carry
        return now - gate * change

    def wind_row(ref, row):
        return tuple(jnp.broadcast_to(ref[pl.ds(row + part, 1), :], (8, COLS)) for part in (0, CR))

    def mix(a, b):
        return tuple(jnp.where(sub8 < 4, one, two) for one, two in zip(a, b))

    def band(phi, m, k, region, fuels, finish):
        at = pl.multiple_of(2 * PAD + 40 * m, 8)
        gate = jnp.broadcast_to(gates[region * 8 + k : region * 8 + k + 1, :], (8, COLS))
        row = 2 * m + 1
        for t in range(5):
            if t == 2:
                e = mix(wind_row(east, row), wind_row(east, row + 1))
                n = mix(wind_row(north, row), wind_row(north, row + 1))
            else:
                e, n = (wind_row(ref, row + t // 3) for ref in (east, north))
            here = pl.multiple_of(at + 8 * t, 8)
            finish(here, update(phi, here, e, n, gate, fuels), fuels)

    def tile_rows(phi, at, row, region, k, fuels):
        gate = jnp.broadcast_to(gates[region * 8 + k : region * 8 + k + 1, :], (8, COLS))
        return update(phi, at, wind_row(east, row), wind_row(north, row), gate, fuels)

    def own_bands(body):
        def step(m, _):
            body(m, 1, own)
            return 0

        lax.fori_loop(1, 9, step, 0)

    def store_to(out):
        def finish(here, new, fuels):
            out[pl.ds(here, 8), :] = new

        return finish

    def flux_band(before, phi, out, k):
        def body(m, region, fuels):
            parts = []

            def finish(here, new, fuels):
                if out is not None:
                    out[pl.ds(here, 8), :] = new
                else:
                    level_out[pl.ds(pl.multiple_of(here - TOP, 8), 8), :] = new[:, 0:FX]
                old = before[pl.ds(here, 8), :]
                there = pl.multiple_of(here - fuels[3], 8)
                parts.append(fuels[2][pl.ds(there, 8), :] * (jnp.tanh(old) - jnp.tanh(new)))

            band(phi, m, k, region, fuels, finish)
            low = parts[0] + parts[1] + jnp.where(sub8 < 4, parts[2], 0.0)
            high = parts[3] + parts[4] + jnp.where(sub8 >= 4, parts[2], 0.0)
            sums[pl.ds(2 * m + 1, 1), :] = jnp.sum(low, axis=0, keepdims=True)
            sums[pl.ds(2 * m + 2, 1), :] = jnp.sum(high, axis=0, keepdims=True)

        return body

    def pooled():
        return exact_dot(sums[...], gather[...]) * (0.5 / (R * R))

    lane_c = lanes((CR, 128))
    row_c = lax.broadcasted_iota(jnp.int32, (CR, 128), 0)
    sums[...] = jnp.zeros((CR, COLS), jnp.float32)

    expand()
    edges(phi_a)
    phi_b[PAD : PAD + 8, :] = tile_rows(phi_a, PAD, 0, 0, 0, upper_edge)
    phi_b[ROWS - 2 * PAD : ROWS - PAD, :] = tile_rows(phi_a, ROWS - 2 * PAD, AY + 5, 2, 0, lower_edge)
    band(phi_a, 0, 0, 0, upper_edge, store_to(phi_b))
    band(phi_a, 9, 0, 2, lower_edge, store_to(phi_b))
    own_bands(lambda m, region, fuels: band(phi_a, m, 0, region, fuels, store_to(phi_b)))
    edges(phi_b)
    second = flux_band(phi_a, phi_b, phi_c, 1)
    second(0, 0, upper_edge)
    second(9, 2, lower_edge)
    own_bands(second)
    edges(phi_c)

    flux0 = pooled()
    ahead = jnp.where(jnp.logical_or(lane_c == AX - 1, lane_c == LEFT), flux0, pltpu.roll(flux0, 127, 1))
    back = jnp.where(jnp.logical_or(lane_c == 0, lane_c == RIGHT), flux0, pltpu.roll(flux0, 1, 1))
    last_rows = jnp.logical_or(row_c == 2, row_c == AY + 2)
    first_rows = jnp.logical_or(row_c == 3, row_c == AY + 3)
    below = jnp.where(last_rows, flux0, pltpu.roll(flux0, CR - 1, 0))
    upper = jnp.where(first_rows, flux0, pltpu.roll(flux0, 1, 0))
    winds[0:CR, :] = 0.9 * winds[0:CR, :] + 20.0 * (ahead - back)
    winds[CR : 2 * CR, :] = 0.9 * winds[CR : 2 * CR, :] + 20.0 * (below - upper)
    expand()

    top = TOP - 8
    bottom = TOP + FY
    phi_b[top : top + 8, :] = tile_rows(phi_c, top, 2, 0, 2, upper_edge)
    phi_b[bottom : bottom + 8, :] = tile_rows(phi_c, bottom, AY + 3, 2, 2, lower_edge)
    own_bands(lambda m, region, fuels: band(phi_c, m, 2, region, fuels, store_to(phi_b)))
    edges(phi_b)
    own_bands(flux_band(phi_c, phi_b, None, 3))
    total = 0.9 * flux0 + pooled()

    packed = jnp.zeros((4, 128), jnp.float32)
    lane4 = lanes((4, 128))
    for q in range(4):
        moved = pltpu.roll(total, 32 * q, 1)[3 + 4 * q : 7 + 4 * q]
        packed = jnp.where(lane4 // AX == q, moved, packed)
    for k in range(NX * NZ):
        slots[k] = packed


def slab(*args):
    big = pltpu.VMEM((ROWS, COLS), jnp.float32)
    edge = pltpu.VMEM((2 * HALO, COLS), jnp.float32)
    return pl.pallas_call(
        slab_kernel,
        in_specs=[VM] * 10,
        out_specs=[VM, VM],
        out_shape=[f32(FY, FX), f32(NX * NZ, 4, 128)],
        scratch_shapes=[big] * 3
        + [edge] * 3
        + [
            pltpu.VMEM((2 * CR, COLS), jnp.float32),
            pltpu.VMEM((2 * CR, COLS), jnp.float32),
            pltpu.VMEM((2 * CR, 128), jnp.float32),
            pltpu.VMEM((CR, COLS), jnp.float32),
            pltpu.VMEM((CR, COLS), jnp.float32),
            pltpu.VMEM((128, COLS), jnp.bfloat16),
            pltpu.VMEM((COLS, 128), jnp.bfloat16),
        ],
        compiler_params=PARAMS,
        name="slab",
    )(*args)


def final_kernel(owner, received, wind, wind_out):
    tile = lax.axis_index("tile")
    source = jnp.int32(0)
    for t in range(NX * NZ):
        source = jnp.where(owner[0, t] == tile, t, source)
    block = received[source]
    flux = jnp.concatenate([pltpu.roll(block, (128 - 32 * q) % 128, 1) for q in range(4)], axis=0)
    lane = lanes((AY, 128))
    row = lax.broadcasted_iota(jnp.int32, (AY, 128), 0)
    ahead = jnp.where(lane == AX - 1, flux, pltpu.roll(flux, 127, 1))
    back = jnp.where(lane == 0, flux, pltpu.roll(flux, 1, 1))
    below = jnp.where(row == AY - 1, flux, pltpu.roll(flux, AY - 1, 0))
    upper = jnp.where(row == 0, flux, pltpu.roll(flux, 1, 0))
    wind_out[0] = 0.81 * wind[0] + 20.0 * (ahead - back)[:, 0:AX]
    wind_out[1] = 0.81 * wind[1] + 20.0 * (below - upper)[:, 0:AX]


def final(owner, received, wind):
    return pl.pallas_call(
        final_kernel, in_specs=[SM, VM, VM], out_specs=VM, out_shape=f32(2, AY, AX), name="final"
    )(owner, received, wind)


def shift(value, axis, step):
    size = lax.axis_size(axis)
    pairs = [(i, i + step) for i in range(size) if 0 <= i + step < size]
    return lax.ppermute(value, axis, pairs)


def shards(level, fuel, wind, owner, active, fuel_rate, fuel_wind, fuel_heat):
    active = jnp.transpose(active, (1, 2, 0))
    to_left, to_right = strips(level, fuel, active)
    from_right = shift(to_left, "tile", -1)
    from_left = shift(to_right, "tile", 1)
    blocks = blocks_of(wind, to_left)
    blocks, from_left, from_right = lax.optimization_barrier((blocks, from_left, from_right))
    blocks = lax.all_to_all(blocks, "tile", 0, 0, tiled=True)
    held, to_up, to_down = rows(level, fuel, from_left, from_right, blocks, owner, active)
    from_down = shift(to_up, "grp", -1)
    from_up = shift(to_down, "grp", 1)
    coefficients = values(fuel, from_left, from_right, held, fuel_rate, fuel_wind, fuel_heat)
    level_out, flux = slab(level, from_left, from_right, from_up, from_down, held, *coefficients)
    flux = lax.all_to_all(flux, "tile", 0, 0, tiled=True)
    return (level_out, final(owner, flux, wind))


def solution(mesh):
    in_specs = (
        P("grp", "tile"),
        P("grp", "tile"),
        P(None, "grp", "tile"),
        P("grp", None),
        P(None, "grp", "tile"),
        P(),
        P(),
        P(),
    )
    out_specs = (P("grp", "tile"), P(None, "grp", "tile"))
    return jax.shard_map(shards, mesh=mesh, in_specs=in_specs, out_specs=out_specs, check_vma=False)
```

```python
import jax
import jax.numpy as jnp
from jax import lax
from jax.experimental import pallas as pl
from jax.experimental.pallas import tpu as pltpu
from jax.sharding import PartitionSpec as P

R = 20
AY = 16
AX = 32
FY = 320
FX = 640
STEPS = 2
SUBSTEPS = 2
NZ = 16
NX = 4
HALO = 48
HALF = 64
PAD = 8
TOP = PAD + HALO
ROWS = TOP + FY + HALO + PAD
COLS = FX + 2 * HALF
NL = COLS // 128
RIGHT = 40
LEFT = 51
CR = 24

VM = pl.BlockSpec(memory_space=pltpu.VMEM)
SM = pl.BlockSpec(memory_space=pltpu.SMEM)
ANY = pl.BlockSpec(memory_space=pl.ANY)
SMALL = pltpu.CompilerParams(vmem_limit_bytes=4 * 1024 * 1024)
LARGE = pltpu.CompilerParams(vmem_limit_bytes=12 * 1024 * 1024)


def lanes(shape):
    return lax.broadcasted_iota(jnp.int32, shape, 1)


def f32(*shape):
    return jax.ShapeDtypeStruct(shape, jnp.float32)


def thirds(x):
    high = x.astype(jnp.bfloat16)
    rest = x - high.astype(jnp.float32)
    middle = rest.astype(jnp.bfloat16)
    low = (rest - middle.astype(jnp.float32)).astype(jnp.bfloat16)
    return jnp.concatenate([high, middle, low], axis=0)


def exact_dot(x, onehot):
    n = x.shape[0]
    out = jnp.dot(thirds(x), onehot, preferred_element_type=jnp.float32)
    return out[:n] + out[n : 2 * n] + out[2 * n :]


def coarse_lane(fine):
    own = fine // R
    right = RIGHT + (fine - FX) // R
    left = LEFT - (COLS - 1 - fine) // R
    edge = jnp.where(fine < FX + 3 * R, right, jnp.where(fine >= COLS - 3 * R, left, -1))
    return jnp.where(fine < FX, own, edge)


def strips_kernel(level, fuel, active, after, to_left, to_right, done, left_level, right_level, left_fuel, right_fuel, arrived):
    first, last = pl.ds(0, 128), pl.ds(FX - 128, 128)
    moves = [
        pltpu.make_async_copy(source.at[:, part], buf, arrived.at[i])
        for i, (source, part, buf) in enumerate((
            (level, first, left_level), (fuel, first, left_fuel),
            (level, last, right_level), (fuel, last, right_fuel),
        ))
    ]
    for move in moves:
        move.start()
    done[...] = jnp.zeros((8, 128), jnp.float32)
    for k in range(8):
        row = jnp.full((1, 128), flag_of(active, k), jnp.float32)
        to_left[FY + k : FY + k + 1, :] = row
        to_right[FY + k : FY + k + 1, :] = row
    lane = lanes((FY, 128))
    moves[0].wait()
    moves[1].wait()
    to_left[0:FY, :] = jnp.where(
        lane < HALF, left_level[...], pltpu.roll(left_fuel[...].astype(jnp.float32), HALF, 1)
    )
    moves[2].wait()
    moves[3].wait()
    to_right[0:FY, :] = jnp.where(
        lane >= HALF, right_level[...], pltpu.roll(right_fuel[...].astype(jnp.float32), HALF, 1)
    )


def strips(level, fuel, active, after):
    strip = pltpu.VMEM((FY, 128), jnp.float32)
    kinds = pltpu.VMEM((FY, 128), jnp.int32)
    return pl.pallas_call(
        strips_kernel,
        in_specs=[ANY, ANY, SM, ANY],
        out_specs=[VM, VM, VM],
        out_shape=[f32(FY + 8, 128), f32(FY + 8, 128), f32(8, 128)],
        scratch_shapes=[strip, strip, kinds, kinds, pltpu.SemaphoreType.DMA((4,))],
        name="strips",
    )(level, fuel, active, after)


def flag_of(active, k):
    return (active[0, 0, min(k, STEPS * SUBSTEPS - 1)] > 0).astype(jnp.float32)


def blocks_kernel(wind, slots):
    parts = [wind[0, 0:8, :], wind[0, 8:16, :], wind[1, 0:8, :], wind[1, 8:16, :]]
    block = jnp.concatenate(parts, axis=1)
    for k in range(NX * NZ):
        slots[k] = block


def blocks_of(wind):
    return pl.pallas_call(
        blocks_kernel, in_specs=[VM], out_specs=VM, out_shape=f32(NX * NZ, 8, 128), name="blocks"
    )(wind)


def rows_kernel(
    from_left, from_right, blocks, owner, active, up, down, held, to_up, to_down,
):
    tile = lax.axis_index("tile")
    lane = lanes((HALO, 128))
    lane8 = lanes((8, 128))
    main = blocks[owner[0, tile]]
    left = blocks[owner[0, jnp.maximum(tile - 1, 0)]]
    right = blocks[owner[0, jnp.minimum(tile + 1, NX * NZ - 1)]]
    is_left = jnp.logical_and(lane8 >= LEFT - 2, lane8 <= LEFT)
    is_right = jnp.logical_and(lane8 >= RIGHT, lane8 <= RIGHT + 2)
    for q in range(4):
        own = pltpu.roll(main, (128 - 32 * q) % 128, 1)
        one = pltpu.roll(left, (LEFT - 31 - 32 * q) % 128, 1)
        two = pltpu.roll(right, (RIGHT - 32 * q) % 128, 1)
        held[8 * q : 8 * q + 8, :] = jnp.where(
            lane8 < AX, own, jnp.where(is_left, one, jnp.where(is_right, two, 0.0))
        )
    for k in range(8):
        held[2 * AY + k : 2 * AY + k + 1, :] = jnp.full((1, 128), flag_of(active, k), jnp.float32)
    for out, part, start, coarse in ((to_up, up, 0, 0), (to_down, down, FY - HALO, AY - 3)):
        out[0 : 2 * HALO, 0:FX] = part[...]
        one = from_left[start : start + HALO, :]
        two = from_right[start : start + HALO, :]
        out[0:HALO, FX:COLS] = jnp.where(lane < HALF, two, one)
        out[HALO : 2 * HALO, FX:COLS] = pltpu.roll(jnp.where(lane < HALF, one, two), HALF, 1)
        for k in range(4):
            row = 2 * HALO + k
            out[row : row + 1, 0:FX] = jnp.full((1, FX), flag_of(active, k), jnp.float32)
            out[row : row + 1, FX:COLS] = jnp.where(
                lane[0:1] < HALF, from_right[FY + k : FY + k + 1, :], from_left[FY + k : FY + k + 1, :]
            )
        row = 2 * HALO + 4
        for c in range(6):
            at = (c // 3) * AY + coarse + c % 3
            out[row : row + 1, 128 * c : 128 * c + 128] = held[at : at + 1, :]
        out[row + 1 : row + 4, :] = jnp.zeros((3, COLS), jnp.float32)


def rows(from_left, from_right, blocks, owner, active, up, down):
    shape = (2 * HALO + 8, COLS)
    return pl.pallas_call(
        rows_kernel,
        in_specs=[VM] * 3 + [SM, SM, VM, VM],
        out_specs=[VM, VM, VM],
        out_shape=[f32(2 * AY + 8, 128), f32(*shape), f32(*shape)],
        compiler_params=SMALL,
        name="rows",
    )(from_left, from_right, blocks, owner, active, up, down)


def table(values):
    lane = lanes((8, 128))
    row = jnp.zeros((8, 128), jnp.float32)
    for c in range(values.shape[0]):
        row = jnp.where(lane == c, values[c], row)
    return row


def look(row, kinds):
    return jnp.take_along_axis(row, kinds, axis=1, mode="promise_in_bounds")


def values_kernel(
    level, fuel, after, fuel_rate, fuel_wind, fuel_heat, rate, drift, three, to_up, to_down, kinds, arrived
):
    moves = [
        pltpu.make_async_copy(source, buf, arrived.at[i])
        for i, (source, buf) in enumerate((
            (fuel, kinds),
            (level.at[0:HALO, :], to_up.at[0:HALO, :]),
            (level.at[FY - HALO : FY, :], to_down.at[0:HALO, :]),
        ))
    ]
    for move in moves:
        move.start()
    tables = [table(fuel_rate), table(fuel_wind), table(fuel_heat)]
    for i in range(3):
        three[8 * i : 8 * i + 8, :] = tables[i]
    moves[0].wait()
    for out, start in ((to_up, 0), (to_down, FY - HALO)):
        out[HALO : 2 * HALO, :] = kinds[start : start + HALO, :].astype(jnp.float32)

    def own_rows(i):
        at = pl.multiple_of(i * 8, 8)
        return [(kinds[pl.ds(at, 8), c : c + 128], at, c) for c in range(0, FX, 128)]

    look_edges(own_rows, tables[0:2], (rate, drift), FY // 8)
    moves[1].wait()
    moves[2].wait()


def values(level, fuel, after, *names):
    shape = (2 * HALO, FX)
    return pl.pallas_call(
        values_kernel,
        in_specs=[ANY, ANY, ANY, SM, SM, SM],
        out_specs=[VM] * 5,
        out_shape=[f32(FY, FX)] * 2 + [f32(24, 128), f32(*shape), f32(*shape)],
        scratch_shapes=[pltpu.VMEM((FY, FX), jnp.int32), pltpu.SemaphoreType.DMA((3,))],
        name="values",
    )(level, fuel, after, *names)


def look_edges(source, tables, outs, steps):
    def body(i, _):
        for kinds, at, col in source(i):
            for row, out in zip(tables, outs):
                out[pl.ds(at, 8), col : col + 128] = look(row, kinds)
        return 0

    lax.fori_loop(0, steps, body, 0, unroll=min(steps, 4))


def level_rows(phi, first, level, from_left, from_right):
    lane8 = lanes((8, 128))

    def own_rows(i, _):
        at = pl.multiple_of(i * 8, 8)
        to = pl.multiple_of(i * 8 + first, 8)
        phi[pl.ds(to, 8), 0:FX] = level[pl.ds(at, 8), :]
        one = from_left[pl.ds(at, 8), :]
        two = from_right[pl.ds(at, 8), :]
        phi[pl.ds(to, 8), FX:COLS] = jnp.where(lane8 < HALF, two, one)
        return 0

    lax.fori_loop(0, FY // 8, own_rows, 0, unroll=4)


def own_flags(out, held, from_left, from_right):
    for c in range(FX // 128):
        out[:, 128 * c : 128 * c + 128] = held[2 * AY : 2 * AY + 8, :]
    out[:, FX:COLS] = jnp.where(
        lanes((8, 128)) < HALF, from_right[FY : FY + 8, :], from_left[FY : FY + 8, :]
    )


def spread_matrix():
    return (
        coarse_lane(lanes((128, COLS))) == lax.broadcasted_iota(jnp.int32, (128, COLS), 0)
    ).astype(jnp.bfloat16)


def expand(winds, spread, east, north):
    wide = exact_dot(winds[...], spread[...])
    rows_each = winds.shape[0] // 2
    for comp, out in ((0, east), (1, north)):
        part = wide[comp * rows_each : comp * rows_each + rows_each]
        out[0:rows_each, :] = jnp.maximum(part, 0.0)
        out[rows_each : 2 * rows_each, :] = jnp.minimum(part, 0.0)


def edge_columns(phi):
    tile = lax.axis_index("tile")
    count = phi.shape[0]

    @pl.when(tile == 0)
    def _():
        old = phi[:, COLS - 128 : COLS]
        new = jnp.broadcast_to(phi[:, 0:1], (count, 128))
        phi[:, COLS - 128 : COLS] = jnp.where(lanes((count, 128)) == 127, new, old)

    @pl.when(tile == lax.axis_size("tile") - 1)
    def _():
        old = phi[:, FX : FX + 128]
        new = jnp.broadcast_to(phi[:, FX - 1 : FX], (count, 128))
        phi[:, FX : FX + 128] = jnp.where(lanes((count, 128)) == 0, new, old)


def fuel_value(refs, at):
    parts = [ref[pl.ds(at, 8), :] for ref in refs]
    return parts[0] if len(parts) == 1 else jnp.concatenate(parts, axis=1)


def update(phi, at, e, n, gate, fuels):
    sub8 = lax.broadcasted_iota(jnp.int32, (8, COLS), 0)
    before = phi[pl.ds(pl.multiple_of(at - 8, 8), 8), :]
    now = phi[pl.ds(at, 8), :]
    after = phi[pl.ds(pl.multiple_of(at + 8, 8), 8), :]
    south = jnp.where(sub8 == 0, pltpu.roll(before, 1, 0), pltpu.roll(now, 1, 0))
    above = jnp.where(sub8 == 7, pltpu.roll(after, 7, 0), pltpu.roll(now, 7, 0))
    west = pltpu.roll(now, 1, 1)
    east_cell = pltpu.roll(now, COLS - 1, 1)
    back_x = now - west
    ahead_x = east_cell - now
    back_y = now - south
    ahead_y = above - now
    bx = jnp.maximum(back_x, 0.0)
    ax = jnp.minimum(ahead_x, 0.0)
    by = jnp.maximum(back_y, 0.0)
    ay = jnp.minimum(ahead_y, 0.0)
    square = bx * bx + ax * ax + by * by + ay * ay + 1e-12
    slope = square * lax.rsqrt(square)
    carry = e[0] * back_x + e[1] * ahead_x + n[0] * back_y + n[1] * ahead_y
    there = pl.multiple_of(at - fuels[3], 8)
    change = fuel_value(fuels[0], there) * slope + fuel_value(fuels[1], there) * carry
    return now - gate * change


def wind_row(ref, row):
    half = ref.shape[0] // 2
    return tuple(jnp.broadcast_to(ref[pl.ds(row + part, 1), :], (8, COLS)) for part in (0, half))


def mix(a, b):
    sub8 = lax.broadcasted_iota(jnp.int32, (8, COLS), 0)
    return tuple(jnp.where(sub8 < 4, one, two) for one, two in zip(a, b))


def band(phi, at, row, winds, gate, fuels, finish):
    east, north = winds
    for t in range(5):
        if t == 2:
            e = mix(wind_row(east, row), wind_row(east, row + 1))
            n = mix(wind_row(north, row), wind_row(north, row + 1))
        else:
            e, n = (wind_row(ref, row + t // 3) for ref in (east, north))
        here = pl.multiple_of(at + 8 * t, 8)
        finish(here, update(phi, here, e, n, gate, fuels), fuels)


def early_kernel(
    level, fuel, from_left, from_right, held, rate, drift, three, once, heat, side_rate, side_drift, side_heat,
    phi, east, north, winds, gates, spread,
):
    lane8 = lanes((8, 128))
    tables = [three[8 * i : 8 * i + 8, :] for i in range(3)]

    def beside(i):
        at = pl.multiple_of(i * 8, 8)
        kinds = jnp.where(lane8 < HALF, from_left[pl.ds(at, 8), :], from_right[pl.ds(at, 8), :])
        return [(pltpu.roll(kinds, HALF, 1).astype(jnp.int32), at, 0)]

    def own_rows(i):
        at = pl.multiple_of(i * 8, 8)
        return [(fuel[pl.ds(at, 8), c : c + 128], at, c) for c in range(0, FX, 128)]

    look_edges(beside, tables, (side_rate, side_drift, side_heat), FY // 8)
    look_edges(own_rows, tables[2:3], (heat,), FY // 8)
    phi[0:8, :] = jnp.zeros((8, COLS), jnp.float32)
    phi[FY + 8 : FY + 16, :] = jnp.zeros((8, COLS), jnp.float32)
    level_rows(phi, 8, level, from_left, from_right)
    own_flags(gates, held, from_left, from_right)
    winds[...] = held[0 : 2 * AY, :]
    spread[...] = spread_matrix()
    expand(winds, spread, east, north)
    edge_columns(phi)
    gate = jnp.broadcast_to(gates[0:1, :], (8, COLS))
    fuels = ((rate, side_rate), (drift, side_drift), None, 8)

    def store(here, new, fuels):
        once[pl.ds(pl.multiple_of(here - 8, 8), 8), :] = new

    def step(m, _):
        at = pl.multiple_of(40 * m + 8, 8)
        band(phi, at, 2 * m, (east, north), gate, fuels, store)
        return 0

    lax.fori_loop(0, FY // 40, step, 0)


def early(*args):
    return pl.pallas_call(
        early_kernel,
        in_specs=[VM] * 8,
        out_specs=[VM] * 5,
        out_shape=[f32(FY, COLS), f32(FY, FX)] + [f32(FY, 128)] * 3,
        scratch_shapes=[
            pltpu.VMEM((FY + 16, COLS), jnp.float32),
            pltpu.VMEM((2 * AY, COLS), jnp.float32),
            pltpu.VMEM((2 * AY, COLS), jnp.float32),
            pltpu.VMEM((2 * AY, 128), jnp.float32),
            pltpu.VMEM((8, COLS), jnp.float32),
            pltpu.VMEM((128, COLS), jnp.bfloat16),
        ],
        compiler_params=SMALL,
        name="early",
    )(*args)


def slab_kernel(
    level, from_left, from_right, from_up, from_down, held, rate, drift, heat, three,
    once, side_rate, side_drift, side_heat,
    level_out, slots,
    phi_a, phi_b, phi_c, edge_rate, edge_drift, edge_heat, east, north, winds, gates, sums, spread, gather,
):
    group = lax.axis_index("grp")
    sub8 = lax.broadcasted_iota(jnp.int32, (8, COLS), 0)

    zero = jnp.zeros((PAD, COLS), jnp.float32)
    phi_a[0:PAD, :] = zero
    phi_a[ROWS - PAD : ROWS, :] = zero
    phi_a[TOP - HALO : TOP, :] = from_up[0:HALO, :]
    phi_a[TOP + FY : TOP + FY + HALO, :] = from_down[0:HALO, :]
    level_rows(phi_a, TOP, level, from_left, from_right)

    def halo(i):
        at = pl.multiple_of(i * 8, 8)
        found = []
        for source, start in ((from_up, 0), (from_down, HALO)):
            for c in range(NL):
                kinds = source[pl.ds(pl.multiple_of(at + HALO, 8), 8), 128 * c : 128 * c + 128]
                found.append((kinds.astype(jnp.int32), pl.multiple_of(at + start, 8), 128 * c))
        return found

    tables = [three[8 * i : 8 * i + 8, :] for i in range(3)]
    look_edges(halo, tables, (edge_rate, edge_drift, edge_heat), HALO // 8)

    gates[0:8, :] = from_up[2 * HALO : 2 * HALO + 8, :]
    gates[16:24, :] = from_down[2 * HALO : 2 * HALO + 8, :]
    own_flags(gates.at[8:16, :], held, from_left, from_right)

    row = 2 * HALO + 4
    for comp in range(2):
        base = comp * CR
        for c in range(3):
            at = 128 * (3 * comp + c)
            winds[base + c : base + c + 1, :] = from_up[row : row + 1, at : at + 128]
            below = base + 3 + AY + c
            winds[below : below + 1, :] = from_down[row : row + 1, at : at + 128]
        winds[base + 3 : base + 3 + AY, :] = held[AY * comp : AY * comp + AY, :]
        winds[base + 6 + AY : base + CR, :] = jnp.zeros((CR - 6 - AY, 128), jnp.float32)

    spread[...] = spread_matrix()
    gather[...] = (
        coarse_lane(lax.broadcasted_iota(jnp.int32, (COLS, 128), 0)) == lanes((COLS, 128))
    ).astype(jnp.bfloat16)

    def edges(phi):
        @pl.when(group == 0)
        def _():
            phi[TOP - 1 : TOP, :] = phi[TOP : TOP + 1, :]

        @pl.when(group == lax.axis_size("grp") - 1)
        def _():
            phi[TOP + FY : TOP + FY + 1, :] = phi[TOP + FY - 1 : TOP + FY, :]

        edge_columns(phi)

    own = ((rate, side_rate), (drift, side_drift), (heat, side_heat), TOP)
    upper_edge = ((edge_rate,), (edge_drift,), (edge_heat,), TOP - HALO)
    lower_edge = ((edge_rate,), (edge_drift,), (edge_heat,), TOP + FY - HALO)
    both = (east, north)

    def gate_row(region, k):
        return jnp.broadcast_to(gates[region * 8 + k : region * 8 + k + 1, :], (8, COLS))

    def forty(phi, m, k, region, fuels, finish):
        at = pl.multiple_of(2 * PAD + 40 * m, 8)
        band(phi, at, 2 * m + 1, both, gate_row(region, k), fuels, finish)

    def tile_rows(phi, out, at, row, region, k, fuels):
        new = update(phi, at, wind_row(east, row), wind_row(north, row), gate_row(region, k), fuels)
        out[at : at + 8, :] = new

    def own_bands(body):
        def step(m, _):
            body(m, 1, own)
            return 0

        lax.fori_loop(1, 9, step, 0)

    def store_to(out):
        def finish(here, new, fuels):
            out[pl.ds(here, 8), :] = new

        return finish

    def flux_band(before, phi, out, k):
        def body(m, region, fuels):
            parts = []

            def finish(here, new, fuels):
                if out is not None:
                    out[pl.ds(here, 8), :] = new
                else:
                    level_out[pl.ds(pl.multiple_of(here - TOP, 8), 8), :] = new[:, 0:FX]
                old = before[pl.ds(here, 8), :]
                there = pl.multiple_of(here - fuels[3], 8)
                parts.append(fuel_value(fuels[2], there) * (jnp.tanh(old) - jnp.tanh(new)))

            forty(phi, m, k, region, fuels, finish)
            low = parts[0] + parts[1] + jnp.where(sub8 < 4, parts[2], 0.0)
            high = parts[3] + parts[4] + jnp.where(sub8 >= 4, parts[2], 0.0)
            sums[pl.ds(2 * m + 1, 1), :] = jnp.sum(low, axis=0, keepdims=True)
            sums[pl.ds(2 * m + 2, 1), :] = jnp.sum(high, axis=0, keepdims=True)

        return body

    def pooled():
        return exact_dot(sums[...], gather[...]) * (0.5 / (R * R))

    lane_c = lanes((CR, 128))
    row_c = lax.broadcasted_iota(jnp.int32, (CR, 128), 0)
    sums[...] = jnp.zeros((CR, COLS), jnp.float32)

    expand(winds, spread, east, north)
    edges(phi_a)
    phi_b[TOP : TOP + FY, :] = once[...]
    tile_rows(phi_a, phi_b, PAD, 0, 0, 0, upper_edge)
    forty(phi_a, 0, 0, 0, upper_edge, store_to(phi_b))
    tile_rows(phi_a, phi_b, TOP, 3, 1, 0, own)
    tile_rows(phi_a, phi_b, TOP + FY - 8, AY + 2, 1, 0, own)
    forty(phi_a, 9, 0, 2, lower_edge, store_to(phi_b))
    tile_rows(phi_a, phi_b, ROWS - 2 * PAD, AY + 5, 2, 0, lower_edge)
    edges(phi_b)
    second = flux_band(phi_a, phi_b, phi_c, 1)
    second(0, 0, upper_edge)
    second(9, 2, lower_edge)
    own_bands(second)
    edges(phi_c)

    flux0 = pooled()
    ahead = jnp.where(jnp.logical_or(lane_c == AX - 1, lane_c == LEFT), flux0, pltpu.roll(flux0, 127, 1))
    back = jnp.where(jnp.logical_or(lane_c == 0, lane_c == RIGHT), flux0, pltpu.roll(flux0, 1, 1))
    last_rows = jnp.logical_or(row_c == 2, row_c == AY + 2)
    first_rows = jnp.logical_or(row_c == 3, row_c == AY + 3)
    below = jnp.where(last_rows, flux0, pltpu.roll(flux0, CR - 1, 0))
    upper = jnp.where(first_rows, flux0, pltpu.roll(flux0, 1, 0))
    winds[0:CR, :] = 0.9 * winds[0:CR, :] + 20.0 * (ahead - back)
    winds[CR : 2 * CR, :] = 0.9 * winds[CR : 2 * CR, :] + 20.0 * (below - upper)
    expand(winds, spread, east, north)

    tile_rows(phi_c, phi_b, TOP - 8, 2, 0, 2, upper_edge)
    tile_rows(phi_c, phi_b, TOP + FY, AY + 3, 2, 2, lower_edge)
    own_bands(lambda m, region, fuels: forty(phi_c, m, 2, region, fuels, store_to(phi_b)))
    edges(phi_b)
    own_bands(flux_band(phi_c, phi_b, None, 3))
    total = 0.9 * flux0 + pooled()

    packed = jnp.zeros((4, 128), jnp.float32)
    lane4 = lanes((4, 128))
    for q in range(4):
        moved = pltpu.roll(total, 32 * q, 1)[3 + 4 * q : 7 + 4 * q]
        packed = jnp.where(lane4 // AX == q, moved, packed)
    for k in range(NX * NZ):
        slots[k] = packed


def slab(*args):
    big = pltpu.VMEM((ROWS, COLS), jnp.float32)
    edge = pltpu.VMEM((2 * HALO, COLS), jnp.float32)
    return pl.pallas_call(
        slab_kernel,
        in_specs=[VM] * 14,
        out_specs=[VM, VM],
        out_shape=[f32(FY, FX), f32(NX * NZ, 4, 128)],
        scratch_shapes=[big] * 3
        + [edge] * 3
        + [
            pltpu.VMEM((2 * CR, COLS), jnp.float32),
            pltpu.VMEM((2 * CR, COLS), jnp.float32),
            pltpu.VMEM((2 * CR, 128), jnp.float32),
            pltpu.VMEM((CR, COLS), jnp.float32),
            pltpu.VMEM((CR, COLS), jnp.float32),
            pltpu.VMEM((128, COLS), jnp.bfloat16),
            pltpu.VMEM((COLS, 128), jnp.bfloat16),
        ],
        compiler_params=LARGE,
        name="slab",
    )(*args)


def final_kernel(owner, received, wind, wind_out):
    tile = lax.axis_index("tile")
    source = jnp.int32(0)
    for t in range(NX * NZ):
        source = jnp.where(owner[0, t] == tile, t, source)
    block = received[source]
    flux = jnp.concatenate([pltpu.roll(block, (128 - 32 * q) % 128, 1) for q in range(4)], axis=0)
    lane = lanes((AY, 128))
    row = lax.broadcasted_iota(jnp.int32, (AY, 128), 0)
    ahead = jnp.where(lane == AX - 1, flux, pltpu.roll(flux, 127, 1))
    back = jnp.where(lane == 0, flux, pltpu.roll(flux, 1, 1))
    below = jnp.where(row == AY - 1, flux, pltpu.roll(flux, AY - 1, 0))
    upper = jnp.where(row == 0, flux, pltpu.roll(flux, 1, 0))
    wind_out[0] = 0.81 * wind[0] + 20.0 * (ahead - back)[:, 0:AX]
    wind_out[1] = 0.81 * wind[1] + 20.0 * (below - upper)[:, 0:AX]


def final(owner, received, wind):
    return pl.pallas_call(
        final_kernel, in_specs=[SM, VM, VM], out_specs=VM, out_shape=f32(2, AY, AX),
        compiler_params=SMALL, name="final"
    )(owner, received, wind)


def shift(value, axis, step):
    size = lax.axis_size(axis)
    pairs = [(i, i + step) for i in range(size) if 0 <= i + step < size]
    return lax.ppermute(value, axis, pairs)


def shards(level, fuel, wind, owner, active, fuel_rate, fuel_wind, fuel_heat):
    active = jnp.transpose(active, (1, 2, 0))
    mine = blocks_of(wind)
    blocks = lax.all_to_all(mine, "tile", 0, 0, tiled=True)
    to_left, to_right, done = strips(level, fuel, active, mine)
    from_right = shift(to_left, "tile", -1)
    from_left = shift(to_right, "tile", 1)
    rate, drift, three, up, down = values(level, fuel, done, fuel_rate, fuel_wind, fuel_heat)
    held, to_up, to_down = rows(from_left, from_right, blocks, owner, active, up, down)
    from_down = shift(to_up, "grp", -1)
    from_up = shift(to_down, "grp", 1)
    once, heat, *sides = early(level, fuel, from_left, from_right, held, rate, drift, three)
    level_out, flux = slab(
        level, from_left, from_right, from_up, from_down, held, rate, drift, heat, three, once, *sides
    )
    flux = lax.all_to_all(flux, "tile", 0, 0, tiled=True)
    return (level_out, final(owner, flux, wind))


def solution(mesh):
    in_specs = (
        P("grp", "tile"),
        P("grp", "tile"),
        P(None, "grp", "tile"),
        P("grp", None),
        P(None, "grp", "tile"),
        P(),
        P(),
        P(),
    )
    out_specs = (P("grp", "tile"), P(None, "grp", "tile"))
    return jax.shard_map(shards, mesh=mesh, in_specs=in_specs, out_specs=out_specs, check_vma=False)
```

```python
import jax
import jax.numpy as jnp
from jax import lax
from jax.experimental import pallas as pl
from jax.experimental.pallas import tpu as pltpu
from jax.sharding import PartitionSpec as P

R = 20
AY = 16
AX = 32
FY = 320
FX = 640
STEPS = 2
SUBSTEPS = 2
NZ = 16
NX = 4
HALO = 48
HALF = 64
PAD = 8
TOP = PAD + HALO
ROWS = TOP + FY + HALO + PAD
COLS = FX + 2 * HALF
NL = COLS // 128
RIGHT = 40
LEFT = 51
CR = 24

VM = pl.BlockSpec(memory_space=pltpu.VMEM)
SM = pl.BlockSpec(memory_space=pltpu.SMEM)
ANY = pl.BlockSpec(memory_space=pl.ANY)
SMALL = pltpu.CompilerParams(vmem_limit_bytes=4 * 1024 * 1024)
LARGE = pltpu.CompilerParams(vmem_limit_bytes=12 * 1024 * 1024)


def lanes(shape):
    return lax.broadcasted_iota(jnp.int32, shape, 1)


def f32(*shape):
    return jax.ShapeDtypeStruct(shape, jnp.float32)


def thirds(x):
    high = x.astype(jnp.bfloat16)
    rest = x - high.astype(jnp.float32)
    middle = rest.astype(jnp.bfloat16)
    low = (rest - middle.astype(jnp.float32)).astype(jnp.bfloat16)
    return jnp.concatenate([high, middle, low], axis=0)


def exact_dot(x, onehot):
    n = x.shape[0]
    out = jnp.dot(thirds(x), onehot, preferred_element_type=jnp.float32)
    return out[:n] + out[n : 2 * n] + out[2 * n :]


def coarse_lane(fine):
    own = fine // R
    right = RIGHT + (fine - FX) // R
    left = LEFT - (COLS - 1 - fine) // R
    edge = jnp.where(fine < FX + 3 * R, right, jnp.where(fine >= COLS - 3 * R, left, -1))
    return jnp.where(fine < FX, own, edge)


def strips_kernel(level, fuel, active, after, to_left, to_right, left_level, right_level, left_fuel, right_fuel, arrived):
    first, last = pl.ds(0, 128), pl.ds(FX - 128, 128)
    moves = [
        pltpu.make_async_copy(source.at[:, part], buf, arrived.at[i])
        for i, (source, part, buf) in enumerate((
            (level, first, left_level), (fuel, first, left_fuel),
            (level, last, right_level), (fuel, last, right_fuel),
        ))
    ]
    for move in moves:
        move.start()
    for k in range(8):
        row = jnp.full((1, 128), flag_of(active, k), jnp.float32)
        to_left[FY + k : FY + k + 1, :] = row
        to_right[FY + k : FY + k + 1, :] = row
    lane = lanes((FY, 128))
    moves[0].wait()
    moves[1].wait()
    to_left[0:FY, :] = jnp.where(
        lane < HALF, left_level[...], pltpu.roll(left_fuel[...].astype(jnp.float32), HALF, 1)
    )
    moves[2].wait()
    moves[3].wait()
    to_right[0:FY, :] = jnp.where(
        lane >= HALF, right_level[...], pltpu.roll(right_fuel[...].astype(jnp.float32), HALF, 1)
    )


def strips(level, fuel, active, after):
    strip = pltpu.VMEM((FY, 128), jnp.float32)
    kinds = pltpu.VMEM((FY, 128), jnp.int32)
    return pl.pallas_call(
        strips_kernel,
        in_specs=[ANY, ANY, SM, ANY],
        out_specs=[VM, VM],
        out_shape=[f32(FY + 8, 128), f32(FY + 8, 128)],
        scratch_shapes=[strip, strip, kinds, kinds, pltpu.SemaphoreType.DMA((4,))],
        name="strips",
    )(level, fuel, active, after)


def flag_of(active, k):
    return (active[0, 0, min(k, STEPS * SUBSTEPS - 1)] > 0).astype(jnp.float32)


def blocks_kernel(wind, slots):
    parts = [wind[0, 0:8, :], wind[0, 8:16, :], wind[1, 0:8, :], wind[1, 8:16, :]]
    block = jnp.concatenate(parts, axis=1)
    for k in range(NX * NZ):
        slots[k] = block


def blocks_of(wind):
    return pl.pallas_call(
        blocks_kernel, in_specs=[VM], out_specs=VM, out_shape=f32(NX * NZ, 8, 128), name="blocks"
    )(wind)


def rows_kernel(
    level, fuel, from_left, from_right, blocks, owner, active, held, to_up, to_down,
):
    tile = lax.axis_index("tile")
    lane = lanes((HALO, 128))
    lane8 = lanes((8, 128))
    main = blocks[owner[0, tile]]
    left = blocks[owner[0, jnp.maximum(tile - 1, 0)]]
    right = blocks[owner[0, jnp.minimum(tile + 1, NX * NZ - 1)]]
    is_left = jnp.logical_and(lane8 >= LEFT - 2, lane8 <= LEFT)
    is_right = jnp.logical_and(lane8 >= RIGHT, lane8 <= RIGHT + 2)
    for q in range(4):
        own = pltpu.roll(main, (128 - 32 * q) % 128, 1)
        one = pltpu.roll(left, (LEFT - 31 - 32 * q) % 128, 1)
        two = pltpu.roll(right, (RIGHT - 32 * q) % 128, 1)
        held[8 * q : 8 * q + 8, :] = jnp.where(
            lane8 < AX, own, jnp.where(is_left, one, jnp.where(is_right, two, 0.0))
        )
    for k in range(8):
        held[2 * AY + k : 2 * AY + k + 1, :] = jnp.full((1, 128), flag_of(active, k), jnp.float32)
    for out, start, coarse in ((to_up, 0, 0), (to_down, FY - HALO, AY - 3)):
        out[0:HALO, 0:FX] = level[start : start + HALO, :]
        out[HALO : 2 * HALO, 0:FX] = fuel[start : start + HALO, :].astype(jnp.float32)
        one = from_left[start : start + HALO, :]
        two = from_right[start : start + HALO, :]
        out[0:HALO, FX:COLS] = jnp.where(lane < HALF, two, one)
        out[HALO : 2 * HALO, FX:COLS] = pltpu.roll(jnp.where(lane < HALF, one, two), HALF, 1)
        for k in range(4):
            row = 2 * HALO + k
            out[row : row + 1, 0:FX] = jnp.full((1, FX), flag_of(active, k), jnp.float32)
            out[row : row + 1, FX:COLS] = jnp.where(
                lane[0:1] < HALF, from_right[FY + k : FY + k + 1, :], from_left[FY + k : FY + k + 1, :]
            )
        row = 2 * HALO + 4
        for c in range(6):
            at = (c // 3) * AY + coarse + c % 3
            out[row : row + 1, 128 * c : 128 * c + 128] = held[at : at + 1, :]
        out[row + 1 : row + 4, :] = jnp.zeros((3, COLS), jnp.float32)


def rows(level, fuel, from_left, from_right, blocks, owner, active):
    shape = (2 * HALO + 8, COLS)
    return pl.pallas_call(
        rows_kernel,
        in_specs=[VM] * 5 + [SM, SM],
        out_specs=[VM, VM, VM],
        out_shape=[f32(2 * AY + 8, 128), f32(*shape), f32(*shape)],
        compiler_params=SMALL,
        name="rows",
    )(level, fuel, from_left, from_right, blocks, owner, active)


def table(values):
    lane = lanes((8, 128))
    row = jnp.zeros((8, 128), jnp.float32)
    for c in range(values.shape[0]):
        row = jnp.where(lane == c, values[c], row)
    return row


def look(row, kinds):
    return jnp.take_along_axis(row, kinds, axis=1, mode="promise_in_bounds")


def values_kernel(
    fuel, from_left, from_right, after, fuel_rate, fuel_wind, fuel_heat, rate, drift, heat, three
):
    lane8 = lanes((8, 128))
    tables = [(table(fuel_rate), rate), (table(fuel_wind), drift), (table(fuel_heat), heat)]
    for i in range(3):
        three[8 * i : 8 * i + 8, :] = tables[i][0]

    def own_rows(i, _):
        at = pl.multiple_of(i * 8, 8)
        one = from_left[pl.ds(at, 8), :]
        two = from_right[pl.ds(at, 8), :]
        beside = pltpu.roll(jnp.where(lane8 < HALF, one, two), HALF, 1).astype(jnp.int32)
        for c in range(NL):
            kinds = beside if c == NL - 1 else fuel[pl.ds(at, 8), 128 * c : 128 * c + 128]
            for row, out in tables:
                out[pl.ds(at, 8), 128 * c : 128 * c + 128] = look(row, kinds)
        return 0

    lax.fori_loop(0, FY // 8, own_rows, 0, unroll=4)


def values(fuel, from_left, from_right, after, *names):
    return pl.pallas_call(
        values_kernel,
        in_specs=[VM, VM, VM, ANY, SM, SM, SM],
        out_specs=[VM] * 4,
        out_shape=[f32(FY, COLS)] * 3 + [f32(24, 128)],
        compiler_params=SMALL,
        name="values",
    )(fuel, from_left, from_right, after, *names)


def slab_kernel(
    level, from_left, from_right, from_up, from_down, held, rate, drift, heat, three,
    level_out, slots,
    phi_a, phi_b, phi_c, edge_rate, edge_drift, edge_heat, east, north, winds, gates, sums, spread, gather,
):
    group = lax.axis_index("grp")
    tile = lax.axis_index("tile")
    first_row = group == 0
    last_row = group == lax.axis_size("grp") - 1
    first_col = tile == 0
    last_col = tile == lax.axis_size("tile") - 1
    lane8 = lanes((8, 128))
    sub8 = lax.broadcasted_iota(jnp.int32, (8, COLS), 0)

    zero = jnp.zeros((PAD, COLS), jnp.float32)
    phi_a[0:PAD, :] = zero
    phi_a[ROWS - PAD : ROWS, :] = zero
    phi_a[TOP - HALO : TOP, :] = from_up[0:HALO, :]
    phi_a[TOP + FY : TOP + FY + HALO, :] = from_down[0:HALO, :]

    def own_rows(i, _):
        at = pl.multiple_of(i * 8, 8)
        to = pl.multiple_of(i * 8 + TOP, 8)
        phi_a[pl.ds(to, 8), 0:FX] = level[pl.ds(at, 8), :]
        one = from_left[pl.ds(at, 8), :]
        two = from_right[pl.ds(at, 8), :]
        phi_a[pl.ds(to, 8), FX:COLS] = jnp.where(lane8 < HALF, two, one)
        return 0

    lax.fori_loop(0, FY // 8, own_rows, 0, unroll=4)
    tables = [
        (three[8 * i : 8 * i + 8, :], out) for i, out in enumerate((edge_rate, edge_drift, edge_heat))
    ]

    def halo_rows(i, _):
        at = pl.multiple_of(i * 8, 8)
        for source, start in ((from_up, 0), (from_down, HALO)):
            to = pl.multiple_of(at + start, 8)
            for c in range(NL):
                kinds = source[pl.ds(pl.multiple_of(at + HALO, 8), 8), 128 * c : 128 * c + 128]
                kinds = kinds.astype(jnp.int32)
                for row, out in tables:
                    out[pl.ds(to, 8), 128 * c : 128 * c + 128] = look(row, kinds)
        return 0

    lax.fori_loop(0, HALO // 8, halo_rows, 0, unroll=3)

    gates[0:8, :] = from_up[2 * HALO : 2 * HALO + 8, :]
    gates[16:24, :] = from_down[2 * HALO : 2 * HALO + 8, :]
    for c in range(FX // 128):
        gates[8:16, 128 * c : 128 * c + 128] = held[2 * AY : 2 * AY + 8, :]
    gates[8:16, FX:COLS] = jnp.where(
        lane8 < HALF, from_right[FY : FY + 8, :], from_left[FY : FY + 8, :]
    )

    row = 2 * HALO + 4
    for comp in range(2):
        base = comp * CR
        for c in range(3):
            at = 128 * (3 * comp + c)
            winds[base + c : base + c + 1, :] = from_up[row : row + 1, at : at + 128]
            below = base + 3 + AY + c
            winds[below : below + 1, :] = from_down[row : row + 1, at : at + 128]
        winds[base + 3 : base + 3 + AY, :] = held[AY * comp : AY * comp + AY, :]
        winds[base + 6 + AY : base + CR, :] = jnp.zeros((CR - 6 - AY, 128), jnp.float32)

    spread[...] = (
        coarse_lane(lanes((128, COLS))) == lax.broadcasted_iota(jnp.int32, (128, COLS), 0)
    ).astype(jnp.bfloat16)
    gather[...] = (
        coarse_lane(lax.broadcasted_iota(jnp.int32, (COLS, 128), 0)) == lanes((COLS, 128))
    ).astype(jnp.bfloat16)

    def expand():
        wide = exact_dot(winds[...], spread[...])
        for comp, out in ((0, east), (1, north)):
            part = wide[comp * CR : comp * CR + CR]
            out[0:CR, :] = jnp.maximum(part, 0.0)
            out[CR : 2 * CR, :] = jnp.minimum(part, 0.0)

    def edges(phi):
        @pl.when(first_row)
        def _():
            phi[TOP - 1 : TOP, :] = phi[TOP : TOP + 1, :]

        @pl.when(last_row)
        def _():
            phi[TOP + FY : TOP + FY + 1, :] = phi[TOP + FY - 1 : TOP + FY, :]

        @pl.when(first_col)
        def _():
            old = phi[:, COLS - 128 : COLS]
            new = jnp.broadcast_to(phi[:, 0:1], (ROWS, 128))
            phi[:, COLS - 128 : COLS] = jnp.where(lanes((ROWS, 128)) == 127, new, old)

        @pl.when(last_col)
        def _():
            old = phi[:, FX : FX + 128]
            new = jnp.broadcast_to(phi[:, FX - 1 : FX], (ROWS, 128))
            phi[:, FX : FX + 128] = jnp.where(lanes((ROWS, 128)) == 0, new, old)

    own = (rate, drift, heat, TOP)
    upper_edge = (edge_rate, edge_drift, edge_heat, TOP - HALO)
    lower_edge = (edge_rate, edge_drift, edge_heat, TOP + FY - HALO)

    def update(phi, at, e, n, gate, fuels):
        before = phi[pl.ds(pl.multiple_of(at - 8, 8), 8), :]
        now = phi[pl.ds(at, 8), :]
        after = phi[pl.ds(pl.multiple_of(at + 8, 8), 8), :]
        south = jnp.where(sub8 == 0, pltpu.roll(before, 1, 0), pltpu.roll(now, 1, 0))
        above = jnp.where(sub8 == 7, pltpu.roll(after, 7, 0), pltpu.roll(now, 7, 0))
        west = pltpu.roll(now, 1, 1)
        east_cell = pltpu.roll(now, COLS - 1, 1)
        back_x = now - west
        ahead_x = east_cell - now
        back_y = now - south
        ahead_y = above - now
        bx = jnp.maximum(back_x, 0.0)
        ax = jnp.minimum(ahead_x, 0.0)
        by = jnp.maximum(back_y, 0.0)
        ay = jnp.minimum(ahead_y, 0.0)
        square = bx * bx + ax * ax + by * by + ay * ay + 1e-12
        slope = square * lax.rsqrt(square)
        carry = e[0] * back_x + e[1] * ahead_x + n[0] * back_y + n[1] * ahead_y
        there = pl.multiple_of(at - fuels[3], 8)
        change = fuels[0][pl.ds(there, 8), :] * slope + fuels[1][pl.ds(there, 8), :] * carry
        return now - gate * change

    def wind_row(ref, row):
        return tuple(jnp.broadcast_to(ref[pl.ds(row + part, 1), :], (8, COLS)) for part in (0, CR))

    def mix(a, b):
        return tuple(jnp.where(sub8 < 4, one, two) for one, two in zip(a, b))

    def band(phi, m, k, region, fuels, finish):
        at = pl.multiple_of(2 * PAD + 40 * m, 8)
        gate = jnp.broadcast_to(gates[region * 8 + k : region * 8 + k + 1, :], (8, COLS))
        row = 2 * m + 1
        for t in range(5):
            if t == 2:
                e = mix(wind_row(east, row), wind_row(east, row + 1))
                n = mix(wind_row(north, row), wind_row(north, row + 1))
            else:
                e, n = (wind_row(ref, row + t // 3) for ref in (east, north))
            here = pl.multiple_of(at + 8 * t, 8)
            finish(here, update(phi, here, e, n, gate, fuels), fuels)

    def tile_rows(phi, at, row, region, k, fuels):
        gate = jnp.broadcast_to(gates[region * 8 + k : region * 8 + k + 1, :], (8, COLS))
        return update(phi, at, wind_row(east, row), wind_row(north, row), gate, fuels)

    def own_bands(body):
        def step(m, _):
            body(m, 1, own)
            return 0

        lax.fori_loop(1, 9, step, 0)

    def store_to(out):
        def finish(here, new, fuels):
            out[pl.ds(here, 8), :] = new

        return finish

    def flux_band(before, phi, out, k):
        def body(m, region, fuels):
            parts = []

            def finish(here, new, fuels):
                if out is not None:
                    out[pl.ds(here, 8), :] = new
                else:
                    level_out[pl.ds(pl.multiple_of(here - TOP, 8), 8), :] = new[:, 0:FX]
                old = before[pl.ds(here, 8), :]
                there = pl.multiple_of(here - fuels[3], 8)
                parts.append(fuels[2][pl.ds(there, 8), :] * (jnp.tanh(old) - jnp.tanh(new)))

            band(phi, m, k, region, fuels, finish)
            low = parts[0] + parts[1] + jnp.where(sub8 < 4, parts[2], 0.0)
            high = parts[3] + parts[4] + jnp.where(sub8 >= 4, parts[2], 0.0)
            sums[pl.ds(2 * m + 1, 1), :] = jnp.sum(low, axis=0, keepdims=True)
            sums[pl.ds(2 * m + 2, 1), :] = jnp.sum(high, axis=0, keepdims=True)

        return body

    def pooled():
        return exact_dot(sums[...], gather[...]) * (0.5 / (R * R))

    lane_c = lanes((CR, 128))
    row_c = lax.broadcasted_iota(jnp.int32, (CR, 128), 0)
    sums[...] = jnp.zeros((CR, COLS), jnp.float32)

    expand()
    edges(phi_a)
    phi_b[PAD : PAD + 8, :] = tile_rows(phi_a, PAD, 0, 0, 0, upper_edge)
    phi_b[ROWS - 2 * PAD : ROWS - PAD, :] = tile_rows(phi_a, ROWS - 2 * PAD, AY + 5, 2, 0, lower_edge)
    band(phi_a, 0, 0, 0, upper_edge, store_to(phi_b))
    band(phi_a, 9, 0, 2, lower_edge, store_to(phi_b))
    own_bands(lambda m, region, fuels: band(phi_a, m, 0, region, fuels, store_to(phi_b)))
    edges(phi_b)
    second = flux_band(phi_a, phi_b, phi_c, 1)
    second(0, 0, upper_edge)
    second(9, 2, lower_edge)
    own_bands(second)
    edges(phi_c)

    flux0 = pooled()
    ahead = jnp.where(jnp.logical_or(lane_c == AX - 1, lane_c == LEFT), flux0, pltpu.roll(flux0, 127, 1))
    back = jnp.where(jnp.logical_or(lane_c == 0, lane_c == RIGHT), flux0, pltpu.roll(flux0, 1, 1))
    last_rows = jnp.logical_or(row_c == 2, row_c == AY + 2)
    first_rows = jnp.logical_or(row_c == 3, row_c == AY + 3)
    below = jnp.where(last_rows, flux0, pltpu.roll(flux0, CR - 1, 0))
    upper = jnp.where(first_rows, flux0, pltpu.roll(flux0, 1, 0))
    winds[0:CR, :] = 0.9 * winds[0:CR, :] + 20.0 * (ahead - back)
    winds[CR : 2 * CR, :] = 0.9 * winds[CR : 2 * CR, :] + 20.0 * (below - upper)
    expand()

    top = TOP - 8
    bottom = TOP + FY
    phi_b[top : top + 8, :] = tile_rows(phi_c, top, 2, 0, 2, upper_edge)
    phi_b[bottom : bottom + 8, :] = tile_rows(phi_c, bottom, AY + 3, 2, 2, lower_edge)
    own_bands(lambda m, region, fuels: band(phi_c, m, 2, region, fuels, store_to(phi_b)))
    edges(phi_b)
    own_bands(flux_band(phi_c, phi_b, None, 3))
    total = 0.9 * flux0 + pooled()

    packed = jnp.zeros((4, 128), jnp.float32)
    lane4 = lanes((4, 128))
    for q in range(4):
        moved = pltpu.roll(total, 32 * q, 1)[3 + 4 * q : 7 + 4 * q]
        packed = jnp.where(lane4 // AX == q, moved, packed)
    for k in range(NX * NZ):
        slots[k] = packed


def slab(*args):
    big = pltpu.VMEM((ROWS, COLS), jnp.float32)
    edge = pltpu.VMEM((2 * HALO, COLS), jnp.float32)
    return pl.pallas_call(
        slab_kernel,
        in_specs=[VM] * 10,
        out_specs=[VM, VM],
        out_shape=[f32(FY, FX), f32(NX * NZ, 4, 128)],
        scratch_shapes=[big] * 3
        + [edge] * 3
        + [
            pltpu.VMEM((2 * CR, COLS), jnp.float32),
            pltpu.VMEM((2 * CR, COLS), jnp.float32),
            pltpu.VMEM((2 * CR, 128), jnp.float32),
            pltpu.VMEM((CR, COLS), jnp.float32),
            pltpu.VMEM((CR, COLS), jnp.float32),
            pltpu.VMEM((128, COLS), jnp.bfloat16),
            pltpu.VMEM((COLS, 128), jnp.bfloat16),
        ],
        compiler_params=LARGE,
        name="slab",
    )(*args)


def final_kernel(owner, received, wind, wind_out):
    tile = lax.axis_index("tile")
    source = jnp.int32(0)
    for t in range(NX * NZ):
        source = jnp.where(owner[0, t] == tile, t, source)
    block = received[source]
    flux = jnp.concatenate([pltpu.roll(block, (128 - 32 * q) % 128, 1) for q in range(4)], axis=0)
    lane = lanes((AY, 128))
    row = lax.broadcasted_iota(jnp.int32, (AY, 128), 0)
    ahead = jnp.where(lane == AX - 1, flux, pltpu.roll(flux, 127, 1))
    back = jnp.where(lane == 0, flux, pltpu.roll(flux, 1, 1))
    below = jnp.where(row == AY - 1, flux, pltpu.roll(flux, AY - 1, 0))
    upper = jnp.where(row == 0, flux, pltpu.roll(flux, 1, 0))
    wind_out[0] = 0.81 * wind[0] + 20.0 * (ahead - back)[:, 0:AX]
    wind_out[1] = 0.81 * wind[1] + 20.0 * (below - upper)[:, 0:AX]


def final(owner, received, wind):
    return pl.pallas_call(
        final_kernel, in_specs=[SM, VM, VM], out_specs=VM, out_shape=f32(2, AY, AX),
        compiler_params=SMALL, name="final"
    )(owner, received, wind)


def shift(value, axis, step):
    size = lax.axis_size(axis)
    pairs = [(i, i + step) for i in range(size) if 0 <= i + step < size]
    return lax.ppermute(value, axis, pairs)


def shards(level, fuel, wind, owner, active, fuel_rate, fuel_wind, fuel_heat):
    active = jnp.transpose(active, (1, 2, 0))
    mine = blocks_of(wind)
    blocks = lax.all_to_all(mine, "tile", 0, 0, tiled=True)
    to_left, to_right = strips(level, fuel, active, mine)
    from_right = shift(to_left, "tile", -1)
    from_left = shift(to_right, "tile", 1)
    held, to_up, to_down = rows(level, fuel, from_left, from_right, blocks, owner, active)
    from_down = shift(to_up, "grp", -1)
    from_up = shift(to_down, "grp", 1)
    coefficients = values(fuel, from_left, from_right, held, fuel_rate, fuel_wind, fuel_heat)
    level_out, flux = slab(level, from_left, from_right, from_up, from_down, held, *coefficients)
    flux = lax.all_to_all(flux, "tile", 0, 0, tiled=True)
    return (level_out, final(owner, flux, wind))


def solution(mesh):
    in_specs = (
        P("grp", "tile"),
        P("grp", "tile"),
        P(None, "grp", "tile"),
        P("grp", None),
        P(None, "grp", "tile"),
        P(),
        P(),
        P(),
    )
    out_specs = (P("grp", "tile"), P(None, "grp", "tile"))
    return jax.shard_map(shards, mesh=mesh, in_specs=in_specs, out_specs=out_specs, check_vma=False)
```

```python
import jax
import jax.numpy as jnp
from jax import lax
from jax.experimental import pallas as pl
from jax.experimental.pallas import tpu as pltpu
from jax.sharding import PartitionSpec as P

R = 20
AY = 16
AX = 32
FY = 320
FX = 640
STEPS = 2
SUBSTEPS = 2
NZ = 16
NX = 4
HALO = 48
HALF = 64
PAD = 8
TOP = PAD + HALO
ROWS = TOP + FY + HALO + PAD
COLS = FX + 2 * HALF
NL = COLS // 128
RIGHT = 40
LEFT = 51
CR = 24

VM = pl.BlockSpec(memory_space=pltpu.VMEM)
SM = pl.BlockSpec(memory_space=pltpu.SMEM)
ANY = pl.BlockSpec(memory_space=pl.ANY)
SMALL = pltpu.CompilerParams(vmem_limit_bytes=4 * 1024 * 1024)
LARGE = pltpu.CompilerParams(vmem_limit_bytes=12 * 1024 * 1024)


def lanes(shape):
    return lax.broadcasted_iota(jnp.int32, shape, 1)


def f32(*shape):
    return jax.ShapeDtypeStruct(shape, jnp.float32)


def thirds(x):
    high = x.astype(jnp.bfloat16)
    rest = x - high.astype(jnp.float32)
    middle = rest.astype(jnp.bfloat16)
    low = (rest - middle.astype(jnp.float32)).astype(jnp.bfloat16)
    return jnp.concatenate([high, middle, low], axis=0)


def exact_dot(x, onehot):
    n = x.shape[0]
    out = jnp.dot(thirds(x), onehot, preferred_element_type=jnp.float32)
    return out[:n] + out[n : 2 * n] + out[2 * n :]


def coarse_lane(fine):
    own = fine // R
    right = RIGHT + (fine - FX) // R
    left = LEFT - (COLS - 1 - fine) // R
    edge = jnp.where(fine < FX + 3 * R, right, jnp.where(fine >= COLS - 3 * R, left, -1))
    return jnp.where(fine < FX, own, edge)


def strips_kernel(level, fuel, active, after, to_left, to_right, left_level, right_level, left_fuel, right_fuel, arrived):
    first, last = pl.ds(0, 128), pl.ds(FX - 128, 128)
    moves = [
        pltpu.make_async_copy(source.at[:, part], buf, arrived.at[i])
        for i, (source, part, buf) in enumerate((
            (level, first, left_level), (fuel, first, left_fuel),
            (level, last, right_level), (fuel, last, right_fuel),
        ))
    ]
    for move in moves:
        move.start()
    for k in range(8):
        row = jnp.full((1, 128), flag_of(active, k), jnp.float32)
        to_left[FY + k : FY + k + 1, :] = row
        to_right[FY + k : FY + k + 1, :] = row
    lane = lanes((FY, 128))
    moves[0].wait()
    moves[1].wait()
    to_left[0:FY, :] = jnp.where(
        lane < HALF, left_level[...], pltpu.roll(left_fuel[...].astype(jnp.float32), HALF, 1)
    )
    moves[2].wait()
    moves[3].wait()
    to_right[0:FY, :] = jnp.where(
        lane >= HALF, right_level[...], pltpu.roll(right_fuel[...].astype(jnp.float32), HALF, 1)
    )


def strips(level, fuel, active, after):
    strip = pltpu.VMEM((FY, 128), jnp.float32)
    kinds = pltpu.VMEM((FY, 128), jnp.int32)
    return pl.pallas_call(
        strips_kernel,
        in_specs=[ANY, ANY, SM, ANY],
        out_specs=[VM, VM],
        out_shape=[f32(FY + 8, 128), f32(FY + 8, 128)],
        scratch_shapes=[strip, strip, kinds, kinds, pltpu.SemaphoreType.DMA((4,))],
        name="strips",
    )(level, fuel, active, after)


def flag_of(active, k):
    return (active[0, 0, min(k, STEPS * SUBSTEPS - 1)] > 0).astype(jnp.float32)


def blocks_kernel(wind, slots):
    parts = [wind[0, 0:8, :], wind[0, 8:16, :], wind[1, 0:8, :], wind[1, 8:16, :]]
    block = jnp.concatenate(parts, axis=1)
    for k in range(NX * NZ):
        slots[k] = block


def blocks_of(wind):
    return pl.pallas_call(
        blocks_kernel, in_specs=[VM], out_specs=VM, out_shape=f32(NX * NZ, 8, 128), name="blocks"
    )(wind)


def rows_kernel(
    level, fuel, from_left, from_right, blocks, owner, active, held, to_up, to_down,
):
    tile = lax.axis_index("tile")
    lane = lanes((HALO, 128))
    lane8 = lanes((8, 128))
    main = blocks[owner[0, tile]]
    left = blocks[owner[0, jnp.maximum(tile - 1, 0)]]
    right = blocks[owner[0, jnp.minimum(tile + 1, NX * NZ - 1)]]
    is_left = jnp.logical_and(lane8 >= LEFT - 2, lane8 <= LEFT)
    is_right = jnp.logical_and(lane8 >= RIGHT, lane8 <= RIGHT + 2)
    for q in range(4):
        own = pltpu.roll(main, (128 - 32 * q) % 128, 1)
        one = pltpu.roll(left, (LEFT - 31 - 32 * q) % 128, 1)
        two = pltpu.roll(right, (RIGHT - 32 * q) % 128, 1)
        held[8 * q : 8 * q + 8, :] = jnp.where(
            lane8 < AX, own, jnp.where(is_left, one, jnp.where(is_right, two, 0.0))
        )
    for k in range(8):
        held[2 * AY + k : 2 * AY + k + 1, :] = jnp.full((1, 128), flag_of(active, k), jnp.float32)
    for out, start, coarse in ((to_up, 0, 0), (to_down, FY - HALO, AY - 3)):
        out[0:HALO, 0:FX] = level[start : start + HALO, :]
        out[HALO : 2 * HALO, 0:FX] = fuel[start : start + HALO, :].astype(jnp.float32)
        one = from_left[start : start + HALO, :]
        two = from_right[start : start + HALO, :]
        out[0:HALO, FX:COLS] = jnp.where(lane < HALF, two, one)
        out[HALO : 2 * HALO, FX:COLS] = pltpu.roll(jnp.where(lane < HALF, one, two), HALF, 1)
        for k in range(4):
            row = 2 * HALO + k
            out[row : row + 1, 0:FX] = jnp.full((1, FX), flag_of(active, k), jnp.float32)
            out[row : row + 1, FX:COLS] = jnp.where(
                lane[0:1] < HALF, from_right[FY + k : FY + k + 1, :], from_left[FY + k : FY + k + 1, :]
            )
        row = 2 * HALO + 4
        for c in range(6):
            at = (c // 3) * AY + coarse + c % 3
            out[row : row + 1, 128 * c : 128 * c + 128] = held[at : at + 1, :]
        out[row + 1 : row + 4, :] = jnp.zeros((3, COLS), jnp.float32)


def rows(level, fuel, from_left, from_right, blocks, owner, active):
    shape = (2 * HALO + 8, COLS)
    return pl.pallas_call(
        rows_kernel,
        in_specs=[VM] * 5 + [SM, SM],
        out_specs=[VM, VM, VM],
        out_shape=[f32(2 * AY + 8, 128), f32(*shape), f32(*shape)],
        compiler_params=SMALL,
        name="rows",
    )(level, fuel, from_left, from_right, blocks, owner, active)


def table(values):
    lane = lanes((8, 128))
    row = jnp.zeros((8, 128), jnp.float32)
    for c in range(values.shape[0]):
        row = jnp.where(lane == c, values[c], row)
    return row


def look(row, kinds):
    return jnp.take_along_axis(row, kinds, axis=1, mode="promise_in_bounds")


def values_kernel(
    fuel, from_left, from_right, after, fuel_rate, fuel_wind, fuel_heat, rate, drift, heat, three
):
    lane8 = lanes((8, 128))
    tables = [(table(fuel_rate), rate), (table(fuel_wind), drift), (table(fuel_heat), heat)]
    for i in range(3):
        three[8 * i : 8 * i + 8, :] = tables[i][0]

    def own_rows(i, _):
        at = pl.multiple_of(i * 8, 8)
        one = from_left[pl.ds(at, 8), :]
        two = from_right[pl.ds(at, 8), :]
        beside = pltpu.roll(jnp.where(lane8 < HALF, one, two), HALF, 1).astype(jnp.int32)
        for c in range(NL):
            kinds = beside if c == NL - 1 else fuel[pl.ds(at, 8), 128 * c : 128 * c + 128]
            for row, out in tables:
                out[pl.ds(at, 8), 128 * c : 128 * c + 128] = look(row, kinds)
        return 0

    lax.fori_loop(0, FY // 8, own_rows, 0, unroll=4)


def values(fuel, from_left, from_right, after, *names):
    return pl.pallas_call(
        values_kernel,
        in_specs=[VM, VM, VM, ANY, SM, SM, SM],
        out_specs=[VM] * 4,
        out_shape=[f32(FY, COLS)] * 3 + [f32(24, 128)],
        compiler_params=SMALL,
        name="values",
    )(fuel, from_left, from_right, after, *names)


def slab_kernel(
    level, from_left, from_right, from_up, from_down, held, rate, drift, heat, three,
    level_out, slots,
    phi_a, phi_b, phi_c, edge_rate, edge_drift, edge_heat, east, north, winds, gates, sums, spread, gather,
):
    group = lax.axis_index("grp")
    tile = lax.axis_index("tile")
    first_row = group == 0
    last_row = group == lax.axis_size("grp") - 1
    first_col = tile == 0
    last_col = tile == lax.axis_size("tile") - 1
    lane8 = lanes((8, 128))
    sub8 = lax.broadcasted_iota(jnp.int32, (8, COLS), 0)

    zero = jnp.zeros((PAD, COLS), jnp.float32)
    phi_a[0:PAD, :] = zero
    phi_a[ROWS - PAD : ROWS, :] = zero
    phi_a[TOP - HALO : TOP, :] = from_up[0:HALO, :]
    phi_a[TOP + FY : TOP + FY + HALO, :] = from_down[0:HALO, :]

    def own_rows(i, _):
        at = pl.multiple_of(i * 8, 8)
        to = pl.multiple_of(i * 8 + TOP, 8)
        phi_a[pl.ds(to, 8), 0:FX] = level[pl.ds(at, 8), :]
        one = from_left[pl.ds(at, 8), :]
        two = from_right[pl.ds(at, 8), :]
        phi_a[pl.ds(to, 8), FX:COLS] = jnp.where(lane8 < HALF, two, one)
        return 0

    lax.fori_loop(0, FY // 8, own_rows, 0, unroll=4)
    tables = [
        (three[8 * i : 8 * i + 8, :], out) for i, out in enumerate((edge_rate, edge_drift, edge_heat))
    ]

    def halo_rows(i, _):
        at = pl.multiple_of(i * 8, 8)
        for source, start in ((from_up, 0), (from_down, HALO)):
            to = pl.multiple_of(at + start, 8)
            for c in range(NL):
                kinds = source[pl.ds(pl.multiple_of(at + HALO, 8), 8), 128 * c : 128 * c + 128]
                kinds = kinds.astype(jnp.int32)
                for row, out in tables:
                    out[pl.ds(to, 8), 128 * c : 128 * c + 128] = look(row, kinds)
        return 0

    lax.fori_loop(0, HALO // 8, halo_rows, 0, unroll=6)

    gates[0:8, :] = from_up[2 * HALO : 2 * HALO + 8, :]
    gates[16:24, :] = from_down[2 * HALO : 2 * HALO + 8, :]
    for c in range(FX // 128):
        gates[8:16, 128 * c : 128 * c + 128] = held[2 * AY : 2 * AY + 8, :]
    gates[8:16, FX:COLS] = jnp.where(
        lane8 < HALF, from_right[FY : FY + 8, :], from_left[FY : FY + 8, :]
    )

    row = 2 * HALO + 4
    for comp in range(2):
        base = comp * CR
        for c in range(3):
            at = 128 * (3 * comp + c)
            winds[base + c : base + c + 1, :] = from_up[row : row + 1, at : at + 128]
            below = base + 3 + AY + c
            winds[below : below + 1, :] = from_down[row : row + 1, at : at + 128]
        winds[base + 3 : base + 3 + AY, :] = held[AY * comp : AY * comp + AY, :]
        winds[base + 6 + AY : base + CR, :] = jnp.zeros((CR - 6 - AY, 128), jnp.float32)

    spread[...] = (
        coarse_lane(lanes((128, COLS))) == lax.broadcasted_iota(jnp.int32, (128, COLS), 0)
    ).astype(jnp.bfloat16)
    gather[...] = (
        coarse_lane(lax.broadcasted_iota(jnp.int32, (COLS, 128), 0)) == lanes((COLS, 128))
    ).astype(jnp.bfloat16)

    def expand():
        wide = exact_dot(winds[...], spread[...])
        east[...] = wide[0:CR]
        north[...] = wide[CR : 2 * CR]

    def edges(phi):
        @pl.when(first_row)
        def _():
            phi[TOP - 1 : TOP, :] = phi[TOP : TOP + 1, :]

        @pl.when(last_row)
        def _():
            phi[TOP + FY : TOP + FY + 1, :] = phi[TOP + FY - 1 : TOP + FY, :]

        @pl.when(first_col)
        def _():
            old = phi[:, COLS - 128 : COLS]
            new = jnp.broadcast_to(phi[:, 0:1], (ROWS, 128))
            phi[:, COLS - 128 : COLS] = jnp.where(lanes((ROWS, 128)) == 127, new, old)

        @pl.when(last_col)
        def _():
            old = phi[:, FX : FX + 128]
            new = jnp.broadcast_to(phi[:, FX - 1 : FX], (ROWS, 128))
            phi[:, FX : FX + 128] = jnp.where(lanes((ROWS, 128)) == 0, new, old)

    own = (rate, drift, heat, TOP)
    upper_edge = (edge_rate, edge_drift, edge_heat, TOP - HALO)
    lower_edge = (edge_rate, edge_drift, edge_heat, TOP + FY - HALO)

    def update(phi, at, e, n, gate, fuels):
        before = phi[pl.ds(pl.multiple_of(at - 8, 8), 8), :]
        now = phi[pl.ds(at, 8), :]
        after = phi[pl.ds(pl.multiple_of(at + 8, 8), 8), :]
        south = jnp.where(sub8 == 0, pltpu.roll(before, 1, 0), pltpu.roll(now, 1, 0))
        above = jnp.where(sub8 == 7, pltpu.roll(after, 7, 0), pltpu.roll(now, 7, 0))
        west = pltpu.roll(now, 1, 1)
        east_cell = pltpu.roll(now, COLS - 1, 1)
        back_x = now - west
        ahead_x = east_cell - now
        back_y = now - south
        ahead_y = above - now
        bx = jnp.maximum(back_x, 0.0)
        ax = jnp.minimum(ahead_x, 0.0)
        by = jnp.maximum(back_y, 0.0)
        ay = jnp.minimum(ahead_y, 0.0)
        square = bx * bx + ax * ax + by * by + ay * ay + 1e-12
        slope = square * lax.rsqrt(square)
        carry = e * jnp.where(e > 0.0, back_x, ahead_x) + n * jnp.where(n > 0.0, back_y, ahead_y)
        there = pl.multiple_of(at - fuels[3], 8)
        change = fuels[0][pl.ds(there, 8), :] * slope + fuels[1][pl.ds(there, 8), :] * carry
        return now - gate * change

    def wind_row(ref, row):
        return jnp.broadcast_to(ref[pl.ds(row, 1), :], (8, COLS))

    def mix(a, b):
        return jnp.where(sub8 < 4, a, b)

    def band(phi, m, k, region, fuels, finish):
        at = pl.multiple_of(2 * PAD + 40 * m, 8)
        gate = jnp.broadcast_to(gates[region * 8 + k : region * 8 + k + 1, :], (8, COLS))
        row = 2 * m + 1
        for t in range(5):
            if t == 2:
                e = mix(wind_row(east, row), wind_row(east, row + 1))
                n = mix(wind_row(north, row), wind_row(north, row + 1))
            else:
                e, n = (wind_row(ref, row + t // 3) for ref in (east, north))
            here = pl.multiple_of(at + 8 * t, 8)
            finish(here, update(phi, here, e, n, gate, fuels), fuels)

    def tile_rows(phi, at, row, region, k, fuels):
        gate = jnp.broadcast_to(gates[region * 8 + k : region * 8 + k + 1, :], (8, COLS))
        return update(phi, at, wind_row(east, row), wind_row(north, row), gate, fuels)

    def own_bands(body):
        def step(m, _):
            body(m, 1, own)
            return 0

        lax.fori_loop(1, 9, step, 0, unroll=8)

    def store_to(out):
        def finish(here, new, fuels):
            out[pl.ds(here, 8), :] = new

        return finish

    def flux_band(before, phi, out, k):
        def body(m, region, fuels):
            parts = []

            def finish(here, new, fuels):
                if out is not None:
                    out[pl.ds(here, 8), :] = new
                else:
                    level_out[pl.ds(pl.multiple_of(here - TOP, 8), 8), :] = new[:, 0:FX]
                old = before[pl.ds(here, 8), :]
                there = pl.multiple_of(here - fuels[3], 8)
                parts.append(fuels[2][pl.ds(there, 8), :] * (jnp.tanh(old) - jnp.tanh(new)))

            band(phi, m, k, region, fuels, finish)
            low = parts[0] + parts[1] + jnp.where(sub8 < 4, parts[2], 0.0)
            high = parts[3] + parts[4] + jnp.where(sub8 >= 4, parts[2], 0.0)
            sums[pl.ds(2 * m + 1, 1), :] = jnp.sum(low, axis=0, keepdims=True)
            sums[pl.ds(2 * m + 2, 1), :] = jnp.sum(high, axis=0, keepdims=True)

        return body

    def pooled():
        return exact_dot(sums[...], gather[...]) * (0.5 / (R * R))

    lane_c = lanes((CR, 128))
    row_c = lax.broadcasted_iota(jnp.int32, (CR, 128), 0)
    sums[...] = jnp.zeros((CR, COLS), jnp.float32)

    expand()
    edges(phi_a)
    phi_b[PAD : PAD + 8, :] = tile_rows(phi_a, PAD, 0, 0, 0, upper_edge)
    phi_b[ROWS - 2 * PAD : ROWS - PAD, :] = tile_rows(phi_a, ROWS - 2 * PAD, AY + 5, 2, 0, lower_edge)
    band(phi_a, 0, 0, 0, upper_edge, store_to(phi_b))
    band(phi_a, 9, 0, 2, lower_edge, store_to(phi_b))
    own_bands(lambda m, region, fuels: band(phi_a, m, 0, region, fuels, store_to(phi_b)))
    edges(phi_b)
    second = flux_band(phi_a, phi_b, phi_c, 1)
    second(0, 0, upper_edge)
    second(9, 2, lower_edge)
    own_bands(second)
    edges(phi_c)

    flux0 = pooled()
    ahead = jnp.where(jnp.logical_or(lane_c == AX - 1, lane_c == LEFT), flux0, pltpu.roll(flux0, 127, 1))
    back = jnp.where(jnp.logical_or(lane_c == 0, lane_c == RIGHT), flux0, pltpu.roll(flux0, 1, 1))
    last_rows = jnp.logical_or(row_c == 2, row_c == AY + 2)
    first_rows = jnp.logical_or(row_c == 3, row_c == AY + 3)
    below = jnp.where(last_rows, flux0, pltpu.roll(flux0, CR - 1, 0))
    upper = jnp.where(first_rows, flux0, pltpu.roll(flux0, 1, 0))
    winds[0:CR, :] = 0.9 * winds[0:CR, :] + 20.0 * (ahead - back)
    winds[CR : 2 * CR, :] = 0.9 * winds[CR : 2 * CR, :] + 20.0 * (below - upper)
    expand()

    top = TOP - 8
    bottom = TOP + FY
    phi_b[top : top + 8, :] = tile_rows(phi_c, top, 2, 0, 2, upper_edge)
    phi_b[bottom : bottom + 8, :] = tile_rows(phi_c, bottom, AY + 3, 2, 2, lower_edge)
    own_bands(lambda m, region, fuels: band(phi_c, m, 2, region, fuels, store_to(phi_b)))
    edges(phi_b)
    own_bands(flux_band(phi_c, phi_b, None, 3))
    total = 0.9 * flux0 + pooled()

    packed = jnp.zeros((4, 128), jnp.float32)
    lane4 = lanes((4, 128))
    for q in range(4):
        moved = pltpu.roll(total, 32 * q, 1)[3 + 4 * q : 7 + 4 * q]
        packed = jnp.where(lane4 // AX == q, moved, packed)
    for k in range(NX * NZ):
        slots[k] = packed


def slab(*args):
    big = pltpu.VMEM((ROWS, COLS), jnp.float32)
    edge = pltpu.VMEM((2 * HALO, COLS), jnp.float32)
    return pl.pallas_call(
        slab_kernel,
        in_specs=[VM] * 10,
        out_specs=[VM, VM],
        out_shape=[f32(FY, FX), f32(NX * NZ, 4, 128)],
        scratch_shapes=[big] * 3
        + [edge] * 3
        + [
            pltpu.VMEM((CR, COLS), jnp.float32),
            pltpu.VMEM((CR, COLS), jnp.float32),
            pltpu.VMEM((2 * CR, 128), jnp.float32),
            pltpu.VMEM((CR, COLS), jnp.float32),
            pltpu.VMEM((CR, COLS), jnp.float32),
            pltpu.VMEM((128, COLS), jnp.bfloat16),
            pltpu.VMEM((COLS, 128), jnp.bfloat16),
        ],
        compiler_params=LARGE,
        name="slab",
    )(*args)


def final_kernel(owner, received, wind, wind_out):
    tile = lax.axis_index("tile")
    source = jnp.int32(0)
    for t in range(NX * NZ):
        source = jnp.where(owner[0, t] == tile, t, source)
    block = received[source]
    flux = jnp.concatenate([pltpu.roll(block, (128 - 32 * q) % 128, 1) for q in range(4)], axis=0)
    lane = lanes((AY, 128))
    row = lax.broadcasted_iota(jnp.int32, (AY, 128), 0)
    ahead = jnp.where(lane == AX - 1, flux, pltpu.roll(flux, 127, 1))
    back = jnp.where(lane == 0, flux, pltpu.roll(flux, 1, 1))
    below = jnp.where(row == AY - 1, flux, pltpu.roll(flux, AY - 1, 0))
    upper = jnp.where(row == 0, flux, pltpu.roll(flux, 1, 0))
    wind_out[0] = 0.81 * wind[0] + 20.0 * (ahead - back)[:, 0:AX]
    wind_out[1] = 0.81 * wind[1] + 20.0 * (below - upper)[:, 0:AX]


def final(owner, received, wind):
    return pl.pallas_call(
        final_kernel, in_specs=[SM, VM, VM], out_specs=VM, out_shape=f32(2, AY, AX),
        compiler_params=SMALL, name="final"
    )(owner, received, wind)


def shift(value, axis, step):
    size = lax.axis_size(axis)
    pairs = [(i, i + step) for i in range(size) if 0 <= i + step < size]
    return lax.ppermute(value, axis, pairs)


def shards(level, fuel, wind, owner, active, fuel_rate, fuel_wind, fuel_heat):
    active = jnp.transpose(active, (1, 2, 0))
    mine = blocks_of(wind)
    blocks = lax.all_to_all(mine, "tile", 0, 0, tiled=True)
    to_left, to_right = strips(level, fuel, active, mine)
    from_right = shift(to_left, "tile", -1)
    from_left = shift(to_right, "tile", 1)
    held, to_up, to_down = rows(level, fuel, from_left, from_right, blocks, owner, active)
    from_down = shift(to_up, "grp", -1)
    from_up = shift(to_down, "grp", 1)
    coefficients = values(fuel, from_left, from_right, held, fuel_rate, fuel_wind, fuel_heat)
    level_out, flux = slab(level, from_left, from_right, from_up, from_down, held, *coefficients)
    flux = lax.all_to_all(flux, "tile", 0, 0, tiled=True)
    return (level_out, final(owner, flux, wind))


def solution(mesh):
    in_specs = (
        P("grp", "tile"),
        P("grp", "tile"),
        P(None, "grp", "tile"),
        P("grp", None),
        P(None, "grp", "tile"),
        P(),
        P(),
        P(),
    )
    out_specs = (P("grp", "tile"), P(None, "grp", "tile"))
    return jax.shard_map(shards, mesh=mesh, in_specs=in_specs, out_specs=out_specs, check_vma=False)
```

```python
import jax
import jax.numpy as jnp
from jax import lax
from jax.experimental import pallas as pl
from jax.experimental.pallas import tpu as pltpu
from jax.sharding import PartitionSpec as P

R = 20
AY = 16
AX = 32
FY = 320
FX = 640
STEPS = 2
SUBSTEPS = 2
NZ = 16
NX = 4
HALO = 48
HALF = 64
PAD = 8
TOP = PAD + HALO
ROWS = TOP + FY + HALO + PAD
COLS = FX + 2 * HALF
NL = COLS // 128
RIGHT = 40
LEFT = 51
CR = 24
BESIDE = 2 * HALO
OWN = BESIDE + 8
WIND = OWN + 8

VM = pl.BlockSpec(memory_space=pltpu.VMEM)
SM = pl.BlockSpec(memory_space=pltpu.SMEM)
ANY = pl.BlockSpec(memory_space=pl.ANY)
SMALL = pltpu.CompilerParams(vmem_limit_bytes=4 * 1024 * 1024)
LARGE = pltpu.CompilerParams(vmem_limit_bytes=12 * 1024 * 1024)


def lanes(shape):
    return lax.broadcasted_iota(jnp.int32, shape, 1)


def f32(*shape):
    return jax.ShapeDtypeStruct(shape, jnp.float32)


def thirds(x):
    high = x.astype(jnp.bfloat16)
    rest = x - high.astype(jnp.float32)
    middle = rest.astype(jnp.bfloat16)
    low = (rest - middle.astype(jnp.float32)).astype(jnp.bfloat16)
    return jnp.concatenate([high, middle, low], axis=0)


def exact_dot(x, onehot):
    n = x.shape[0]
    out = jnp.dot(thirds(x), onehot, preferred_element_type=jnp.float32)
    return out[:n] + out[n : 2 * n] + out[2 * n :]


def coarse_lane(fine):
    own = fine // R
    right = RIGHT + (fine - FX) // R
    left = LEFT - (COLS - 1 - fine) // R
    edge = jnp.where(fine < FX + 3 * R, right, jnp.where(fine >= COLS - 3 * R, left, -1))
    return jnp.where(fine < FX, own, edge)


def strips_kernel(
    level, fuel, active, after, to_left, to_right, to_up, to_down, done,
    left_level, right_level, left_fuel, right_fuel, up_fuel, down_fuel, arrived,
):
    first, last = (slice(None), pl.ds(0, 128)), (slice(None), pl.ds(FX - 128, 128))
    top, bottom = (pl.ds(0, HALO), slice(None)), (pl.ds(FY - HALO, HALO), slice(None))
    up_level, down_level = to_up.at[0:HALO, :], to_down.at[0:HALO, :]
    moves = [
        pltpu.make_async_copy(source.at[part], buf, arrived.at[i])
        for i, (source, part, buf) in enumerate((
            (level, first, left_level), (fuel, first, left_fuel),
            (level, last, right_level), (fuel, last, right_fuel),
            (level, top, up_level), (fuel, top, up_fuel),
            (level, bottom, down_level), (fuel, bottom, down_fuel),
        ))
    ]
    for move in moves:
        move.start()
    for k in range(8):
        row = jnp.full((1, 128), flag_of(active, k), jnp.float32)
        to_left[FY + k : FY + k + 1, :] = row
        to_right[FY + k : FY + k + 1, :] = row
    done[...] = jnp.zeros((8, 128), jnp.float32)
    lane = lanes((FY, 128))
    moves[0].wait()
    moves[1].wait()
    to_left[0:FY, :] = jnp.where(
        lane < HALF, left_level[...], pltpu.roll(left_fuel[...].astype(jnp.float32), HALF, 1)
    )
    moves[2].wait()
    moves[3].wait()
    to_right[0:FY, :] = jnp.where(
        lane >= HALF, right_level[...], pltpu.roll(right_fuel[...].astype(jnp.float32), HALF, 1)
    )
    for move in moves[4:]:
        move.wait()
    to_up[HALO : 2 * HALO, :] = up_fuel[...].astype(jnp.float32)
    to_down[HALO : 2 * HALO, :] = down_fuel[...].astype(jnp.float32)


def strips(level, fuel, active, after):
    strip = pltpu.VMEM((FY, 128), jnp.float32)
    kinds = pltpu.VMEM((FY, 128), jnp.int32)
    edge = pltpu.VMEM((HALO, FX), jnp.int32)
    return pl.pallas_call(
        strips_kernel,
        in_specs=[ANY, ANY, SM, ANY],
        out_specs=[VM] * 5,
        out_shape=[f32(FY + 8, 128)] * 2 + [f32(2 * HALO, FX)] * 2 + [f32(8, 128)],
        scratch_shapes=[strip, strip, kinds, kinds, edge, edge, pltpu.SemaphoreType.DMA((8,))],
        name="strips",
    )(level, fuel, active, after)


def flag_of(active, k):
    return (active[0, 0, min(k, STEPS * SUBSTEPS - 1)] > 0).astype(jnp.float32)


def blocks_kernel(wind, slots):
    parts = [wind[0, 0:8, :], wind[0, 8:16, :], wind[1, 0:8, :], wind[1, 8:16, :]]
    block = jnp.concatenate(parts, axis=1)
    for k in range(NX * NZ):
        slots[k] = block


def blocks_of(wind):
    return pl.pallas_call(
        blocks_kernel, in_specs=[VM], out_specs=VM, out_shape=f32(NX * NZ, 8, 128), name="blocks"
    )(wind)


def corners_kernel(from_left, from_right, blocks, owner, active, after, held, to_up, to_down):
    tile = lax.axis_index("tile")
    lane = lanes((HALO, 128))
    lane8 = lanes((8, 128))
    main = blocks[owner[0, tile]]
    left = blocks[owner[0, jnp.maximum(tile - 1, 0)]]
    right = blocks[owner[0, jnp.minimum(tile + 1, NX * NZ - 1)]]
    is_left = jnp.logical_and(lane8 >= LEFT - 2, lane8 <= LEFT)
    is_right = jnp.logical_and(lane8 >= RIGHT, lane8 <= RIGHT + 2)
    for q in range(4):
        own = pltpu.roll(main, (128 - 32 * q) % 128, 1)
        one = pltpu.roll(left, (LEFT - 31 - 32 * q) % 128, 1)
        two = pltpu.roll(right, (RIGHT - 32 * q) % 128, 1)
        held[8 * q : 8 * q + 8, :] = jnp.where(
            lane8 < AX, own, jnp.where(is_left, one, jnp.where(is_right, two, 0.0))
        )
    for k in range(8):
        held[2 * AY + k : 2 * AY + k + 1, :] = jnp.full((1, 128), flag_of(active, k), jnp.float32)
    for out, start, coarse in ((to_up, 0, 0), (to_down, FY - HALO, AY - 3)):
        one = from_left[start : start + HALO, :]
        two = from_right[start : start + HALO, :]
        out[0:HALO, :] = jnp.where(lane < HALF, two, one)
        out[HALO : 2 * HALO, :] = pltpu.roll(jnp.where(lane < HALF, one, two), HALF, 1)
        out[BESIDE : BESIDE + 8, :] = jnp.where(
            lane8 < HALF, from_right[FY : FY + 8, :], from_left[FY : FY + 8, :]
        )
        out[OWN : OWN + 8, :] = held[2 * AY : 2 * AY + 8, :]
        for comp in range(2):
            at = comp * AY + coarse
            out[WIND + 3 * comp : WIND + 3 * comp + 3, :] = held[at : at + 3, :]
        out[WIND + 6 : WIND + 8, :] = jnp.zeros((2, 128), jnp.float32)


def corners(from_left, from_right, blocks, owner, active, after):
    return pl.pallas_call(
        corners_kernel,
        in_specs=[VM] * 3 + [SM, SM, ANY],
        out_specs=[VM, VM, VM],
        out_shape=[f32(2 * AY + 8, 128), f32(WIND + 8, 128), f32(WIND + 8, 128)],
        compiler_params=SMALL,
        name="corners",
    )(from_left, from_right, blocks, owner, active, after)


def table(values):
    lane = lanes((8, 128))
    row = jnp.zeros((8, 128), jnp.float32)
    for c in range(values.shape[0]):
        row = jnp.where(lane == c, values[c], row)
    return row


def look(row, kinds):
    return jnp.take_along_axis(row, kinds, axis=1, mode="promise_in_bounds")


def values_kernel(fuel, after, fuel_rate, fuel_wind, fuel_heat, rate, drift, heat, three, kinds, arrived):
    move = pltpu.make_async_copy(fuel, kinds, arrived)
    move.start()
    tables = [table(fuel_rate), table(fuel_wind), table(fuel_heat)]
    for i in range(3):
        three[8 * i : 8 * i + 8, :] = tables[i]
    move.wait()

    def own_rows(i, _):
        at = pl.multiple_of(i * 8, 8)
        for c in range(0, FX, 128):
            found = kinds[pl.ds(at, 8), c : c + 128]
            for row, out in zip(tables, (rate, drift, heat)):
                out[pl.ds(at, 8), c : c + 128] = look(row, found)
        return 0

    lax.fori_loop(0, FY // 8, own_rows, 0, unroll=4)


def values(fuel, after, *names):
    return pl.pallas_call(
        values_kernel,
        in_specs=[ANY, ANY, SM, SM, SM],
        out_specs=[VM] * 4,
        out_shape=[f32(FY, FX)] * 3 + [f32(24, 128)],
        scratch_shapes=[pltpu.VMEM((FY, FX), jnp.int32), pltpu.SemaphoreType.DMA(())],
        name="values",
    )(fuel, after, *names)


def sides_kernel(from_left, from_right, three, after, rate, drift, heat):
    lane8 = lanes((8, 128))
    tables = [three[8 * i : 8 * i + 8, :] for i in range(3)]

    def own_rows(i, _):
        at = pl.multiple_of(i * 8, 8)
        kinds = jnp.where(lane8 < HALF, from_left[pl.ds(at, 8), :], from_right[pl.ds(at, 8), :])
        kinds = pltpu.roll(kinds, HALF, 1).astype(jnp.int32)
        for row, out in zip(tables, (rate, drift, heat)):
            out[pl.ds(at, 8), :] = look(row, kinds)
        return 0

    lax.fori_loop(0, FY // 8, own_rows, 0, unroll=8)


def sides(*args):
    return pl.pallas_call(
        sides_kernel,
        in_specs=[VM, VM, VM, ANY],
        out_specs=[VM] * 3,
        out_shape=[f32(FY, 128)] * 3,
        compiler_params=SMALL,
        name="sides",
    )(*args)


def fuel_value(refs, at):
    parts = [ref[pl.ds(at, 8), :] for ref in refs]
    return parts[0] if len(parts) == 1 else jnp.concatenate(parts, axis=1)


def slab_kernel(
    level, from_left, from_right, from_up, from_down, corner_up, corner_down, held, three,
    side_rate, side_drift, side_heat, all_rate, all_drift, all_heat,
    level_out, slots,
    phi_a, phi_b, phi_c, edge_rate, edge_drift, edge_heat, east, north, winds, gates, sums, spread, gather,
    rate, drift, heat, arrived,
):
    moves = [
        pltpu.make_async_copy(source, buf, arrived.at[i])
        for i, (source, buf) in enumerate(((all_rate, rate), (all_drift, drift), (all_heat, heat)))
    ]
    for move in moves:
        move.start()
    group = lax.axis_index("grp")
    tile = lax.axis_index("tile")
    first_row = group == 0
    last_row = group == lax.axis_size("grp") - 1
    first_col = tile == 0
    last_col = tile == lax.axis_size("tile") - 1
    lane8 = lanes((8, 128))
    sub8 = lax.broadcasted_iota(jnp.int32, (8, COLS), 0)

    zero = jnp.zeros((PAD, COLS), jnp.float32)
    phi_a[0:PAD, :] = zero
    phi_a[ROWS - PAD : ROWS, :] = zero
    for rows, corner, at in ((from_up, corner_up, TOP - HALO), (from_down, corner_down, TOP + FY)):
        phi_a[at : at + HALO, 0:FX] = rows[0:HALO, :]
        phi_a[at : at + HALO, FX:COLS] = corner[0:HALO, :]

    def own_rows(i, _):
        at = pl.multiple_of(i * 8, 8)
        to = pl.multiple_of(i * 8 + TOP, 8)
        phi_a[pl.ds(to, 8), 0:FX] = level[pl.ds(at, 8), :]
        one = from_left[pl.ds(at, 8), :]
        two = from_right[pl.ds(at, 8), :]
        phi_a[pl.ds(to, 8), FX:COLS] = jnp.where(lane8 < HALF, two, one)
        return 0

    lax.fori_loop(0, FY // 8, own_rows, 0, unroll=4)
    tables = [
        (three[8 * i : 8 * i + 8, :], out) for i, out in enumerate((edge_rate, edge_drift, edge_heat))
    ]

    def halo_rows(i, _):
        at = pl.multiple_of(i * 8, 8)
        for rows, corner, start in ((from_up, corner_up, 0), (from_down, corner_down, HALO)):
            to = pl.multiple_of(at + start, 8)
            for c in range(NL):
                source, col = (corner, 0) if c == NL - 1 else (rows, 128 * c)
                kinds = source[pl.ds(pl.multiple_of(at + HALO, 8), 8), col : col + 128]
                kinds = kinds.astype(jnp.int32)
                for row, out in tables:
                    out[pl.ds(to, 8), 128 * c : 128 * c + 128] = look(row, kinds)
        return 0

    lax.fori_loop(0, HALO // 8, halo_rows, 0, unroll=6)

    for c in range(FX // 128):
        col = pl.ds(128 * c, 128)
        gates[0:8, col] = corner_up[OWN : OWN + 8, :]
        gates[8:16, col] = held[2 * AY : 2 * AY + 8, :]
        gates[16:24, col] = corner_down[OWN : OWN + 8, :]
    gates[0:8, FX:COLS] = corner_up[BESIDE : BESIDE + 8, :]
    gates[16:24, FX:COLS] = corner_down[BESIDE : BESIDE + 8, :]
    gates[8:16, FX:COLS] = jnp.where(
        lane8 < HALF, from_right[FY : FY + 8, :], from_left[FY : FY + 8, :]
    )

    for comp in range(2):
        base = comp * CR
        at = WIND + 3 * comp
        winds[base : base + 3, :] = corner_up[at : at + 3, :]
        winds[base + 3 + AY : base + 6 + AY, :] = corner_down[at : at + 3, :]
        winds[base + 3 : base + 3 + AY, :] = held[AY * comp : AY * comp + AY, :]
        winds[base + 6 + AY : base + CR, :] = jnp.zeros((CR - 6 - AY, 128), jnp.float32)

    spread[...] = (
        coarse_lane(lanes((128, COLS))) == lax.broadcasted_iota(jnp.int32, (128, COLS), 0)
    ).astype(jnp.bfloat16)
    gather[...] = (
        coarse_lane(lax.broadcasted_iota(jnp.int32, (COLS, 128), 0)) == lanes((COLS, 128))
    ).astype(jnp.bfloat16)

    def expand():
        wide = exact_dot(winds[...], spread[...])
        east[...] = wide[0:CR]
        north[...] = wide[CR : 2 * CR]

    def edges(phi):
        @pl.when(first_row)
        def _():
            phi[TOP - 1 : TOP, :] = phi[TOP : TOP + 1, :]

        @pl.when(last_row)
        def _():
            phi[TOP + FY : TOP + FY + 1, :] = phi[TOP + FY - 1 : TOP + FY, :]

        @pl.when(first_col)
        def _():
            old = phi[:, COLS - 128 : COLS]
            new = jnp.broadcast_to(phi[:, 0:1], (ROWS, 128))
            phi[:, COLS - 128 : COLS] = jnp.where(lanes((ROWS, 128)) == 127, new, old)

        @pl.when(last_col)
        def _():
            old = phi[:, FX : FX + 128]
            new = jnp.broadcast_to(phi[:, FX - 1 : FX], (ROWS, 128))
            phi[:, FX : FX + 128] = jnp.where(lanes((ROWS, 128)) == 0, new, old)

    own = ((rate, side_rate), (drift, side_drift), (heat, side_heat), TOP)
    upper_edge = ((edge_rate,), (edge_drift,), (edge_heat,), TOP - HALO)
    lower_edge = ((edge_rate,), (edge_drift,), (edge_heat,), TOP + FY - HALO)

    def update(phi, at, e, n, gate, fuels):
        before = phi[pl.ds(pl.multiple_of(at - 8, 8), 8), :]
        now = phi[pl.ds(at, 8), :]
        after = phi[pl.ds(pl.multiple_of(at + 8, 8), 8), :]
        south = jnp.where(sub8 == 0, pltpu.roll(before, 1, 0), pltpu.roll(now, 1, 0))
        above = jnp.where(sub8 == 7, pltpu.roll(after, 7, 0), pltpu.roll(now, 7, 0))
        west = pltpu.roll(now, 1, 1)
        east_cell = pltpu.roll(now, COLS - 1, 1)
        back_x = now - west
        ahead_x = east_cell - now
        back_y = now - south
        ahead_y = above - now
        bx = jnp.maximum(back_x, 0.0)
        ax = jnp.minimum(ahead_x, 0.0)
        by = jnp.maximum(back_y, 0.0)
        ay = jnp.minimum(ahead_y, 0.0)
        square = bx * bx + ax * ax + by * by + ay * ay + 1e-12
        slope = square * lax.rsqrt(square)
        carry = e * jnp.where(e > 0.0, back_x, ahead_x) + n * jnp.where(n > 0.0, back_y, ahead_y)
        there = pl.multiple_of(at - fuels[3], 8)
        change = fuel_value(fuels[0], there) * slope + fuel_value(fuels[1], there) * carry
        return now - gate * change

    def wind_row(ref, row):
        return jnp.broadcast_to(ref[pl.ds(row, 1), :], (8, COLS))

    def mix(a, b):
        return jnp.where(sub8 < 4, a, b)

    def band(phi, m, k, region, fuels, finish):
        at = pl.multiple_of(2 * PAD + 40 * m, 8)
        gate = jnp.broadcast_to(gates[region * 8 + k : region * 8 + k + 1, :], (8, COLS))
        row = 2 * m + 1
        for t in range(5):
            if t == 2:
                e = mix(wind_row(east, row), wind_row(east, row + 1))
                n = mix(wind_row(north, row), wind_row(north, row + 1))
            else:
                e, n = (wind_row(ref, row + t // 3) for ref in (east, north))
            here = pl.multiple_of(at + 8 * t, 8)
            finish(here, update(phi, here, e, n, gate, fuels), fuels)

    def tile_rows(phi, at, row, region, k, fuels):
        gate = jnp.broadcast_to(gates[region * 8 + k : region * 8 + k + 1, :], (8, COLS))
        return update(phi, at, wind_row(east, row), wind_row(north, row), gate, fuels)

    def own_bands(body):
        def step(m, _):
            body(m, 1, own)
            return 0

        lax.fori_loop(1, 9, step, 0, unroll=8)

    def store_to(out):
        def finish(here, new, fuels):
            out[pl.ds(here, 8), :] = new

        return finish

    def flux_band(before, phi, out, k):
        def body(m, region, fuels):
            parts = []

            def finish(here, new, fuels):
                if out is not None:
                    out[pl.ds(here, 8), :] = new
                else:
                    level_out[pl.ds(pl.multiple_of(here - TOP, 8), 8), :] = new[:, 0:FX]
                old = before[pl.ds(here, 8), :]
                there = pl.multiple_of(here - fuels[3], 8)
                parts.append(fuel_value(fuels[2], there) * (jnp.tanh(old) - jnp.tanh(new)))

            band(phi, m, k, region, fuels, finish)
            low = parts[0] + parts[1] + jnp.where(sub8 < 4, parts[2], 0.0)
            high = parts[3] + parts[4] + jnp.where(sub8 >= 4, parts[2], 0.0)
            sums[pl.ds(2 * m + 1, 1), :] = jnp.sum(low, axis=0, keepdims=True)
            sums[pl.ds(2 * m + 2, 1), :] = jnp.sum(high, axis=0, keepdims=True)

        return body

    def pooled():
        return exact_dot(sums[...], gather[...]) * (0.5 / (R * R))

    lane_c = lanes((CR, 128))
    row_c = lax.broadcasted_iota(jnp.int32, (CR, 128), 0)
    sums[...] = jnp.zeros((CR, COLS), jnp.float32)

    expand()
    edges(phi_a)
    phi_b[PAD : PAD + 8, :] = tile_rows(phi_a, PAD, 0, 0, 0, upper_edge)
    phi_b[ROWS - 2 * PAD : ROWS - PAD, :] = tile_rows(phi_a, ROWS - 2 * PAD, AY + 5, 2, 0, lower_edge)
    band(phi_a, 0, 0, 0, upper_edge, store_to(phi_b))
    band(phi_a, 9, 0, 2, lower_edge, store_to(phi_b))
    for move in moves:
        move.wait()
    own_bands(lambda m, region, fuels: band(phi_a, m, 0, region, fuels, store_to(phi_b)))
    edges(phi_b)
    second = flux_band(phi_a, phi_b, phi_c, 1)
    second(0, 0, upper_edge)
    second(9, 2, lower_edge)
    own_bands(second)
    edges(phi_c)

    flux0 = pooled()
    ahead = jnp.where(jnp.logical_or(lane_c == AX - 1, lane_c == LEFT), flux0, pltpu.roll(flux0, 127, 1))
    back = jnp.where(jnp.logical_or(lane_c == 0, lane_c == RIGHT), flux0, pltpu.roll(flux0, 1, 1))
    last_rows = jnp.logical_or(row_c == 2, row_c == AY + 2)
    first_rows = jnp.logical_or(row_c == 3, row_c == AY + 3)
    below = jnp.where(last_rows, flux0, pltpu.roll(flux0, CR - 1, 0))
    upper = jnp.where(first_rows, flux0, pltpu.roll(flux0, 1, 0))
    winds[0:CR, :] = 0.9 * winds[0:CR, :] + 20.0 * (ahead - back)
    winds[CR : 2 * CR, :] = 0.9 * winds[CR : 2 * CR, :] + 20.0 * (below - upper)
    expand()

    top = TOP - 8
    bottom = TOP + FY
    phi_b[top : top + 8, :] = tile_rows(phi_c, top, 2, 0, 2, upper_edge)
    phi_b[bottom : bottom + 8, :] = tile_rows(phi_c, bottom, AY + 3, 2, 2, lower_edge)
    own_bands(lambda m, region, fuels: band(phi_c, m, 2, region, fuels, store_to(phi_b)))
    edges(phi_b)
    own_bands(flux_band(phi_c, phi_b, None, 3))
    total = 0.9 * flux0 + pooled()

    packed = jnp.zeros((4, 128), jnp.float32)
    lane4 = lanes((4, 128))
    for q in range(4):
        moved = pltpu.roll(total, 32 * q, 1)[3 + 4 * q : 7 + 4 * q]
        packed = jnp.where(lane4 // AX == q, moved, packed)
    for k in range(NX * NZ):
        slots[k] = packed


def slab(*args):
    big = pltpu.VMEM((ROWS, COLS), jnp.float32)
    edge = pltpu.VMEM((2 * HALO, COLS), jnp.float32)
    return pl.pallas_call(
        slab_kernel,
        in_specs=[VM] * 12 + [ANY] * 3,
        out_specs=[VM, VM],
        out_shape=[f32(FY, FX), f32(NX * NZ, 4, 128)],
        scratch_shapes=[big] * 3
        + [edge] * 3
        + [
            pltpu.VMEM((CR, COLS), jnp.float32),
            pltpu.VMEM((CR, COLS), jnp.float32),
            pltpu.VMEM((2 * CR, 128), jnp.float32),
            pltpu.VMEM((CR, COLS), jnp.float32),
            pltpu.VMEM((CR, COLS), jnp.float32),
            pltpu.VMEM((128, COLS), jnp.bfloat16),
            pltpu.VMEM((COLS, 128), jnp.bfloat16),
        ]
        + [pltpu.VMEM((FY, FX), jnp.float32)] * 3
        + [
            pltpu.SemaphoreType.DMA((3,)),
        ],
        compiler_params=LARGE,
        name="slab",
    )(*args)


def final_kernel(owner, received, wind, wind_out):
    tile = lax.axis_index("tile")
    source = jnp.int32(0)
    for t in range(NX * NZ):
        source = jnp.where(owner[0, t] == tile, t, source)
    block = received[source]
    flux = jnp.concatenate([pltpu.roll(block, (128 - 32 * q) % 128, 1) for q in range(4)], axis=0)
    lane = lanes((AY, 128))
    row = lax.broadcasted_iota(jnp.int32, (AY, 128), 0)
    ahead = jnp.where(lane == AX - 1, flux, pltpu.roll(flux, 127, 1))
    back = jnp.where(lane == 0, flux, pltpu.roll(flux, 1, 1))
    below = jnp.where(row == AY - 1, flux, pltpu.roll(flux, AY - 1, 0))
    upper = jnp.where(row == 0, flux, pltpu.roll(flux, 1, 0))
    wind_out[0] = 0.81 * wind[0] + 20.0 * (ahead - back)[:, 0:AX]
    wind_out[1] = 0.81 * wind[1] + 20.0 * (below - upper)[:, 0:AX]


def final(owner, received, wind):
    return pl.pallas_call(
        final_kernel, in_specs=[SM, VM, VM], out_specs=VM, out_shape=f32(2, AY, AX),
        compiler_params=SMALL, name="final"
    )(owner, received, wind)


def shift(value, axis, step):
    size = lax.axis_size(axis)
    pairs = [(i, i + step) for i in range(size) if 0 <= i + step < size]
    return lax.ppermute(value, axis, pairs)


def shards(level, fuel, wind, owner, active, fuel_rate, fuel_wind, fuel_heat):
    active = jnp.transpose(active, (1, 2, 0))
    mine = blocks_of(wind)
    blocks = lax.all_to_all(mine, "tile", 0, 0, tiled=True)
    to_left, to_right, to_up, to_down, done = strips(level, fuel, active, mine)
    from_right = shift(to_left, "tile", -1)
    from_left = shift(to_right, "tile", 1)
    from_down = shift(to_up, "grp", -1)
    from_up = shift(to_down, "grp", 1)
    *own, three = values(fuel, done, fuel_rate, fuel_wind, fuel_heat)
    own = [pltpu.with_memory_space_constraint(value, pltpu.HBM) for value in own]
    held, to_up, to_down = corners(from_left, from_right, blocks, owner, active, own[0])
    corner_down = shift(to_up, "grp", -1)
    corner_up = shift(to_down, "grp", 1)
    beside = sides(from_left, from_right, three, held)
    level_out, flux = slab(
        level, from_left, from_right, from_up, from_down, corner_up, corner_down, held, three, *beside, *own
    )
    flux = lax.all_to_all(flux, "tile", 0, 0, tiled=True)
    return (level_out, final(owner, flux, wind))


def solution(mesh):
    in_specs = (
        P("grp", "tile"),
        P("grp", "tile"),
        P(None, "grp", "tile"),
        P("grp", None),
        P(None, "grp", "tile"),
        P(),
        P(),
        P(),
    )
    out_specs = (P("grp", "tile"), P(None, "grp", "tile"))
    return jax.shard_map(shards, mesh=mesh, in_specs=in_specs, out_specs=out_specs, check_vma=False)
```

```python
import jax
import jax.numpy as jnp
from jax import lax
from jax.experimental import pallas as pl
from jax.experimental.pallas import tpu as pltpu
from jax.sharding import PartitionSpec as P

R = 20
AY = 16
AX = 32
FY = 320
FX = 640
STEPS = 2
SUBSTEPS = 2
NZ = 16
NX = 4
HALO = 48
HALF = 64
PAD = 8
TOP = PAD + HALO
ROWS = TOP + FY + HALO + PAD
COLS = FX + 2 * HALF
NL = COLS // 128
RIGHT = 40
LEFT = 51
CR = 24

VM = pl.BlockSpec(memory_space=pltpu.VMEM)
SM = pl.BlockSpec(memory_space=pltpu.SMEM)
ANY = pl.BlockSpec(memory_space=pl.ANY)
SMALL = pltpu.CompilerParams(vmem_limit_bytes=4 * 1024 * 1024)
LARGE = pltpu.CompilerParams(vmem_limit_bytes=12 * 1024 * 1024)


def lanes(shape):
    return lax.broadcasted_iota(jnp.int32, shape, 1)


def f32(*shape):
    return jax.ShapeDtypeStruct(shape, jnp.float32)


def thirds(x):
    high = x.astype(jnp.bfloat16)
    rest = x - high.astype(jnp.float32)
    middle = rest.astype(jnp.bfloat16)
    low = (rest - middle.astype(jnp.float32)).astype(jnp.bfloat16)
    return jnp.concatenate([high, middle, low], axis=0)


def exact_dot(x, onehot):
    n = x.shape[0]
    out = jnp.dot(thirds(x), onehot, preferred_element_type=jnp.float32)
    return out[:n] + out[n : 2 * n] + out[2 * n :]


def coarse_lane(fine):
    own = fine // R
    right = RIGHT + (fine - FX) // R
    left = LEFT - (COLS - 1 - fine) // R
    edge = jnp.where(fine < FX + 3 * R, right, jnp.where(fine >= COLS - 3 * R, left, -1))
    return jnp.where(fine < FX, own, edge)


def strips_kernel(level, fuel, active, after, to_left, to_right, left_level, right_level, left_fuel, right_fuel, arrived):
    first, last = pl.ds(0, 128), pl.ds(FX - 128, 128)
    moves = [
        pltpu.make_async_copy(source.at[:, part], buf, arrived.at[i])
        for i, (source, part, buf) in enumerate((
            (level, first, left_level), (fuel, first, left_fuel),
            (level, last, right_level), (fuel, last, right_fuel),
        ))
    ]
    for move in moves:
        move.start()
    for k in range(8):
        row = jnp.full((1, 128), flag_of(active, k), jnp.float32)
        to_left[FY + k : FY + k + 1, :] = row
        to_right[FY + k : FY + k + 1, :] = row
    lane = lanes((FY, 128))
    moves[0].wait()
    moves[1].wait()
    to_left[0:FY, :] = jnp.where(
        lane < HALF, left_level[...], pltpu.roll(left_fuel[...].astype(jnp.float32), HALF, 1)
    )
    moves[2].wait()
    moves[3].wait()
    to_right[0:FY, :] = jnp.where(
        lane >= HALF, right_level[...], pltpu.roll(right_fuel[...].astype(jnp.float32), HALF, 1)
    )


def strips(level, fuel, active, after):
    strip = pltpu.VMEM((FY, 128), jnp.float32)
    kinds = pltpu.VMEM((FY, 128), jnp.int32)
    return pl.pallas_call(
        strips_kernel,
        in_specs=[ANY, ANY, SM, ANY],
        out_specs=[VM, VM],
        out_shape=[f32(FY + 8, 128), f32(FY + 8, 128)],
        scratch_shapes=[strip, strip, kinds, kinds, pltpu.SemaphoreType.DMA((4,))],
        name="strips",
    )(level, fuel, active, after)


def flag_of(active, k):
    return (active[0, 0, min(k, STEPS * SUBSTEPS - 1)] > 0).astype(jnp.float32)


def blocks_kernel(wind, slots):
    parts = [wind[0, 0:8, :], wind[0, 8:16, :], wind[1, 0:8, :], wind[1, 8:16, :]]
    block = jnp.concatenate(parts, axis=1)
    for k in range(NX):
        slots[k] = block


def blocks_of(wind):
    return pl.pallas_call(
        blocks_kernel, in_specs=[VM], out_specs=VM, out_shape=f32(NX, 8, 128), name="blocks"
    )(wind)


def route_kernel(owner, blocks, slots):
    tile = lax.axis_index("tile")
    first = (tile // NZ) * NZ
    inside = lanes((8, 128)) % AX
    for k in range(NZ):
        reader = first + k
        main = blocks[owner[0, reader] // NZ]
        left = blocks[owner[0, jnp.maximum(reader - 1, 0)] // NZ]
        right = blocks[owner[0, jnp.minimum(reader + 1, NX * NZ - 1)] // NZ]
        edges = jnp.where(inside >= AX - 3, left, jnp.where(inside < 3, right, 0.0))
        edges = pltpu.roll(edges, 3, 1)
        small = edges[0:2]
        for b in range(1, 4):
            small = small + pltpu.roll(edges[2 * b : 2 * b + 2], 8 * b, 1)
        for b in range(4):
            slots[5 * k + b] = main[2 * b : 2 * b + 2]
        slots[5 * k + 4] = small


def route(owner, blocks):
    return pl.pallas_call(
        route_kernel, in_specs=[SM, VM], out_specs=VM, out_shape=f32(5 * NZ, 2, 128),
        compiler_params=SMALL, name="route"
    )(owner, blocks)


def rows_kernel(
    level, fuel, from_left, from_right, blocks, owner, active, held, to_up, to_down,
):
    tile = lax.axis_index("tile")
    lane = lanes((HALO, 128))
    lane8 = lanes((8, 128))
    main_at = 5 * (owner[0, tile] % NZ)
    left_at = 5 * (owner[0, jnp.maximum(tile - 1, 0)] % NZ) + 4
    right_at = 5 * (owner[0, jnp.minimum(tile + 1, NX * NZ - 1)] % NZ) + 4
    main = jnp.concatenate([blocks[main_at + b] for b in range(4)], axis=0)
    left, right = (
        jnp.concatenate([pltpu.roll(small, (128 - 8 * b) % 128, 1) for b in range(4)], axis=0)
        for small in (blocks[left_at], blocks[right_at])
    )
    is_left = jnp.logical_and(lane8 >= LEFT - 2, lane8 <= LEFT)
    is_right = jnp.logical_and(lane8 >= RIGHT, lane8 <= RIGHT + 2)
    for q in range(4):
        own = pltpu.roll(main, (128 - 32 * q) % 128, 1)
        one = pltpu.roll(left, (LEFT - 2 - 32 * (q + 1)) % 128, 1)
        two = pltpu.roll(right, (RIGHT - 3 - 32 * q) % 128, 1)
        held[8 * q : 8 * q + 8, :] = jnp.where(
            lane8 < AX, own, jnp.where(is_left, one, jnp.where(is_right, two, 0.0))
        )
    for k in range(8):
        held[2 * AY + k : 2 * AY + k + 1, :] = jnp.full((1, 128), flag_of(active, k), jnp.float32)
    for out, start, coarse in ((to_up, 0, 0), (to_down, FY - HALO, AY - 3)):
        out[0:HALO, 0:FX] = level[start : start + HALO, :]
        out[HALO : 2 * HALO, 0:FX] = fuel[start : start + HALO, :].astype(jnp.float32)
        one = from_left[start : start + HALO, :]
        two = from_right[start : start + HALO, :]
        out[0:HALO, FX:COLS] = jnp.where(lane < HALF, two, one)
        out[HALO : 2 * HALO, FX:COLS] = pltpu.roll(jnp.where(lane < HALF, one, two), HALF, 1)
        for k in range(4):
            row = 2 * HALO + k
            out[row : row + 1, 0:FX] = jnp.full((1, FX), flag_of(active, k), jnp.float32)
            out[row : row + 1, FX:COLS] = jnp.where(
                lane[0:1] < HALF, from_right[FY + k : FY + k + 1, :], from_left[FY + k : FY + k + 1, :]
            )
        row = 2 * HALO + 4
        for c in range(6):
            at = (c // 3) * AY + coarse + c % 3
            out[row : row + 1, 128 * c : 128 * c + 128] = held[at : at + 1, :]
        out[row + 1 : row + 4, :] = jnp.zeros((3, COLS), jnp.float32)


def rows(level, fuel, from_left, from_right, blocks, owner, active):
    shape = (2 * HALO + 8, COLS)
    return pl.pallas_call(
        rows_kernel,
        in_specs=[VM] * 5 + [SM, SM],
        out_specs=[VM, VM, VM],
        out_shape=[f32(2 * AY + 8, 128), f32(*shape), f32(*shape)],
        compiler_params=SMALL,
        name="rows",
    )(level, fuel, from_left, from_right, blocks, owner, active)


def table(values):
    lane = lanes((8, 128))
    row = jnp.zeros((8, 128), jnp.float32)
    for c in range(values.shape[0]):
        row = jnp.where(lane == c, values[c], row)
    return row


def look(row, kinds):
    return jnp.take_along_axis(row, kinds, axis=1, mode="promise_in_bounds")


def values_kernel(
    fuel, from_left, from_right, after, fuel_rate, fuel_wind, fuel_heat, rate, drift, heat, three
):
    lane8 = lanes((8, 128))
    tables = [(table(fuel_rate), rate), (table(fuel_wind), drift), (table(fuel_heat), heat)]
    for i in range(3):
        three[8 * i : 8 * i + 8, :] = tables[i][0]

    def own_rows(i, _):
        at = pl.multiple_of(i * 8, 8)
        one = from_left[pl.ds(at, 8), :]
        two = from_right[pl.ds(at, 8), :]
        beside = pltpu.roll(jnp.where(lane8 < HALF, one, two), HALF, 1).astype(jnp.int32)
        for c in range(NL):
            kinds = beside if c == NL - 1 else fuel[pl.ds(at, 8), 128 * c : 128 * c + 128]
            for row, out in tables:
                out[pl.ds(at, 8), 128 * c : 128 * c + 128] = look(row, kinds)
        return 0

    lax.fori_loop(0, FY // 8, own_rows, 0, unroll=4)


def values(fuel, from_left, from_right, after, *names):
    return pl.pallas_call(
        values_kernel,
        in_specs=[VM, VM, VM, ANY, SM, SM, SM],
        out_specs=[VM] * 4,
        out_shape=[f32(FY, COLS)] * 3 + [f32(24, 128)],
        compiler_params=SMALL,
        name="values",
    )(fuel, from_left, from_right, after, *names)


def slab_kernel(
    level, from_left, from_right, from_up, from_down, held, rate, drift, heat, three,
    level_out, slots,
    phi_a, phi_b, phi_c, edge_rate, edge_drift, edge_heat, east, north, winds, gates, sums, spread, gather,
):
    group = lax.axis_index("grp")
    tile = lax.axis_index("tile")
    first_row = group == 0
    last_row = group == lax.axis_size("grp") - 1
    first_col = tile == 0
    last_col = tile == lax.axis_size("tile") - 1
    lane8 = lanes((8, 128))
    sub8 = lax.broadcasted_iota(jnp.int32, (8, COLS), 0)

    zero = jnp.zeros((PAD, COLS), jnp.float32)
    phi_a[0:PAD, :] = zero
    phi_a[ROWS - PAD : ROWS, :] = zero
    phi_a[TOP - HALO : TOP, :] = from_up[0:HALO, :]
    phi_a[TOP + FY : TOP + FY + HALO, :] = from_down[0:HALO, :]

    def own_rows(i, _):
        at = pl.multiple_of(i * 8, 8)
        to = pl.multiple_of(i * 8 + TOP, 8)
        phi_a[pl.ds(to, 8), 0:FX] = level[pl.ds(at, 8), :]
        one = from_left[pl.ds(at, 8), :]
        two = from_right[pl.ds(at, 8), :]
        phi_a[pl.ds(to, 8), FX:COLS] = jnp.where(lane8 < HALF, two, one)
        return 0

    lax.fori_loop(0, FY // 8, own_rows, 0, unroll=4)
    tables = [
        (three[8 * i : 8 * i + 8, :], out) for i, out in enumerate((edge_rate, edge_drift, edge_heat))
    ]

    def halo_rows(i, _):
        at = pl.multiple_of(i * 8, 8)
        for source, start in ((from_up, 0), (from_down, HALO)):
            to = pl.multiple_of(at + start, 8)
            for c in range(NL):
                kinds = source[pl.ds(pl.multiple_of(at + HALO, 8), 8), 128 * c : 128 * c + 128]
                kinds = kinds.astype(jnp.int32)
                for row, out in tables:
                    out[pl.ds(to, 8), 128 * c : 128 * c + 128] = look(row, kinds)
        return 0

    lax.fori_loop(0, HALO // 8, halo_rows, 0, unroll=6)

    gates[0:8, :] = from_up[2 * HALO : 2 * HALO + 8, :]
    gates[16:24, :] = from_down[2 * HALO : 2 * HALO + 8, :]
    for c in range(FX // 128):
        gates[8:16, 128 * c : 128 * c + 128] = held[2 * AY : 2 * AY + 8, :]
    gates[8:16, FX:COLS] = jnp.where(
        lane8 < HALF, from_right[FY : FY + 8, :], from_left[FY : FY + 8, :]
    )

    row = 2 * HALO + 4
    for comp in range(2):
        base = comp * CR
        for c in range(3):
            at = 128 * (3 * comp + c)
            winds[base + c : base + c + 1, :] = from_up[row : row + 1, at : at + 128]
            below = base + 3 + AY + c
            winds[below : below + 1, :] = from_down[row : row + 1, at : at + 128]
        winds[base + 3 : base + 3 + AY, :] = held[AY * comp : AY * comp + AY, :]
        winds[base + 6 + AY : base + CR, :] = jnp.zeros((CR - 6 - AY, 128), jnp.float32)

    spread[...] = (
        coarse_lane(lanes((128, COLS))) == lax.broadcasted_iota(jnp.int32, (128, COLS), 0)
    ).astype(jnp.bfloat16)
    gather[...] = (
        coarse_lane(lax.broadcasted_iota(jnp.int32, (COLS, 128), 0)) == lanes((COLS, 128))
    ).astype(jnp.bfloat16)

    def expand():
        wide = exact_dot(winds[...], spread[...])
        east[...] = wide[0:CR]
        north[...] = wide[CR : 2 * CR]

    def edges(phi):
        @pl.when(first_row)
        def _():
            phi[TOP - 1 : TOP, :] = phi[TOP : TOP + 1, :]

        @pl.when(last_row)
        def _():
            phi[TOP + FY : TOP + FY + 1, :] = phi[TOP + FY - 1 : TOP + FY, :]

        @pl.when(first_col)
        def _():
            old = phi[:, COLS - 128 : COLS]
            new = jnp.broadcast_to(phi[:, 0:1], (ROWS, 128))
            phi[:, COLS - 128 : COLS] = jnp.where(lanes((ROWS, 128)) == 127, new, old)

        @pl.when(last_col)
        def _():
            old = phi[:, FX : FX + 128]
            new = jnp.broadcast_to(phi[:, FX - 1 : FX], (ROWS, 128))
            phi[:, FX : FX + 128] = jnp.where(lanes((ROWS, 128)) == 0, new, old)

    own = (rate, drift, heat, TOP)
    upper_edge = (edge_rate, edge_drift, edge_heat, TOP - HALO)
    lower_edge = (edge_rate, edge_drift, edge_heat, TOP + FY - HALO)

    def update(phi, at, e, n, gate, fuels, cols=COLS):
        before = phi[pl.ds(pl.multiple_of(at - 8, 8), 8), :]
        now = phi[pl.ds(at, 8), :]
        after = phi[pl.ds(pl.multiple_of(at + 8, 8), 8), :]
        west = pltpu.roll(now, 1, 1)[:, 0:cols]
        east_cell = pltpu.roll(now, COLS - 1, 1)[:, 0:cols]
        before, now, after = before[:, 0:cols], now[:, 0:cols], after[:, 0:cols]
        e, n, gate, sub = e[:, 0:cols], n[:, 0:cols], gate[:, 0:cols], sub8[:, 0:cols]
        south = jnp.where(sub == 0, pltpu.roll(before, 1, 0), pltpu.roll(now, 1, 0))
        above = jnp.where(sub == 7, pltpu.roll(after, 7, 0), pltpu.roll(now, 7, 0))
        back_x = now - west
        ahead_x = east_cell - now
        back_y = now - south
        ahead_y = above - now
        bx = jnp.maximum(back_x, 0.0)
        ax = jnp.minimum(ahead_x, 0.0)
        by = jnp.maximum(back_y, 0.0)
        ay = jnp.minimum(ahead_y, 0.0)
        square = bx * bx + ax * ax + by * by + ay * ay + 1e-12
        slope = square * lax.rsqrt(square)
        carry = e * jnp.where(e > 0.0, back_x, ahead_x) + n * jnp.where(n > 0.0, back_y, ahead_y)
        there = pl.multiple_of(at - fuels[3], 8)
        change = fuels[0][pl.ds(there, 8), 0:cols] * slope + fuels[1][pl.ds(there, 8), 0:cols] * carry
        return now - gate * change

    def wind_row(ref, row):
        return jnp.broadcast_to(ref[pl.ds(row, 1), :], (8, COLS))

    def mix(a, b):
        return jnp.where(sub8 < 4, a, b)

    def band(phi, m, k, region, fuels, finish, cols=COLS):
        at = pl.multiple_of(2 * PAD + 40 * m, 8)
        gate = jnp.broadcast_to(gates[region * 8 + k : region * 8 + k + 1, :], (8, COLS))
        row = 2 * m + 1
        for t in range(5):
            if t == 2:
                e = mix(wind_row(east, row), wind_row(east, row + 1))
                n = mix(wind_row(north, row), wind_row(north, row + 1))
            else:
                e, n = (wind_row(ref, row + t // 3) for ref in (east, north))
            here = pl.multiple_of(at + 8 * t, 8)
            finish(here, update(phi, here, e, n, gate, fuels, cols), fuels)

    def tile_rows(phi, at, row, region, k, fuels):
        gate = jnp.broadcast_to(gates[region * 8 + k : region * 8 + k + 1, :], (8, COLS))
        return update(phi, at, wind_row(east, row), wind_row(north, row), gate, fuels)

    def own_bands(body):
        def step(m, _):
            body(m, 1, own)
            return 0

        lax.fori_loop(1, 9, step, 0, unroll=8)

    def store_to(out):
        def finish(here, new, fuels):
            out[pl.ds(here, 8), :] = new

        return finish

    def flux_band(before, phi, out, k):
        cols = COLS if out is not None else FX

        def body(m, region, fuels):
            parts = []

            def finish(here, new, fuels):
                if out is not None:
                    out[pl.ds(here, 8), :] = new
                else:
                    level_out[pl.ds(pl.multiple_of(here - TOP, 8), 8), :] = new
                old = before[pl.ds(here, 8), 0:cols]
                there = pl.multiple_of(here - fuels[3], 8)
                parts.append(fuels[2][pl.ds(there, 8), 0:cols] * (jnp.tanh(old) - jnp.tanh(new)))

            band(phi, m, k, region, fuels, finish, cols)
            low = parts[0] + parts[1] + jnp.where(sub8[:, 0:cols] < 4, parts[2], 0.0)
            high = parts[3] + parts[4] + jnp.where(sub8[:, 0:cols] >= 4, parts[2], 0.0)
            sums[pl.ds(2 * m + 1, 1), 0:cols] = jnp.sum(low, axis=0, keepdims=True)
            sums[pl.ds(2 * m + 2, 1), 0:cols] = jnp.sum(high, axis=0, keepdims=True)

        return body

    def pooled():
        return exact_dot(sums[...], gather[...]) * (0.5 / (R * R))

    lane_c = lanes((CR, 128))
    row_c = lax.broadcasted_iota(jnp.int32, (CR, 128), 0)
    sums[...] = jnp.zeros((CR, COLS), jnp.float32)

    expand()
    edges(phi_a)
    phi_b[PAD : PAD + 8, :] = tile_rows(phi_a, PAD, 0, 0, 0, upper_edge)
    phi_b[ROWS - 2 * PAD : ROWS - PAD, :] = tile_rows(phi_a, ROWS - 2 * PAD, AY + 5, 2, 0, lower_edge)
    band(phi_a, 0, 0, 0, upper_edge, store_to(phi_b))
    band(phi_a, 9, 0, 2, lower_edge, store_to(phi_b))
    own_bands(lambda m, region, fuels: band(phi_a, m, 0, region, fuels, store_to(phi_b)))
    edges(phi_b)
    second = flux_band(phi_a, phi_b, phi_c, 1)
    second(0, 0, upper_edge)
    second(9, 2, lower_edge)
    own_bands(second)
    edges(phi_c)

    flux0 = pooled()
    ahead = jnp.where(jnp.logical_or(lane_c == AX - 1, lane_c == LEFT), flux0, pltpu.roll(flux0, 127, 1))
    back = jnp.where(jnp.logical_or(lane_c == 0, lane_c == RIGHT), flux0, pltpu.roll(flux0, 1, 1))
    last_rows = jnp.logical_or(row_c == 2, row_c == AY + 2)
    first_rows = jnp.logical_or(row_c == 3, row_c == AY + 3)
    below = jnp.where(last_rows, flux0, pltpu.roll(flux0, CR - 1, 0))
    upper = jnp.where(first_rows, flux0, pltpu.roll(flux0, 1, 0))
    winds[0:CR, :] = 0.9 * winds[0:CR, :] + 20.0 * (ahead - back)
    winds[CR : 2 * CR, :] = 0.9 * winds[CR : 2 * CR, :] + 20.0 * (below - upper)
    expand()

    top = TOP - 8
    bottom = TOP + FY
    phi_b[top : top + 8, :] = tile_rows(phi_c, top, 2, 0, 2, upper_edge)
    phi_b[bottom : bottom + 8, :] = tile_rows(phi_c, bottom, AY + 3, 2, 2, lower_edge)
    own_bands(lambda m, region, fuels: band(phi_c, m, 2, region, fuels, store_to(phi_b)))
    edges(phi_b)
    own_bands(flux_band(phi_c, phi_b, None, 3))
    total = 0.9 * flux0 + pooled()

    packed = jnp.zeros((4, 128), jnp.float32)
    lane4 = lanes((4, 128))
    for q in range(4):
        moved = pltpu.roll(total, 32 * q, 1)[3 + 4 * q : 7 + 4 * q]
        packed = jnp.where(lane4 // AX == q, moved, packed)
    for k in range(NX * NZ):
        slots[k] = packed


def slab(*args):
    big = pltpu.VMEM((ROWS, COLS), jnp.float32)
    edge = pltpu.VMEM((2 * HALO, COLS), jnp.float32)
    return pl.pallas_call(
        slab_kernel,
        in_specs=[VM] * 10,
        out_specs=[VM, VM],
        out_shape=[f32(FY, FX), f32(NX * NZ, 4, 128)],
        scratch_shapes=[big] * 3
        + [edge] * 3
        + [
            pltpu.VMEM((CR, COLS), jnp.float32),
            pltpu.VMEM((CR, COLS), jnp.float32),
            pltpu.VMEM((2 * CR, 128), jnp.float32),
            pltpu.VMEM((CR, COLS), jnp.float32),
            pltpu.VMEM((CR, COLS), jnp.float32),
            pltpu.VMEM((128, COLS), jnp.bfloat16),
            pltpu.VMEM((COLS, 128), jnp.bfloat16),
        ],
        compiler_params=LARGE,
        name="slab",
    )(*args)


def final_kernel(owner, received, wind, wind_out):
    tile = lax.axis_index("tile")
    source = jnp.int32(0)
    for t in range(NX * NZ):
        source = jnp.where(owner[0, t] == tile, t, source)
    block = received[source]
    flux = jnp.concatenate([pltpu.roll(block, (128 - 32 * q) % 128, 1) for q in range(4)], axis=0)
    lane = lanes((AY, 128))
    row = lax.broadcasted_iota(jnp.int32, (AY, 128), 0)
    ahead = jnp.where(lane == AX - 1, flux, pltpu.roll(flux, 127, 1))
    back = jnp.where(lane == 0, flux, pltpu.roll(flux, 1, 1))
    below = jnp.where(row == AY - 1, flux, pltpu.roll(flux, AY - 1, 0))
    upper = jnp.where(row == 0, flux, pltpu.roll(flux, 1, 0))
    wind_out[0] = 0.81 * wind[0] + 20.0 * (ahead - back)[:, 0:AX]
    wind_out[1] = 0.81 * wind[1] + 20.0 * (below - upper)[:, 0:AX]


def final(owner, received, wind):
    return pl.pallas_call(
        final_kernel, in_specs=[SM, VM, VM], out_specs=VM, out_shape=f32(2, AY, AX),
        compiler_params=SMALL, name="final"
    )(owner, received, wind)


def shift(value, axis, step):
    size = lax.axis_size(axis)
    pairs = [(i, i + step) for i in range(size) if 0 <= i + step < size]
    return lax.ppermute(value, axis, pairs)


def shards(level, fuel, wind, owner, active, fuel_rate, fuel_wind, fuel_heat):
    active = jnp.transpose(active, (1, 2, 0))
    along_x = [[x * NZ + z for x in range(NX)] for z in range(NZ)]
    along_z = [[x * NZ + z for z in range(NZ)] for x in range(NX)]
    mine = blocks_of(wind)
    blocks = lax.all_to_all(mine, "tile", 0, 0, tiled=True, axis_index_groups=along_x)
    to_left, to_right = strips(level, fuel, active, mine)
    from_right = shift(to_left, "tile", -1)
    from_left = shift(to_right, "tile", 1)
    blocks = route(owner, blocks)
    blocks = lax.all_to_all(blocks, "tile", 0, 0, tiled=True, axis_index_groups=along_z)
    held, to_up, to_down = rows(level, fuel, from_left, from_right, blocks, owner, active)
    from_down = shift(to_up, "grp", -1)
    from_up = shift(to_down, "grp", 1)
    coefficients = values(fuel, from_left, from_right, held, fuel_rate, fuel_wind, fuel_heat)
    level_out, flux = slab(level, from_left, from_right, from_up, from_down, held, *coefficients)
    flux = lax.all_to_all(flux, "tile", 0, 0, tiled=True)
    return (level_out, final(owner, flux, wind))


def solution(mesh):
    in_specs = (
        P("grp", "tile"),
        P("grp", "tile"),
        P(None, "grp", "tile"),
        P("grp", None),
        P(None, "grp", "tile"),
        P(),
        P(),
        P(),
    )
    out_specs = (P("grp", "tile"), P(None, "grp", "tile"))
    return jax.shard_map(shards, mesh=mesh, in_specs=in_specs, out_specs=out_specs, check_vma=False)
```

```python
import jax
import jax.numpy as jnp
from jax import lax
from jax.experimental import pallas as pl
from jax.experimental.pallas import tpu as pltpu
from jax.sharding import PartitionSpec as P

R = 20
AY = 16
AX = 32
FY = 320
FX = 640
STEPS = 2
SUBSTEPS = 2
NZ = 16
NX = 4
HALO = 48
HALF = 64
PAD = 8
TOP = PAD + HALO
ROWS = TOP + FY + HALO + PAD
COLS = FX + 2 * HALF
NL = COLS // 128
RIGHT = 40
LEFT = 51
CR = 24

VM = pl.BlockSpec(memory_space=pltpu.VMEM)
SM = pl.BlockSpec(memory_space=pltpu.SMEM)
ANY = pl.BlockSpec(memory_space=pl.ANY)
SMALL = pltpu.CompilerParams(vmem_limit_bytes=4 * 1024 * 1024)
LARGE = pltpu.CompilerParams(vmem_limit_bytes=12 * 1024 * 1024)


def lanes(shape):
    return lax.broadcasted_iota(jnp.int32, shape, 1)


def f32(*shape):
    return jax.ShapeDtypeStruct(shape, jnp.float32)


def thirds(x):
    high = x.astype(jnp.bfloat16)
    rest = x - high.astype(jnp.float32)
    middle = rest.astype(jnp.bfloat16)
    low = (rest - middle.astype(jnp.float32)).astype(jnp.bfloat16)
    return jnp.concatenate([high, middle, low], axis=0)


def exact_dot(x, onehot):
    n = x.shape[0]
    out = jnp.dot(thirds(x), onehot, preferred_element_type=jnp.float32)
    return out[:n] + out[n : 2 * n] + out[2 * n :]


def coarse_lane(fine):
    own = fine // R
    right = RIGHT + (fine - FX) // R
    left = LEFT - (COLS - 1 - fine) // R
    edge = jnp.where(fine < FX + 3 * R, right, jnp.where(fine >= COLS - 3 * R, left, -1))
    return jnp.where(fine < FX, own, edge)


def strips_kernel(level, fuel, active, after, to_left, to_right, left_level, right_level, left_fuel, right_fuel, arrived):
    first, last = pl.ds(0, 128), pl.ds(FX - 128, 128)
    moves = [
        pltpu.make_async_copy(source.at[:, part], buf, arrived.at[i])
        for i, (source, part, buf) in enumerate((
            (level, first, left_level), (fuel, first, left_fuel),
            (level, last, right_level), (fuel, last, right_fuel),
        ))
    ]
    for move in moves:
        move.start()
    for k in range(8):
        row = jnp.full((1, 128), flag_of(active, k), jnp.float32)
        to_left[FY + k : FY + k + 1, :] = row
        to_right[FY + k : FY + k + 1, :] = row
    lane = lanes((FY, 128))
    moves[0].wait()
    moves[1].wait()
    to_left[0:FY, :] = jnp.where(
        lane < HALF, left_level[...], pltpu.roll(left_fuel[...].astype(jnp.float32), HALF, 1)
    )
    moves[2].wait()
    moves[3].wait()
    to_right[0:FY, :] = jnp.where(
        lane >= HALF, right_level[...], pltpu.roll(right_fuel[...].astype(jnp.float32), HALF, 1)
    )


def strips(level, fuel, active, after):
    strip = pltpu.VMEM((FY, 128), jnp.float32)
    kinds = pltpu.VMEM((FY, 128), jnp.int32)
    return pl.pallas_call(
        strips_kernel,
        in_specs=[ANY, ANY, SM, ANY],
        out_specs=[VM, VM],
        out_shape=[f32(FY + 8, 128), f32(FY + 8, 128)],
        scratch_shapes=[strip, strip, kinds, kinds, pltpu.SemaphoreType.DMA((4,))],
        compiler_params=SMALL,
        name="strips",
    )(level, fuel, active, after)


def flag_of(active, k):
    return (active[0, 0, min(k, STEPS * SUBSTEPS - 1)] > 0).astype(jnp.float32)


def blocks_kernel(wind, slots):
    parts = [wind[0, 0:8, :], wind[0, 8:16, :], wind[1, 0:8, :], wind[1, 8:16, :]]
    block = jnp.concatenate(parts, axis=1)
    for k in range(NX * NZ):
        slots[k] = block


def blocks_of(wind):
    return pl.pallas_call(
        blocks_kernel, in_specs=[VM], out_specs=VM, out_shape=f32(NX * NZ, 8, 128), name="blocks"
    )(wind)


def rows_kernel(
    level, fuel, from_left, from_right, blocks, owner, active, held, to_up, to_down,
):
    tile = lax.axis_index("tile")
    lane = lanes((HALO, 128))
    lane8 = lanes((8, 128))
    main = blocks[owner[0, tile]]
    left = blocks[owner[0, jnp.maximum(tile - 1, 0)]]
    right = blocks[owner[0, jnp.minimum(tile + 1, NX * NZ - 1)]]
    is_left = jnp.logical_and(lane8 >= LEFT - 2, lane8 <= LEFT)
    is_right = jnp.logical_and(lane8 >= RIGHT, lane8 <= RIGHT + 2)
    for q in range(4):
        own = pltpu.roll(main, (128 - 32 * q) % 128, 1)
        one = pltpu.roll(left, (LEFT - 31 - 32 * q) % 128, 1)
        two = pltpu.roll(right, (RIGHT - 32 * q) % 128, 1)
        held[8 * q : 8 * q + 8, :] = jnp.where(
            lane8 < AX, own, jnp.where(is_left, one, jnp.where(is_right, two, 0.0))
        )
    for k in range(8):
        held[2 * AY + k : 2 * AY + k + 1, :] = jnp.full((1, 128), flag_of(active, k), jnp.float32)
    for out, start, coarse in ((to_up, 0, 0), (to_down, FY - HALO, AY - 3)):
        out[0:HALO, 0:FX] = level[start : start + HALO, :]
        out[HALO : 2 * HALO, 0:FX] = fuel[start : start + HALO, :].astype(jnp.float32)
        one = from_left[start : start + HALO, :]
        two = from_right[start : start + HALO, :]
        out[0:HALO, FX:COLS] = jnp.where(lane < HALF, two, one)
        out[HALO : 2 * HALO, FX:COLS] = pltpu.roll(jnp.where(lane < HALF, one, two), HALF, 1)
        for k in range(4):
            row = 2 * HALO + k
            out[row : row + 1, 0:FX] = jnp.full((1, FX), flag_of(active, k), jnp.float32)
            out[row : row + 1, FX:COLS] = jnp.where(
                lane[0:1] < HALF, from_right[FY + k : FY + k + 1, :], from_left[FY + k : FY + k + 1, :]
            )
        row = 2 * HALO + 4
        for c in range(6):
            at = (c // 3) * AY + coarse + c % 3
            out[row : row + 1, 128 * c : 128 * c + 128] = held[at : at + 1, :]
        out[row + 1 : row + 4, :] = jnp.zeros((3, COLS), jnp.float32)


def rows(level, fuel, from_left, from_right, blocks, owner, active):
    shape = (2 * HALO + 8, COLS)
    return pl.pallas_call(
        rows_kernel,
        in_specs=[VM] * 5 + [SM, SM],
        out_specs=[VM, VM, VM],
        out_shape=[f32(2 * AY + 8, 128), f32(*shape), f32(*shape)],
        compiler_params=SMALL,
        name="rows",
    )(level, fuel, from_left, from_right, blocks, owner, active)


def table(values):
    lane = lanes((8, 128))
    row = jnp.zeros((8, 128), jnp.float32)
    for c in range(values.shape[0]):
        row = jnp.where(lane == c, values[c], row)
    return row


def look(row, kinds):
    return jnp.take_along_axis(row, kinds, axis=1, mode="promise_in_bounds")


def values_kernel(
    fuel, from_left, from_right, after, fuel_rate, fuel_wind, fuel_heat, rate, drift, heat, three
):
    lane8 = lanes((8, 128))
    tables = [(table(fuel_rate), rate), (table(fuel_wind), drift), (table(fuel_heat), heat)]
    for i in range(3):
        three[8 * i : 8 * i + 8, :] = tables[i][0]

    def own_rows(i, _):
        at = pl.multiple_of(i * 8, 8)
        one = from_left[pl.ds(at, 8), :]
        two = from_right[pl.ds(at, 8), :]
        beside = pltpu.roll(jnp.where(lane8 < HALF, one, two), HALF, 1).astype(jnp.int32)
        for c in range(NL):
            kinds = beside if c == NL - 1 else fuel[pl.ds(at, 8), 128 * c : 128 * c + 128]
            for row, out in tables:
                out[pl.ds(at, 8), 128 * c : 128 * c + 128] = look(row, kinds)
        return 0

    lax.fori_loop(0, FY // 8, own_rows, 0, unroll=4)


def values(fuel, from_left, from_right, after, *names):
    return pl.pallas_call(
        values_kernel,
        in_specs=[VM, VM, VM, ANY, SM, SM, SM],
        out_specs=[VM] * 4,
        out_shape=[f32(FY, COLS)] * 3 + [f32(24, 128)],
        compiler_params=SMALL,
        name="values",
    )(fuel, from_left, from_right, after, *names)


def slab_kernel(
    level, from_left, from_right, from_up, from_down, held, rate, drift, heat, three,
    level_out, slots,
    phi_a, phi_b, phi_c, edge_rate, edge_drift, edge_heat, east, north, winds, gates, sums, spread, gather,
):
    group = lax.axis_index("grp")
    tile = lax.axis_index("tile")
    first_row = group == 0
    last_row = group == lax.axis_size("grp") - 1
    first_col = tile == 0
    last_col = tile == lax.axis_size("tile") - 1
    lane8 = lanes((8, 128))
    sub8 = lax.broadcasted_iota(jnp.int32, (8, COLS), 0)

    zero = jnp.zeros((PAD, COLS), jnp.float32)
    phi_a[0:PAD, :] = zero
    phi_a[ROWS - PAD : ROWS, :] = zero
    phi_a[TOP - HALO : TOP, :] = from_up[0:HALO, :]
    phi_a[TOP + FY : TOP + FY + HALO, :] = from_down[0:HALO, :]

    def own_rows(i, _):
        at = pl.multiple_of(i * 8, 8)
        to = pl.multiple_of(i * 8 + TOP, 8)
        phi_a[pl.ds(to, 8), 0:FX] = level[pl.ds(at, 8), :]
        one = from_left[pl.ds(at, 8), :]
        two = from_right[pl.ds(at, 8), :]
        phi_a[pl.ds(to, 8), FX:COLS] = jnp.where(lane8 < HALF, two, one)
        return 0

    lax.fori_loop(0, FY // 8, own_rows, 0, unroll=4)
    tables = [
        (three[8 * i : 8 * i + 8, :], out) for i, out in enumerate((edge_rate, edge_drift, edge_heat))
    ]

    def halo_rows(i, _):
        at = pl.multiple_of(i * 8, 8)
        for source, start in ((from_up, 0), (from_down, HALO)):
            to = pl.multiple_of(at + start, 8)
            for c in range(NL):
                kinds = source[pl.ds(pl.multiple_of(at + HALO, 8), 8), 128 * c : 128 * c + 128]
                kinds = kinds.astype(jnp.int32)
                for row, out in tables:
                    out[pl.ds(to, 8), 128 * c : 128 * c + 128] = look(row, kinds)
        return 0

    lax.fori_loop(0, HALO // 8, halo_rows, 0, unroll=6)

    gates[0:8, :] = from_up[2 * HALO : 2 * HALO + 8, :]
    gates[16:24, :] = from_down[2 * HALO : 2 * HALO + 8, :]
    for c in range(FX // 128):
        gates[8:16, 128 * c : 128 * c + 128] = held[2 * AY : 2 * AY + 8, :]
    gates[8:16, FX:COLS] = jnp.where(
        lane8 < HALF, from_right[FY : FY + 8, :], from_left[FY : FY + 8, :]
    )

    row = 2 * HALO + 4
    for comp in range(2):
        base = comp * CR
        for c in range(3):
            at = 128 * (3 * comp + c)
            winds[base + c : base + c + 1, :] = from_up[row : row + 1, at : at + 128]
            below = base + 3 + AY + c
            winds[below : below + 1, :] = from_down[row : row + 1, at : at + 128]
        winds[base + 3 : base + 3 + AY, :] = held[AY * comp : AY * comp + AY, :]
        winds[base + 6 + AY : base + CR, :] = jnp.zeros((CR - 6 - AY, 128), jnp.float32)

    spread[...] = (
        coarse_lane(lanes((128, COLS))) == lax.broadcasted_iota(jnp.int32, (128, COLS), 0)
    ).astype(jnp.bfloat16)
    gather[...] = (
        coarse_lane(lax.broadcasted_iota(jnp.int32, (COLS, 128), 0)) == lanes((COLS, 128))
    ).astype(jnp.bfloat16)

    def expand():
        wide = exact_dot(winds[...], spread[...])
        east[...] = wide[0:CR]
        north[...] = wide[CR : 2 * CR]

    def edges(phi):
        @pl.when(first_row)
        def _():
            phi[TOP - 1 : TOP, :] = phi[TOP : TOP + 1, :]

        @pl.when(last_row)
        def _():
            phi[TOP + FY : TOP + FY + 1, :] = phi[TOP + FY - 1 : TOP + FY, :]

        @pl.when(first_col)
        def _():
            old = phi[:, COLS - 128 : COLS]
            new = jnp.broadcast_to(phi[:, 0:1], (ROWS, 128))
            phi[:, COLS - 128 : COLS] = jnp.where(lanes((ROWS, 128)) == 127, new, old)

        @pl.when(last_col)
        def _():
            old = phi[:, FX : FX + 128]
            new = jnp.broadcast_to(phi[:, FX - 1 : FX], (ROWS, 128))
            phi[:, FX : FX + 128] = jnp.where(lanes((ROWS, 128)) == 0, new, old)

    own = (rate, drift, heat, TOP)
    upper_edge = (edge_rate, edge_drift, edge_heat, TOP - HALO)
    lower_edge = (edge_rate, edge_drift, edge_heat, TOP + FY - HALO)

    def update(phi, at, e, n, gate, fuels, cols=COLS):
        before = phi[pl.ds(pl.multiple_of(at - 8, 8), 8), :]
        now = phi[pl.ds(at, 8), :]
        after = phi[pl.ds(pl.multiple_of(at + 8, 8), 8), :]
        west = pltpu.roll(now, 1, 1)[:, 0:cols]
        east_cell = pltpu.roll(now, COLS - 1, 1)[:, 0:cols]
        before, now, after = before[:, 0:cols], now[:, 0:cols], after[:, 0:cols]
        e, n, gate, sub = e[:, 0:cols], n[:, 0:cols], gate[:, 0:cols], sub8[:, 0:cols]
        south = jnp.where(sub == 0, pltpu.roll(before, 1, 0), pltpu.roll(now, 1, 0))
        above = jnp.where(sub == 7, pltpu.roll(after, 7, 0), pltpu.roll(now, 7, 0))
        back_x = now - west
        ahead_x = east_cell - now
        back_y = now - south
        ahead_y = above - now
        bx = jnp.maximum(back_x, 0.0)
        ax = jnp.minimum(ahead_x, 0.0)
        by = jnp.maximum(back_y, 0.0)
        ay = jnp.minimum(ahead_y, 0.0)
        square = bx * bx + ax * ax + by * by + ay * ay + 1e-12
        slope = square * lax.rsqrt(square)
        carry = e * jnp.where(e > 0.0, back_x, ahead_x) + n * jnp.where(n > 0.0, back_y, ahead_y)
        there = pl.multiple_of(at - fuels[3], 8)
        change = fuels[0][pl.ds(there, 8), 0:cols] * slope + fuels[1][pl.ds(there, 8), 0:cols] * carry
        return now - gate * change

    def wind_row(ref, row):
        return jnp.broadcast_to(ref[pl.ds(row, 1), :], (8, COLS))

    def mix(a, b):
        return jnp.where(sub8 < 4, a, b)

    def band(phi, m, k, region, fuels, finish, cols=COLS):
        at = pl.multiple_of(2 * PAD + 40 * m, 8)
        gate = jnp.broadcast_to(gates[region * 8 + k : region * 8 + k + 1, :], (8, COLS))
        row = 2 * m + 1
        for t in range(5):
            if t == 2:
                e = mix(wind_row(east, row), wind_row(east, row + 1))
                n = mix(wind_row(north, row), wind_row(north, row + 1))
            else:
                e, n = (wind_row(ref, row + t // 3) for ref in (east, north))
            here = pl.multiple_of(at + 8 * t, 8)
            finish(here, update(phi, here, e, n, gate, fuels, cols), fuels)

    def tile_rows(phi, at, row, region, k, fuels):
        gate = jnp.broadcast_to(gates[region * 8 + k : region * 8 + k + 1, :], (8, COLS))
        return update(phi, at, wind_row(east, row), wind_row(north, row), gate, fuels)

    def own_bands(body):
        def step(m, _):
            body(m, 1, own)
            return 0

        lax.fori_loop(1, 9, step, 0, unroll=8)

    def store_to(out):
        def finish(here, new, fuels):
            out[pl.ds(here, 8), :] = new

        return finish

    def flux_band(before, phi, out, k):
        cols = COLS if out is not None else FX

        def body(m, region, fuels):
            parts = []

            def finish(here, new, fuels):
                if out is not None:
                    out[pl.ds(here, 8), :] = new
                else:
                    level_out[pl.ds(pl.multiple_of(here - TOP, 8), 8), :] = new
                old = before[pl.ds(here, 8), 0:cols]
                there = pl.multiple_of(here - fuels[3], 8)
                parts.append(fuels[2][pl.ds(there, 8), 0:cols] * (jnp.tanh(old) - jnp.tanh(new)))

            band(phi, m, k, region, fuels, finish, cols)
            low = parts[0] + parts[1] + jnp.where(sub8[:, 0:cols] < 4, parts[2], 0.0)
            high = parts[3] + parts[4] + jnp.where(sub8[:, 0:cols] >= 4, parts[2], 0.0)
            sums[pl.ds(2 * m + 1, 1), 0:cols] = jnp.sum(low, axis=0, keepdims=True)
            sums[pl.ds(2 * m + 2, 1), 0:cols] = jnp.sum(high, axis=0, keepdims=True)

        return body

    def pooled():
        return exact_dot(sums[...], gather[...]) * (0.5 / (R * R))

    lane_c = lanes((CR, 128))
    row_c = lax.broadcasted_iota(jnp.int32, (CR, 128), 0)
    sums[...] = jnp.zeros((CR, COLS), jnp.float32)

    expand()
    edges(phi_a)
    phi_b[PAD : PAD + 8, :] = tile_rows(phi_a, PAD, 0, 0, 0, upper_edge)
    phi_b[ROWS - 2 * PAD : ROWS - PAD, :] = tile_rows(phi_a, ROWS - 2 * PAD, AY + 5, 2, 0, lower_edge)
    band(phi_a, 0, 0, 0, upper_edge, store_to(phi_b))
    band(phi_a, 9, 0, 2, lower_edge, store_to(phi_b))
    own_bands(lambda m, region, fuels: band(phi_a, m, 0, region, fuels, store_to(phi_b)))
    edges(phi_b)
    second = flux_band(phi_a, phi_b, phi_c, 1)
    second(0, 0, upper_edge)
    second(9, 2, lower_edge)
    own_bands(second)
    edges(phi_c)

    flux0 = pooled()
    ahead = jnp.where(jnp.logical_or(lane_c == AX - 1, lane_c == LEFT), flux0, pltpu.roll(flux0, 127, 1))
    back = jnp.where(jnp.logical_or(lane_c == 0, lane_c == RIGHT), flux0, pltpu.roll(flux0, 1, 1))
    last_rows = jnp.logical_or(row_c == 2, row_c == AY + 2)
    first_rows = jnp.logical_or(row_c == 3, row_c == AY + 3)
    below = jnp.where(last_rows, flux0, pltpu.roll(flux0, CR - 1, 0))
    upper = jnp.where(first_rows, flux0, pltpu.roll(flux0, 1, 0))
    winds[0:CR, :] = 0.9 * winds[0:CR, :] + 20.0 * (ahead - back)
    winds[CR : 2 * CR, :] = 0.9 * winds[CR : 2 * CR, :] + 20.0 * (below - upper)
    expand()

    top = TOP - 8
    bottom = TOP + FY
    phi_b[top : top + 8, :] = tile_rows(phi_c, top, 2, 0, 2, upper_edge)
    phi_b[bottom : bottom + 8, :] = tile_rows(phi_c, bottom, AY + 3, 2, 2, lower_edge)
    own_bands(lambda m, region, fuels: band(phi_c, m, 2, region, fuels, store_to(phi_b)))
    edges(phi_b)
    own_bands(flux_band(phi_c, phi_b, None, 3))
    total = 0.9 * flux0 + pooled()

    packed = jnp.zeros((4, 128), jnp.float32)
    lane4 = lanes((4, 128))
    for q in range(4):
        moved = pltpu.roll(total, 32 * q, 1)[3 + 4 * q : 7 + 4 * q]
        packed = jnp.where(lane4 // AX == q, moved, packed)
    for k in range(NX * NZ):
        slots[k] = packed


def slab(*args):
    big = pltpu.VMEM((ROWS, COLS), jnp.float32)
    edge = pltpu.VMEM((2 * HALO, COLS), jnp.float32)
    return pl.pallas_call(
        slab_kernel,
        in_specs=[VM] * 10,
        out_specs=[VM, VM],
        out_shape=[f32(FY, FX), f32(NX * NZ, 4, 128)],
        scratch_shapes=[big] * 3
        + [edge] * 3
        + [
            pltpu.VMEM((CR, COLS), jnp.float32),
            pltpu.VMEM((CR, COLS), jnp.float32),
            pltpu.VMEM((2 * CR, 128), jnp.float32),
            pltpu.VMEM((CR, COLS), jnp.float32),
            pltpu.VMEM((CR, COLS), jnp.float32),
            pltpu.VMEM((128, COLS), jnp.bfloat16),
            pltpu.VMEM((COLS, 128), jnp.bfloat16),
        ],
        compiler_params=LARGE,
        name="slab",
    )(*args)


def final_kernel(owner, received, wind, wind_out):
    tile = lax.axis_index("tile")
    source = jnp.int32(0)
    for t in range(NX * NZ):
        source = jnp.where(owner[0, t] == tile, t, source)
    block = received[source]
    flux = jnp.concatenate([pltpu.roll(block, (128 - 32 * q) % 128, 1) for q in range(4)], axis=0)
    lane = lanes((AY, 128))
    row = lax.broadcasted_iota(jnp.int32, (AY, 128), 0)
    ahead = jnp.where(lane == AX - 1, flux, pltpu.roll(flux, 127, 1))
    back = jnp.where(lane == 0, flux, pltpu.roll(flux, 1, 1))
    below = jnp.where(row == AY - 1, flux, pltpu.roll(flux, AY - 1, 0))
    upper = jnp.where(row == 0, flux, pltpu.roll(flux, 1, 0))
    wind_out[0] = 0.81 * wind[0] + 20.0 * (ahead - back)[:, 0:AX]
    wind_out[1] = 0.81 * wind[1] + 20.0 * (below - upper)[:, 0:AX]


def final(owner, received, wind):
    return pl.pallas_call(
        final_kernel, in_specs=[SM, VM, VM], out_specs=VM, out_shape=f32(2, AY, AX),
        compiler_params=SMALL, name="final"
    )(owner, received, wind)


def shift(value, axis, step):
    size = lax.axis_size(axis)
    pairs = [(i, i + step) for i in range(size) if 0 <= i + step < size]
    return lax.ppermute(value, axis, pairs)


def shards(level, fuel, wind, owner, active, fuel_rate, fuel_wind, fuel_heat):
    active = jnp.transpose(active, (1, 2, 0))
    mine = blocks_of(wind)
    blocks = lax.all_to_all(mine, "tile", 0, 0, tiled=True)
    stay = [pltpu.with_memory_space_constraint(value, pltpu.HBM) for value in (level, fuel, active, mine)]
    to_left, to_right = strips(*stay)
    from_right = shift(to_left, "tile", -1)
    from_left = shift(to_right, "tile", 1)
    held, to_up, to_down = rows(level, fuel, from_left, from_right, blocks, owner, active)
    from_down = shift(to_up, "grp", -1)
    from_up = shift(to_down, "grp", 1)
    coefficients = values(fuel, from_left, from_right, held, fuel_rate, fuel_wind, fuel_heat)
    level_out, flux = slab(level, from_left, from_right, from_up, from_down, held, *coefficients)
    flux = lax.all_to_all(flux, "tile", 0, 0, tiled=True)
    return (level_out, final(owner, flux, wind))


def solution(mesh):
    in_specs = (
        P("grp", "tile"),
        P("grp", "tile"),
        P(None, "grp", "tile"),
        P("grp", None),
        P(None, "grp", "tile"),
        P(),
        P(),
        P(),
    )
    out_specs = (P("grp", "tile"), P(None, "grp", "tile"))
    return jax.shard_map(shards, mesh=mesh, in_specs=in_specs, out_specs=out_specs, check_vma=False)
```

```python
import jax
import jax.numpy as jnp
from jax import lax
from jax.experimental import pallas as pl
from jax.experimental.pallas import tpu as pltpu
from jax.sharding import PartitionSpec as P

R = 20
AY = 16
AX = 32
FY = 320
FX = 640
STEPS = 2
SUBSTEPS = 2
NZ = 16
NX = 4
HALO = 48
HALF = 64
PAD = 8
TOP = PAD + HALO
ROWS = TOP + FY + HALO + PAD
COLS = FX + 2 * HALF
NL = COLS // 128
RIGHT = 40
LEFT = 51
CR = 24
UP_ROWS = (42, 43, 44)
DOWN_ROWS = (5, 4, 0)

VM = pl.BlockSpec(memory_space=pltpu.VMEM)
SM = pl.BlockSpec(memory_space=pltpu.SMEM)
ANY = pl.BlockSpec(memory_space=pl.ANY)
SMALL = pltpu.CompilerParams(vmem_limit_bytes=4 * 1024 * 1024)
LARGE = pltpu.CompilerParams(vmem_limit_bytes=12 * 1024 * 1024)


def lanes(shape):
    return lax.broadcasted_iota(jnp.int32, shape, 1)


def f32(*shape):
    return jax.ShapeDtypeStruct(shape, jnp.float32)


def thirds(x):
    high = x.astype(jnp.bfloat16)
    rest = x - high.astype(jnp.float32)
    middle = rest.astype(jnp.bfloat16)
    low = (rest - middle.astype(jnp.float32)).astype(jnp.bfloat16)
    return jnp.concatenate([high, middle, low], axis=0)


def exact_dot(x, onehot):
    n = x.shape[0]
    out = jnp.dot(thirds(x), onehot, preferred_element_type=jnp.float32)
    return out[:n] + out[n : 2 * n] + out[2 * n :]


def coarse_lane(fine):
    own = fine // R
    right = RIGHT + (fine - FX) // R
    left = LEFT - (COLS - 1 - fine) // R
    edge = jnp.where(fine < FX + 3 * R, right, jnp.where(fine >= COLS - 3 * R, left, -1))
    return jnp.where(fine < FX, own, edge)


def strips_kernel(level, fuel, active, after, to_left, to_right, left_level, right_level, left_fuel, right_fuel, arrived):
    first, last = pl.ds(0, 128), pl.ds(FX - 128, 128)
    moves = [
        pltpu.make_async_copy(source.at[:, part], buf, arrived.at[i])
        for i, (source, part, buf) in enumerate((
            (level, first, left_level), (fuel, first, left_fuel),
            (level, last, right_level), (fuel, last, right_fuel),
        ))
    ]
    for move in moves:
        move.start()
    for k in range(8):
        row = jnp.full((1, 128), flag_of(active, k), jnp.float32)
        to_left[FY + k : FY + k + 1, :] = row
        to_right[FY + k : FY + k + 1, :] = row
    lane = lanes((FY, 128))
    moves[0].wait()
    moves[1].wait()
    to_left[0:FY, :] = jnp.where(
        lane < HALF, left_level[...], pltpu.roll(left_fuel[...].astype(jnp.float32), HALF, 1)
    )
    moves[2].wait()
    moves[3].wait()
    to_right[0:FY, :] = jnp.where(
        lane >= HALF, right_level[...], pltpu.roll(right_fuel[...].astype(jnp.float32), HALF, 1)
    )


def strips(level, fuel, active, after):
    strip = pltpu.VMEM((FY, 128), jnp.float32)
    kinds = pltpu.VMEM((FY, 128), jnp.int32)
    return pl.pallas_call(
        strips_kernel,
        in_specs=[ANY, ANY, SM, ANY],
        out_specs=[VM, VM],
        out_shape=[f32(FY + 8, 128), f32(FY + 8, 128)],
        scratch_shapes=[strip, strip, kinds, kinds, pltpu.SemaphoreType.DMA((4,))],
        compiler_params=SMALL,
        name="strips",
    )(level, fuel, active, after)


def flag_of(active, k):
    return (active[0, 0, min(k, STEPS * SUBSTEPS - 1)] > 0).astype(jnp.float32)


def blocks_kernel(wind, slots):
    parts = [wind[0, 0:8, :], wind[0, 8:16, :], wind[1, 0:8, :], wind[1, 8:16, :]]
    block = jnp.concatenate(parts, axis=1)
    for k in range(NX * NZ):
        slots[k] = block


def blocks_of(wind):
    return pl.pallas_call(
        blocks_kernel, in_specs=[VM], out_specs=VM, out_shape=f32(NX * NZ, 8, 128), name="blocks"
    )(wind)


def rows_kernel(
    level, fuel, from_left, from_right, blocks, owner, active, held, to_up, to_down,
):
    tile = lax.axis_index("tile")
    lane = lanes((HALO, 128))
    lane8 = lanes((8, 128))
    main = blocks[owner[0, tile]]
    left = blocks[owner[0, jnp.maximum(tile - 1, 0)]]
    right = blocks[owner[0, jnp.minimum(tile + 1, NX * NZ - 1)]]
    is_left = jnp.logical_and(lane8 >= LEFT - 2, lane8 <= LEFT)
    is_right = jnp.logical_and(lane8 >= RIGHT, lane8 <= RIGHT + 2)
    for q in range(4):
        own = pltpu.roll(main, (128 - 32 * q) % 128, 1)
        one = pltpu.roll(left, (LEFT - 31 - 32 * q) % 128, 1)
        two = pltpu.roll(right, (RIGHT - 32 * q) % 128, 1)
        held[8 * q : 8 * q + 8, :] = jnp.where(
            lane8 < AX, own, jnp.where(is_left, one, jnp.where(is_right, two, 0.0))
        )
    for k in range(8):
        held[2 * AY + k : 2 * AY + k + 1, :] = jnp.full((1, 128), flag_of(active, k), jnp.float32)
    for out, start, near, more, coarse, (fuel_at, wind_at, flags_at) in (
        (to_up, 0, 0, 40, 0, UP_ROWS),
        (to_down, FY - HALO, 8, 7, AY - 3, DOWN_ROWS),
    ):
        one = from_left[start : start + HALO, :]
        two = from_right[start : start + HALO, :]
        side = pltpu.roll(jnp.where(lane < HALF, one, two), HALF, 1)
        kinds = fuel[start : start + HALO, :].astype(jnp.float32)
        out[0:HALO, 0:FX] = level[start : start + HALO, :]
        out[0:HALO, FX:COLS] = jnp.where(lane < HALF, two, one)
        out[HALO : HALO + 40, 0:FX] = kinds[near : near + 40]
        out[HALO : HALO + 40, FX:COLS] = side[near : near + 40]
        out[fuel_at : fuel_at + 1, 0:FX] = kinds[more : more + 1]
        out[fuel_at : fuel_at + 1, FX:COLS] = side[more : more + 1]
        for k in range(4):
            row = flags_at + k
            out[row : row + 1, 0:FX] = jnp.full((1, FX), flag_of(active, k), jnp.float32)
            out[row : row + 1, FX:COLS] = jnp.where(
                lane[0:1] < HALF, from_right[FY + k : FY + k + 1, :], from_left[FY + k : FY + k + 1, :]
            )
        for c in range(6):
            at = (c // 3) * AY + coarse + c % 3
            out[wind_at : wind_at + 1, 128 * c : 128 * c + 128] = held[at : at + 1, :]


def rows(level, fuel, from_left, from_right, blocks, owner, active):
    shape = (HALO + 40, COLS)
    return pl.pallas_call(
        rows_kernel,
        in_specs=[VM] * 5 + [SM, SM],
        out_specs=[VM, VM, VM],
        out_shape=[f32(2 * AY + 8, 128), f32(*shape), f32(*shape)],
        compiler_params=SMALL,
        name="rows",
    )(level, fuel, from_left, from_right, blocks, owner, active)


def table(values):
    lane = lanes((8, 128))
    row = jnp.zeros((8, 128), jnp.float32)
    for c in range(values.shape[0]):
        row = jnp.where(lane == c, values[c], row)
    return row


def look(row, kinds):
    return jnp.take_along_axis(row, kinds, axis=1, mode="promise_in_bounds")


def values_kernel(
    fuel, from_left, from_right, after, fuel_rate, fuel_wind, fuel_heat, rate, drift, heat, three
):
    lane8 = lanes((8, 128))
    tables = [(table(fuel_rate), rate), (table(fuel_wind), drift), (table(fuel_heat), heat)]
    for i in range(3):
        three[8 * i : 8 * i + 8, :] = tables[i][0]

    def own_rows(i, _):
        at = pl.multiple_of(i * 8, 8)
        one = from_left[pl.ds(at, 8), :]
        two = from_right[pl.ds(at, 8), :]
        beside = pltpu.roll(jnp.where(lane8 < HALF, one, two), HALF, 1).astype(jnp.int32)
        for c in range(NL):
            kinds = beside if c == NL - 1 else fuel[pl.ds(at, 8), 128 * c : 128 * c + 128]
            for row, out in tables:
                out[pl.ds(at, 8), 128 * c : 128 * c + 128] = look(row, kinds)
        return 0

    lax.fori_loop(0, FY // 8, own_rows, 0, unroll=4)


def values(fuel, from_left, from_right, after, *names):
    return pl.pallas_call(
        values_kernel,
        in_specs=[VM, VM, VM, ANY, SM, SM, SM],
        out_specs=[VM] * 4,
        out_shape=[f32(FY, COLS)] * 3 + [f32(24, 128)],
        compiler_params=SMALL,
        name="values",
    )(fuel, from_left, from_right, after, *names)


def slab_kernel(
    level, from_left, from_right, from_up, from_down, held, rate, drift, heat, three,
    level_out, slots,
    phi_a, phi_b, phi_c, edge_rate, edge_drift, edge_heat, east, north, winds, gates, sums, spread, gather,
):
    group = lax.axis_index("grp")
    tile = lax.axis_index("tile")
    first_row = group == 0
    last_row = group == lax.axis_size("grp") - 1
    first_col = tile == 0
    last_col = tile == lax.axis_size("tile") - 1
    lane8 = lanes((8, 128))
    sub8 = lax.broadcasted_iota(jnp.int32, (8, COLS), 0)

    zero = jnp.zeros((PAD, COLS), jnp.float32)
    phi_a[0:PAD, :] = zero
    phi_a[ROWS - PAD : ROWS, :] = zero
    phi_a[TOP - HALO : TOP, :] = from_up[0:HALO, :]
    phi_a[TOP + FY : TOP + FY + HALO, :] = from_down[0:HALO, :]

    def own_rows(i, _):
        at = pl.multiple_of(i * 8, 8)
        to = pl.multiple_of(i * 8 + TOP, 8)
        phi_a[pl.ds(to, 8), 0:FX] = level[pl.ds(at, 8), :]
        one = from_left[pl.ds(at, 8), :]
        two = from_right[pl.ds(at, 8), :]
        phi_a[pl.ds(to, 8), FX:COLS] = jnp.where(lane8 < HALF, two, one)
        return 0

    lax.fori_loop(0, FY // 8, own_rows, 0, unroll=4)
    tables = [
        (three[8 * i : 8 * i + 8, :], out) for i, out in enumerate((edge_rate, edge_drift, edge_heat))
    ]

    def look_rows(source, to):
        for c in range(NL):
            kinds = source(128 * c).astype(jnp.int32)
            for row, out in tables:
                out[pl.ds(to, 8), 128 * c : 128 * c + 128] = look(row, kinds)

    def halo_rows(i, _):
        at = pl.multiple_of(i * 8 + HALO, 8)
        look_rows(lambda c: from_up[pl.ds(at, 8), c : c + 128], pl.multiple_of(i * 8 + 8, 8))
        look_rows(lambda c: from_down[pl.ds(at, 8), c : c + 128], at)
        return 0

    lax.fori_loop(0, 5, halo_rows, 0, unroll=5)
    for source, row, to in ((from_up, DOWN_ROWS[0], 0), (from_down, UP_ROWS[0], 2 * HALO - 8)):
        look_rows(lambda c: jnp.broadcast_to(source[row : row + 1, c : c + 128], (8, 128)), to)

    gates[0:4, :] = from_up[DOWN_ROWS[2] : DOWN_ROWS[2] + 4, :]
    gates[16:20, :] = from_down[UP_ROWS[2] : UP_ROWS[2] + 4, :]
    for c in range(FX // 128):
        gates[8:16, 128 * c : 128 * c + 128] = held[2 * AY : 2 * AY + 8, :]
    gates[8:16, FX:COLS] = jnp.where(
        lane8 < HALF, from_right[FY : FY + 8, :], from_left[FY : FY + 8, :]
    )

    above, under = DOWN_ROWS[1], UP_ROWS[1]
    for comp in range(2):
        base = comp * CR
        for c in range(3):
            at = 128 * (3 * comp + c)
            winds[base + c : base + c + 1, :] = from_up[above : above + 1, at : at + 128]
            below = base + 3 + AY + c
            winds[below : below + 1, :] = from_down[under : under + 1, at : at + 128]
        winds[base + 3 : base + 3 + AY, :] = held[AY * comp : AY * comp + AY, :]
        winds[base + 6 + AY : base + CR, :] = jnp.zeros((CR - 6 - AY, 128), jnp.float32)

    spread[...] = (
        coarse_lane(lanes((128, COLS))) == lax.broadcasted_iota(jnp.int32, (128, COLS), 0)
    ).astype(jnp.bfloat16)
    gather[...] = (
        coarse_lane(lax.broadcasted_iota(jnp.int32, (COLS, 128), 0)) == lanes((COLS, 128))
    ).astype(jnp.bfloat16)

    def expand():
        wide = exact_dot(winds[...], spread[...])
        east[...] = wide[0:CR]
        north[...] = wide[CR : 2 * CR]

    def edges(phi):
        @pl.when(first_row)
        def _():
            phi[TOP - 1 : TOP, :] = phi[TOP : TOP + 1, :]

        @pl.when(last_row)
        def _():
            phi[TOP + FY : TOP + FY + 1, :] = phi[TOP + FY - 1 : TOP + FY, :]

        @pl.when(first_col)
        def _():
            old = phi[:, COLS - 128 : COLS]
            new = jnp.broadcast_to(phi[:, 0:1], (ROWS, 128))
            phi[:, COLS - 128 : COLS] = jnp.where(lanes((ROWS, 128)) == 127, new, old)

        @pl.when(last_col)
        def _():
            old = phi[:, FX : FX + 128]
            new = jnp.broadcast_to(phi[:, FX - 1 : FX], (ROWS, 128))
            phi[:, FX : FX + 128] = jnp.where(lanes((ROWS, 128)) == 0, new, old)

    own = (rate, drift, heat, TOP)
    upper_edge = (edge_rate, edge_drift, edge_heat, TOP - HALO)
    lower_edge = (edge_rate, edge_drift, edge_heat, TOP + FY - HALO)

    def update(phi, at, e, n, gate, fuels, cols=COLS):
        before = phi[pl.ds(pl.multiple_of(at - 8, 8), 8), :]
        now = phi[pl.ds(at, 8), :]
        after = phi[pl.ds(pl.multiple_of(at + 8, 8), 8), :]
        west = pltpu.roll(now, 1, 1)[:, 0:cols]
        east_cell = pltpu.roll(now, COLS - 1, 1)[:, 0:cols]
        before, now, after = before[:, 0:cols], now[:, 0:cols], after[:, 0:cols]
        e, n, gate, sub = e[:, 0:cols], n[:, 0:cols], gate[:, 0:cols], sub8[:, 0:cols]
        south = jnp.where(sub == 0, pltpu.roll(before, 1, 0), pltpu.roll(now, 1, 0))
        above = jnp.where(sub == 7, pltpu.roll(after, 7, 0), pltpu.roll(now, 7, 0))
        back_x = now - west
        ahead_x = east_cell - now
        back_y = now - south
        ahead_y = above - now
        bx = jnp.maximum(back_x, 0.0)
        ax = jnp.minimum(ahead_x, 0.0)
        by = jnp.maximum(back_y, 0.0)
        ay = jnp.minimum(ahead_y, 0.0)
        square = bx * bx + ax * ax + by * by + ay * ay + 1e-12
        slope = square * lax.rsqrt(square)
        carry = e * jnp.where(e > 0.0, back_x, ahead_x) + n * jnp.where(n > 0.0, back_y, ahead_y)
        there = pl.multiple_of(at - fuels[3], 8)
        change = fuels[0][pl.ds(there, 8), 0:cols] * slope + fuels[1][pl.ds(there, 8), 0:cols] * carry
        return now - gate * change

    def wind_row(ref, row):
        return jnp.broadcast_to(ref[pl.ds(row, 1), :], (8, COLS))

    def mix(a, b):
        return jnp.where(sub8 < 4, a, b)

    def band(phi, m, k, region, fuels, finish, cols=COLS):
        at = pl.multiple_of(2 * PAD + 40 * m, 8)
        gate = jnp.broadcast_to(gates[region * 8 + k : region * 8 + k + 1, :], (8, COLS))
        row = 2 * m + 1
        for t in range(5):
            if t == 2:
                e = mix(wind_row(east, row), wind_row(east, row + 1))
                n = mix(wind_row(north, row), wind_row(north, row + 1))
            else:
                e, n = (wind_row(ref, row + t // 3) for ref in (east, north))
            here = pl.multiple_of(at + 8 * t, 8)
            finish(here, update(phi, here, e, n, gate, fuels, cols), fuels)

    def tile_rows(phi, at, row, region, k, fuels):
        gate = jnp.broadcast_to(gates[region * 8 + k : region * 8 + k + 1, :], (8, COLS))
        return update(phi, at, wind_row(east, row), wind_row(north, row), gate, fuels)

    def own_bands(body):
        def step(m, _):
            body(m, 1, own)
            return 0

        lax.fori_loop(1, 9, step, 0, unroll=8)

    def store_to(out):
        def finish(here, new, fuels):
            out[pl.ds(here, 8), :] = new

        return finish

    def flux_band(before, phi, out, k):
        cols = COLS if out is not None else FX

        def body(m, region, fuels):
            parts = []

            def finish(here, new, fuels):
                if out is not None:
                    out[pl.ds(here, 8), :] = new
                else:
                    level_out[pl.ds(pl.multiple_of(here - TOP, 8), 8), :] = new
                old = before[pl.ds(here, 8), 0:cols]
                there = pl.multiple_of(here - fuels[3], 8)
                parts.append(fuels[2][pl.ds(there, 8), 0:cols] * (jnp.tanh(old) - jnp.tanh(new)))

            band(phi, m, k, region, fuels, finish, cols)
            low = parts[0] + parts[1] + jnp.where(sub8[:, 0:cols] < 4, parts[2], 0.0)
            high = parts[3] + parts[4] + jnp.where(sub8[:, 0:cols] >= 4, parts[2], 0.0)
            sums[pl.ds(2 * m + 1, 1), 0:cols] = jnp.sum(low, axis=0, keepdims=True)
            sums[pl.ds(2 * m + 2, 1), 0:cols] = jnp.sum(high, axis=0, keepdims=True)

        return body

    def pooled():
        return exact_dot(sums[...], gather[...]) * (0.5 / (R * R))

    lane_c = lanes((CR, 128))
    row_c = lax.broadcasted_iota(jnp.int32, (CR, 128), 0)
    sums[...] = jnp.zeros((CR, COLS), jnp.float32)

    expand()
    edges(phi_a)
    phi_b[PAD : PAD + 8, :] = tile_rows(phi_a, PAD, 0, 0, 0, upper_edge)
    phi_b[ROWS - 2 * PAD : ROWS - PAD, :] = tile_rows(phi_a, ROWS - 2 * PAD, AY + 5, 2, 0, lower_edge)
    band(phi_a, 0, 0, 0, upper_edge, store_to(phi_b))
    band(phi_a, 9, 0, 2, lower_edge, store_to(phi_b))
    own_bands(lambda m, region, fuels: band(phi_a, m, 0, region, fuels, store_to(phi_b)))
    edges(phi_b)
    second = flux_band(phi_a, phi_b, phi_c, 1)
    second(0, 0, upper_edge)
    second(9, 2, lower_edge)
    own_bands(second)
    edges(phi_c)

    flux0 = pooled()
    ahead = jnp.where(jnp.logical_or(lane_c == AX - 1, lane_c == LEFT), flux0, pltpu.roll(flux0, 127, 1))
    back = jnp.where(jnp.logical_or(lane_c == 0, lane_c == RIGHT), flux0, pltpu.roll(flux0, 1, 1))
    last_rows = jnp.logical_or(row_c == 2, row_c == AY + 2)
    first_rows = jnp.logical_or(row_c == 3, row_c == AY + 3)
    below = jnp.where(last_rows, flux0, pltpu.roll(flux0, CR - 1, 0))
    upper = jnp.where(first_rows, flux0, pltpu.roll(flux0, 1, 0))
    winds[0:CR, :] = 0.9 * winds[0:CR, :] + 20.0 * (ahead - back)
    winds[CR : 2 * CR, :] = 0.9 * winds[CR : 2 * CR, :] + 20.0 * (below - upper)
    expand()

    top = TOP - 8
    bottom = TOP + FY
    phi_b[top : top + 8, :] = tile_rows(phi_c, top, 2, 0, 2, upper_edge)
    phi_b[bottom : bottom + 8, :] = tile_rows(phi_c, bottom, AY + 3, 2, 2, lower_edge)
    own_bands(lambda m, region, fuels: band(phi_c, m, 2, region, fuels, store_to(phi_b)))
    edges(phi_b)
    own_bands(flux_band(phi_c, phi_b, None, 3))
    total = 0.9 * flux0 + pooled()

    packed = jnp.zeros((4, 128), jnp.float32)
    lane4 = lanes((4, 128))
    for q in range(4):
        moved = pltpu.roll(total, 32 * q, 1)[3 + 4 * q : 7 + 4 * q]
        packed = jnp.where(lane4 // AX == q, moved, packed)
    for k in range(NX * NZ):
        slots[k] = packed


def slab(*args):
    big = pltpu.VMEM((ROWS, COLS), jnp.float32)
    edge = pltpu.VMEM((2 * HALO, COLS), jnp.float32)
    return pl.pallas_call(
        slab_kernel,
        in_specs=[VM] * 10,
        out_specs=[VM, VM],
        out_shape=[f32(FY, FX), f32(NX * NZ, 4, 128)],
        scratch_shapes=[big] * 3
        + [edge] * 3
        + [
            pltpu.VMEM((CR, COLS), jnp.float32),
            pltpu.VMEM((CR, COLS), jnp.float32),
            pltpu.VMEM((2 * CR, 128), jnp.float32),
            pltpu.VMEM((CR, COLS), jnp.float32),
            pltpu.VMEM((CR, COLS), jnp.float32),
            pltpu.VMEM((128, COLS), jnp.bfloat16),
            pltpu.VMEM((COLS, 128), jnp.bfloat16),
        ],
        compiler_params=LARGE,
        name="slab",
    )(*args)


def final_kernel(owner, received, wind, wind_out):
    tile = lax.axis_index("tile")
    source = jnp.int32(0)
    for t in range(NX * NZ):
        source = jnp.where(owner[0, t] == tile, t, source)
    block = received[source]
    flux = jnp.concatenate([pltpu.roll(block, (128 - 32 * q) % 128, 1) for q in range(4)], axis=0)
    lane = lanes((AY, 128))
    row = lax.broadcasted_iota(jnp.int32, (AY, 128), 0)
    ahead = jnp.where(lane == AX - 1, flux, pltpu.roll(flux, 127, 1))
    back = jnp.where(lane == 0, flux, pltpu.roll(flux, 1, 1))
    below = jnp.where(row == AY - 1, flux, pltpu.roll(flux, AY - 1, 0))
    upper = jnp.where(row == 0, flux, pltpu.roll(flux, 1, 0))
    wind_out[0] = 0.81 * wind[0] + 20.0 * (ahead - back)[:, 0:AX]
    wind_out[1] = 0.81 * wind[1] + 20.0 * (below - upper)[:, 0:AX]


def final(owner, received, wind):
    return pl.pallas_call(
        final_kernel, in_specs=[SM, VM, VM], out_specs=VM, out_shape=f32(2, AY, AX),
        compiler_params=SMALL, name="final"
    )(owner, received, wind)


def shift(value, axis, step):
    size = lax.axis_size(axis)
    pairs = [(i, i + step) for i in range(size) if 0 <= i + step < size]
    return lax.ppermute(value, axis, pairs)


def shards(level, fuel, wind, owner, active, fuel_rate, fuel_wind, fuel_heat):
    active = jnp.transpose(active, (1, 2, 0))
    mine = blocks_of(wind)
    blocks = lax.all_to_all(mine, "tile", 0, 0, tiled=True)
    stay = [pltpu.with_memory_space_constraint(value, pltpu.HBM) for value in (level, fuel, active, mine)]
    to_left, to_right = strips(*stay)
    from_right = shift(to_left, "tile", -1)
    from_left = shift(to_right, "tile", 1)
    held, to_up, to_down = rows(level, fuel, from_left, from_right, blocks, owner, active)
    from_down = shift(to_up, "grp", -1)
    from_up = shift(to_down, "grp", 1)
    coefficients = values(fuel, from_left, from_right, held, fuel_rate, fuel_wind, fuel_heat)
    level_out, flux = slab(level, from_left, from_right, from_up, from_down, held, *coefficients)
    flux = lax.all_to_all(flux, "tile", 0, 0, tiled=True)
    return (level_out, final(owner, flux, wind))


def solution(mesh):
    in_specs = (
        P("grp", "tile"),
        P("grp", "tile"),
        P(None, "grp", "tile"),
        P("grp", None),
        P(None, "grp", "tile"),
        P(),
        P(),
        P(),
    )
    out_specs = (P("grp", "tile"), P(None, "grp", "tile"))
    return jax.shard_map(shards, mesh=mesh, in_specs=in_specs, out_specs=out_specs, check_vma=False)
```

```python
import jax
import jax.numpy as jnp
from jax import lax
from jax.experimental import pallas as pl
from jax.experimental.pallas import tpu as pltpu
from jax.sharding import PartitionSpec as P

R = 20
AY = 16
AX = 32
FY = 320
FX = 640
STEPS = 2
SUBSTEPS = 2
NZ = 16
NX = 4
HALO = 48
HALF = 64
PAD = 8
TOP = PAD + HALO
ROWS = TOP + FY + HALO + PAD
COLS = FX + 2 * HALF
NL = COLS // 128
RIGHT = 40
LEFT = 51
CR = 24
UP_ROWS = (42, 43, 44)
DOWN_ROWS = (5, 4, 0)

VM = pl.BlockSpec(memory_space=pltpu.VMEM)
SM = pl.BlockSpec(memory_space=pltpu.SMEM)
ANY = pl.BlockSpec(memory_space=pl.ANY)
SMALL = pltpu.CompilerParams(vmem_limit_bytes=4 * 1024 * 1024)
LARGE = pltpu.CompilerParams(vmem_limit_bytes=12 * 1024 * 1024)


def lanes(shape):
    return lax.broadcasted_iota(jnp.int32, shape, 1)


def f32(*shape):
    return jax.ShapeDtypeStruct(shape, jnp.float32)


def thirds(x):
    high = x.astype(jnp.bfloat16)
    rest = x - high.astype(jnp.float32)
    middle = rest.astype(jnp.bfloat16)
    low = (rest - middle.astype(jnp.float32)).astype(jnp.bfloat16)
    return jnp.concatenate([high, middle, low], axis=0)


def exact_dot(x, onehot):
    n = x.shape[0]
    out = jnp.dot(thirds(x), onehot, preferred_element_type=jnp.float32)
    return out[:n] + out[n : 2 * n] + out[2 * n :]


def coarse_lane(fine):
    own = fine // R
    right = RIGHT + (fine - FX) // R
    left = LEFT - (COLS - 1 - fine) // R
    edge = jnp.where(fine < FX + 3 * R, right, jnp.where(fine >= COLS - 3 * R, left, -1))
    return jnp.where(fine < FX, own, edge)


def strips_kernel(level, fuel, active, after, to_left, to_right, left_level, right_level, left_fuel, right_fuel, arrived):
    first, last = pl.ds(0, 128), pl.ds(FX - 128, 128)
    moves = [
        pltpu.make_async_copy(source.at[:, part], buf, arrived.at[i])
        for i, (source, part, buf) in enumerate((
            (level, first, left_level), (fuel, first, left_fuel),
            (level, last, right_level), (fuel, last, right_fuel),
        ))
    ]
    for move in moves:
        move.start()
    for k in range(8):
        row = jnp.full((1, 128), flag_of(active, k), jnp.float32)
        to_left[FY + k : FY + k + 1, :] = row
        to_right[FY + k : FY + k + 1, :] = row
    lane = lanes((FY, 128))
    moves[0].wait()
    moves[1].wait()
    to_left[0:FY, :] = jnp.where(
        lane < HALF, left_level[...], pltpu.roll(left_fuel[...].astype(jnp.float32), HALF, 1)
    )
    moves[2].wait()
    moves[3].wait()
    to_right[0:FY, :] = jnp.where(
        lane >= HALF, right_level[...], pltpu.roll(right_fuel[...].astype(jnp.float32), HALF, 1)
    )


def strips(level, fuel, active, after):
    strip = pltpu.VMEM((FY, 128), jnp.float32)
    kinds = pltpu.VMEM((FY, 128), jnp.int32)
    return pl.pallas_call(
        strips_kernel,
        in_specs=[ANY, ANY, SM, ANY],
        out_specs=[VM, VM],
        out_shape=[f32(FY + 8, 128), f32(FY + 8, 128)],
        scratch_shapes=[strip, strip, kinds, kinds, pltpu.SemaphoreType.DMA((4,))],
        compiler_params=SMALL,
        name="strips",
    )(level, fuel, active, after)


def flag_of(active, k):
    return (active[0, 0, min(k, STEPS * SUBSTEPS - 1)] > 0).astype(jnp.float32)


def blocks_kernel(wind, slots):
    parts = [wind[0, 0:8, :], wind[0, 8:16, :], wind[1, 0:8, :], wind[1, 8:16, :]]
    block = jnp.concatenate(parts, axis=1)
    for k in range(NX * NZ):
        slots[k] = block


def blocks_of(wind):
    return pl.pallas_call(
        blocks_kernel, in_specs=[VM], out_specs=VM, out_shape=f32(NX * NZ, 8, 128), name="blocks"
    )(wind)


def rows_kernel(
    level, fuel, from_left, from_right, blocks, owner, active, held, to_up, to_down,
):
    tile = lax.axis_index("tile")
    lane = lanes((HALO, 128))
    lane8 = lanes((8, 128))
    main = blocks[owner[0, tile]]
    left = blocks[owner[0, jnp.maximum(tile - 1, 0)]]
    right = blocks[owner[0, jnp.minimum(tile + 1, NX * NZ - 1)]]
    is_left = jnp.logical_and(lane8 >= LEFT - 2, lane8 <= LEFT)
    is_right = jnp.logical_and(lane8 >= RIGHT, lane8 <= RIGHT + 2)
    for q in range(4):
        own = pltpu.roll(main, (128 - 32 * q) % 128, 1)
        one = pltpu.roll(left, (LEFT - 31 - 32 * q) % 128, 1)
        two = pltpu.roll(right, (RIGHT - 32 * q) % 128, 1)
        held[8 * q : 8 * q + 8, :] = jnp.where(
            lane8 < AX, own, jnp.where(is_left, one, jnp.where(is_right, two, 0.0))
        )
    for k in range(8):
        held[2 * AY + k : 2 * AY + k + 1, :] = jnp.full((1, 128), flag_of(active, k), jnp.float32)
    for out, start, near, more, coarse, (fuel_at, wind_at, flags_at) in (
        (to_up, 0, 0, 40, 0, UP_ROWS),
        (to_down, FY - HALO, 8, 7, AY - 3, DOWN_ROWS),
    ):
        one = from_left[start : start + HALO, :]
        two = from_right[start : start + HALO, :]
        side = pltpu.roll(jnp.where(lane < HALF, one, two), HALF, 1)
        kinds = fuel[start : start + HALO, :].astype(jnp.float32)
        out[0:HALO, 0:FX] = level[start : start + HALO, :]
        out[0:HALO, FX:COLS] = jnp.where(lane < HALF, two, one)
        out[HALO : HALO + 40, 0:FX] = kinds[near : near + 40]
        out[HALO : HALO + 40, FX:COLS] = side[near : near + 40]
        out[fuel_at : fuel_at + 1, 0:FX] = kinds[more : more + 1]
        out[fuel_at : fuel_at + 1, FX:COLS] = side[more : more + 1]
        for k in range(4):
            row = flags_at + k
            out[row : row + 1, 0:FX] = jnp.full((1, FX), flag_of(active, k), jnp.float32)
            out[row : row + 1, FX:COLS] = jnp.where(
                lane[0:1] < HALF, from_right[FY + k : FY + k + 1, :], from_left[FY + k : FY + k + 1, :]
            )
        for c in range(6):
            at = (c // 3) * AY + coarse + c % 3
            out[wind_at : wind_at + 1, 128 * c : 128 * c + 128] = held[at : at + 1, :]


def rows(level, fuel, from_left, from_right, blocks, owner, active):
    shape = (HALO + 40, COLS)
    return pl.pallas_call(
        rows_kernel,
        in_specs=[VM] * 5 + [SM, SM],
        out_specs=[VM, VM, VM],
        out_shape=[f32(2 * AY + 8, 128), f32(*shape), f32(*shape)],
        compiler_params=SMALL,
        name="rows",
    )(level, fuel, from_left, from_right, blocks, owner, active)


def table(values):
    lane = lanes((8, 128))
    row = jnp.zeros((8, 128), jnp.float32)
    for c in range(values.shape[0]):
        row = jnp.where(lane == c, values[c], row)
    return row


def look(row, kinds):
    return jnp.take_along_axis(row, kinds, axis=1, mode="promise_in_bounds")


def values_kernel(
    fuel, from_left, from_right, after, fuel_rate, fuel_wind, fuel_heat, rate, drift, heat, three
):
    lane8 = lanes((8, 128))
    tables = [(table(fuel_rate), rate), (table(fuel_wind), drift), (table(fuel_heat), heat)]
    for i in range(3):
        three[8 * i : 8 * i + 8, :] = tables[i][0]

    def own_rows(i, _):
        at = pl.multiple_of(i * 8, 8)
        one = from_left[pl.ds(at, 8), :]
        two = from_right[pl.ds(at, 8), :]
        beside = pltpu.roll(jnp.where(lane8 < HALF, one, two), HALF, 1).astype(jnp.int32)
        for c in range(NL):
            kinds = beside if c == NL - 1 else fuel[pl.ds(at, 8), 128 * c : 128 * c + 128]
            for row, out in tables:
                out[pl.ds(at, 8), 128 * c : 128 * c + 128] = look(row, kinds)
        return 0

    lax.fori_loop(0, FY // 8, own_rows, 0, unroll=8)


def values(fuel, from_left, from_right, after, *names):
    return pl.pallas_call(
        values_kernel,
        in_specs=[VM, VM, VM, ANY, SM, SM, SM],
        out_specs=[VM] * 4,
        out_shape=[f32(FY, COLS)] * 3 + [f32(24, 128)],
        compiler_params=SMALL,
        name="values",
    )(fuel, from_left, from_right, after, *names)


def slab_kernel(
    level, from_left, from_right, from_up, from_down, held, rate, drift, heat, three,
    level_out, slots,
    phi_a, phi_b, phi_c, edge_rate, edge_drift, edge_heat, east, north, winds, gates, sums, spread, gather,
):
    group = lax.axis_index("grp")
    tile = lax.axis_index("tile")
    first_row = group == 0
    last_row = group == lax.axis_size("grp") - 1
    first_col = tile == 0
    last_col = tile == lax.axis_size("tile") - 1
    lane8 = lanes((8, 128))
    sub8 = lax.broadcasted_iota(jnp.int32, (8, COLS), 0)

    zero = jnp.zeros((PAD, COLS), jnp.float32)
    phi_a[0:PAD, :] = zero
    phi_a[ROWS - PAD : ROWS, :] = zero
    phi_a[TOP - HALO : TOP, :] = from_up[0:HALO, :]
    phi_a[TOP + FY : TOP + FY + HALO, :] = from_down[0:HALO, :]

    def own_rows(i, _):
        at = pl.multiple_of(i * 8, 8)
        to = pl.multiple_of(i * 8 + TOP, 8)
        phi_a[pl.ds(to, 8), 0:FX] = level[pl.ds(at, 8), :]
        one = from_left[pl.ds(at, 8), :]
        two = from_right[pl.ds(at, 8), :]
        phi_a[pl.ds(to, 8), FX:COLS] = jnp.where(lane8 < HALF, two, one)
        return 0

    lax.fori_loop(0, FY // 8, own_rows, 0, unroll=8)
    tables = [
        (three[8 * i : 8 * i + 8, :], out) for i, out in enumerate((edge_rate, edge_drift, edge_heat))
    ]

    def look_rows(source, to):
        for c in range(NL):
            kinds = source(128 * c).astype(jnp.int32)
            for row, out in tables:
                out[pl.ds(to, 8), 128 * c : 128 * c + 128] = look(row, kinds)

    def halo_rows(i, _):
        at = pl.multiple_of(i * 8 + HALO, 8)
        look_rows(lambda c: from_up[pl.ds(at, 8), c : c + 128], pl.multiple_of(i * 8 + 8, 8))
        look_rows(lambda c: from_down[pl.ds(at, 8), c : c + 128], at)
        return 0

    lax.fori_loop(0, 5, halo_rows, 0, unroll=5)
    for source, row, to in ((from_up, DOWN_ROWS[0], 0), (from_down, UP_ROWS[0], 2 * HALO - 8)):
        look_rows(lambda c: jnp.broadcast_to(source[row : row + 1, c : c + 128], (8, 128)), to)

    gates[0:4, :] = from_up[DOWN_ROWS[2] : DOWN_ROWS[2] + 4, :]
    gates[16:20, :] = from_down[UP_ROWS[2] : UP_ROWS[2] + 4, :]
    for c in range(FX // 128):
        gates[8:16, 128 * c : 128 * c + 128] = held[2 * AY : 2 * AY + 8, :]
    gates[8:16, FX:COLS] = jnp.where(
        lane8 < HALF, from_right[FY : FY + 8, :], from_left[FY : FY + 8, :]
    )

    above, under = DOWN_ROWS[1], UP_ROWS[1]
    for comp in range(2):
        base = comp * CR
        for c in range(3):
            at = 128 * (3 * comp + c)
            winds[base + c : base + c + 1, :] = from_up[above : above + 1, at : at + 128]
            below = base + 3 + AY + c
            winds[below : below + 1, :] = from_down[under : under + 1, at : at + 128]
        winds[base + 3 : base + 3 + AY, :] = held[AY * comp : AY * comp + AY, :]
        winds[base + 6 + AY : base + CR, :] = jnp.zeros((CR - 6 - AY, 128), jnp.float32)

    spread[...] = (
        coarse_lane(lanes((128, COLS))) == lax.broadcasted_iota(jnp.int32, (128, COLS), 0)
    ).astype(jnp.bfloat16)
    gather[...] = (
        coarse_lane(lax.broadcasted_iota(jnp.int32, (COLS, 128), 0)) == lanes((COLS, 128))
    ).astype(jnp.bfloat16)

    def expand():
        wide = exact_dot(winds[...], spread[...])
        east[...] = wide[0:CR]
        north[...] = wide[CR : 2 * CR]

    def edges(phi):
        @pl.when(first_row)
        def _():
            phi[TOP - 1 : TOP, :] = phi[TOP : TOP + 1, :]

        @pl.when(last_row)
        def _():
            phi[TOP + FY : TOP + FY + 1, :] = phi[TOP + FY - 1 : TOP + FY, :]

        @pl.when(first_col)
        def _():
            old = phi[:, COLS - 128 : COLS]
            new = jnp.broadcast_to(phi[:, 0:1], (ROWS, 128))
            phi[:, COLS - 128 : COLS] = jnp.where(lanes((ROWS, 128)) == 127, new, old)

        @pl.when(last_col)
        def _():
            old = phi[:, FX : FX + 128]
            new = jnp.broadcast_to(phi[:, FX - 1 : FX], (ROWS, 128))
            phi[:, FX : FX + 128] = jnp.where(lanes((ROWS, 128)) == 0, new, old)

    own = (rate, drift, heat, TOP)
    upper_edge = (edge_rate, edge_drift, edge_heat, TOP - HALO)
    lower_edge = (edge_rate, edge_drift, edge_heat, TOP + FY - HALO)

    def update(phi, at, e, n, gate, fuels, cols=COLS):
        before = phi[pl.ds(pl.multiple_of(at - 8, 8), 8), :]
        now = phi[pl.ds(at, 8), :]
        after = phi[pl.ds(pl.multiple_of(at + 8, 8), 8), :]
        west = pltpu.roll(now, 1, 1)[:, 0:cols]
        east_cell = pltpu.roll(now, COLS - 1, 1)[:, 0:cols]
        before, now, after = before[:, 0:cols], now[:, 0:cols], after[:, 0:cols]
        e, n, gate, sub = e[:, 0:cols], n[:, 0:cols], gate[:, 0:cols], sub8[:, 0:cols]
        south = jnp.where(sub == 0, pltpu.roll(before, 1, 0), pltpu.roll(now, 1, 0))
        above = jnp.where(sub == 7, pltpu.roll(after, 7, 0), pltpu.roll(now, 7, 0))
        back_x = now - west
        ahead_x = east_cell - now
        back_y = now - south
        ahead_y = above - now
        bx = jnp.maximum(back_x, 0.0)
        ax = jnp.minimum(ahead_x, 0.0)
        by = jnp.maximum(back_y, 0.0)
        ay = jnp.minimum(ahead_y, 0.0)
        square = bx * bx + ax * ax + by * by + ay * ay + 1e-12
        slope = square * lax.rsqrt(square)
        carry = e * jnp.where(e > 0.0, back_x, ahead_x) + n * jnp.where(n > 0.0, back_y, ahead_y)
        there = pl.multiple_of(at - fuels[3], 8)
        change = fuels[0][pl.ds(there, 8), 0:cols] * slope + fuels[1][pl.ds(there, 8), 0:cols] * carry
        return now - gate * change

    def wind_row(ref, row):
        return jnp.broadcast_to(ref[pl.ds(row, 1), :], (8, COLS))

    def mix(a, b):
        return jnp.where(sub8 < 4, a, b)

    def band(phi, m, k, region, fuels, finish, cols=COLS):
        at = pl.multiple_of(2 * PAD + 40 * m, 8)
        gate = jnp.broadcast_to(gates[region * 8 + k : region * 8 + k + 1, :], (8, COLS))
        row = 2 * m + 1
        for t in range(5):
            if t == 2:
                e = mix(wind_row(east, row), wind_row(east, row + 1))
                n = mix(wind_row(north, row), wind_row(north, row + 1))
            else:
                e, n = (wind_row(ref, row + t // 3) for ref in (east, north))
            here = pl.multiple_of(at + 8 * t, 8)
            finish(here, update(phi, here, e, n, gate, fuels, cols), fuels)

    def tile_rows(phi, at, row, region, k, fuels):
        gate = jnp.broadcast_to(gates[region * 8 + k : region * 8 + k + 1, :], (8, COLS))
        return update(phi, at, wind_row(east, row), wind_row(north, row), gate, fuels)

    def own_bands(body):
        def step(m, _):
            body(m, 1, own)
            return 0

        lax.fori_loop(1, 9, step, 0, unroll=8)

    def store_to(out):
        def finish(here, new, fuels):
            out[pl.ds(here, 8), :] = new

        return finish

    def flux_band(before, phi, out, k):
        cols = COLS if out is not None else FX

        def body(m, region, fuels):
            parts = []

            def finish(here, new, fuels):
                if out is not None:
                    out[pl.ds(here, 8), :] = new
                else:
                    level_out[pl.ds(pl.multiple_of(here - TOP, 8), 8), :] = new
                old = before[pl.ds(here, 8), 0:cols]
                there = pl.multiple_of(here - fuels[3], 8)
                parts.append(fuels[2][pl.ds(there, 8), 0:cols] * (jnp.tanh(old) - jnp.tanh(new)))

            band(phi, m, k, region, fuels, finish, cols)
            low = parts[0] + parts[1] + jnp.where(sub8[:, 0:cols] < 4, parts[2], 0.0)
            high = parts[3] + parts[4] + jnp.where(sub8[:, 0:cols] >= 4, parts[2], 0.0)
            sums[pl.ds(2 * m + 1, 1), 0:cols] = jnp.sum(low, axis=0, keepdims=True)
            sums[pl.ds(2 * m + 2, 1), 0:cols] = jnp.sum(high, axis=0, keepdims=True)

        return body

    def pooled():
        return exact_dot(sums[...], gather[...]) * (0.5 / (R * R))

    lane_c = lanes((CR, 128))
    row_c = lax.broadcasted_iota(jnp.int32, (CR, 128), 0)
    sums[...] = jnp.zeros((CR, COLS), jnp.float32)

    expand()
    edges(phi_a)
    phi_b[PAD : PAD + 8, :] = tile_rows(phi_a, PAD, 0, 0, 0, upper_edge)
    phi_b[ROWS - 2 * PAD : ROWS - PAD, :] = tile_rows(phi_a, ROWS - 2 * PAD, AY + 5, 2, 0, lower_edge)
    band(phi_a, 0, 0, 0, upper_edge, store_to(phi_b))
    band(phi_a, 9, 0, 2, lower_edge, store_to(phi_b))
    own_bands(lambda m, region, fuels: band(phi_a, m, 0, region, fuels, store_to(phi_b)))
    edges(phi_b)
    second = flux_band(phi_a, phi_b, phi_c, 1)
    second(0, 0, upper_edge)
    second(9, 2, lower_edge)
    own_bands(second)
    edges(phi_c)

    flux0 = pooled()
    ahead = jnp.where(jnp.logical_or(lane_c == AX - 1, lane_c == LEFT), flux0, pltpu.roll(flux0, 127, 1))
    back = jnp.where(jnp.logical_or(lane_c == 0, lane_c == RIGHT), flux0, pltpu.roll(flux0, 1, 1))
    last_rows = jnp.logical_or(row_c == 2, row_c == AY + 2)
    first_rows = jnp.logical_or(row_c == 3, row_c == AY + 3)
    below = jnp.where(last_rows, flux0, pltpu.roll(flux0, CR - 1, 0))
    upper = jnp.where(first_rows, flux0, pltpu.roll(flux0, 1, 0))
    winds[0:CR, :] = 0.9 * winds[0:CR, :] + 20.0 * (ahead - back)
    winds[CR : 2 * CR, :] = 0.9 * winds[CR : 2 * CR, :] + 20.0 * (below - upper)
    expand()

    top = TOP - 8
    bottom = TOP + FY
    phi_b[top : top + 8, :] = tile_rows(phi_c, top, 2, 0, 2, upper_edge)
    phi_b[bottom : bottom + 8, :] = tile_rows(phi_c, bottom, AY + 3, 2, 2, lower_edge)
    own_bands(lambda m, region, fuels: band(phi_c, m, 2, region, fuels, store_to(phi_b)))
    edges(phi_b)
    own_bands(flux_band(phi_c, phi_b, None, 3))
    total = 0.9 * flux0 + pooled()

    packed = jnp.zeros((4, 128), jnp.float32)
    lane4 = lanes((4, 128))
    for q in range(4):
        moved = pltpu.roll(total, 32 * q, 1)[3 + 4 * q : 7 + 4 * q]
        packed = jnp.where(lane4 // AX == q, moved, packed)
    for k in range(NX * NZ):
        slots[k] = packed


def slab(*args):
    big = pltpu.VMEM((ROWS, COLS), jnp.float32)
    edge = pltpu.VMEM((2 * HALO, COLS), jnp.float32)
    return pl.pallas_call(
        slab_kernel,
        in_specs=[VM] * 10,
        out_specs=[VM, VM],
        out_shape=[f32(FY, FX), f32(NX * NZ, 4, 128)],
        scratch_shapes=[big] * 3
        + [edge] * 3
        + [
            pltpu.VMEM((CR, COLS), jnp.float32),
            pltpu.VMEM((CR, COLS), jnp.float32),
            pltpu.VMEM((2 * CR, 128), jnp.float32),
            pltpu.VMEM((CR, COLS), jnp.float32),
            pltpu.VMEM((CR, COLS), jnp.float32),
            pltpu.VMEM((128, COLS), jnp.bfloat16),
            pltpu.VMEM((COLS, 128), jnp.bfloat16),
        ],
        compiler_params=LARGE,
        name="slab",
    )(*args)


def final_kernel(owner, received, wind, wind_out):
    tile = lax.axis_index("tile")
    source = jnp.int32(0)
    for t in range(NX * NZ):
        source = jnp.where(owner[0, t] == tile, t, source)
    block = received[source]
    flux = jnp.concatenate([pltpu.roll(block, (128 - 32 * q) % 128, 1) for q in range(4)], axis=0)
    lane = lanes((AY, 128))
    row = lax.broadcasted_iota(jnp.int32, (AY, 128), 0)
    ahead = jnp.where(lane == AX - 1, flux, pltpu.roll(flux, 127, 1))
    back = jnp.where(lane == 0, flux, pltpu.roll(flux, 1, 1))
    below = jnp.where(row == AY - 1, flux, pltpu.roll(flux, AY - 1, 0))
    upper = jnp.where(row == 0, flux, pltpu.roll(flux, 1, 0))
    wind_out[0] = 0.81 * wind[0] + 20.0 * (ahead - back)[:, 0:AX]
    wind_out[1] = 0.81 * wind[1] + 20.0 * (below - upper)[:, 0:AX]


def final(owner, received, wind):
    return pl.pallas_call(
        final_kernel, in_specs=[SM, VM, VM], out_specs=VM, out_shape=f32(2, AY, AX),
        compiler_params=SMALL, name="final"
    )(owner, received, wind)


def shift(value, axis, step):
    size = lax.axis_size(axis)
    pairs = [(i, i + step) for i in range(size) if 0 <= i + step < size]
    return lax.ppermute(value, axis, pairs)


def shards(level, fuel, wind, owner, active, fuel_rate, fuel_wind, fuel_heat):
    active = jnp.transpose(active, (1, 2, 0))
    mine = blocks_of(wind)
    blocks = lax.all_to_all(mine, "tile", 0, 0, tiled=True)
    stay = [pltpu.with_memory_space_constraint(value, pltpu.HBM) for value in (level, fuel, active, mine)]
    to_left, to_right = strips(*stay)
    from_right = shift(to_left, "tile", -1)
    from_left = shift(to_right, "tile", 1)
    held, to_up, to_down = rows(level, fuel, from_left, from_right, blocks, owner, active)
    from_down = shift(to_up, "grp", -1)
    from_up = shift(to_down, "grp", 1)
    coefficients = values(fuel, from_left, from_right, held, fuel_rate, fuel_wind, fuel_heat)
    level_out, flux = slab(level, from_left, from_right, from_up, from_down, held, *coefficients)
    flux = lax.all_to_all(flux, "tile", 0, 0, tiled=True)
    return (level_out, final(owner, flux, wind))


def solution(mesh):
    in_specs = (
        P("grp", "tile"),
        P("grp", "tile"),
        P(None, "grp", "tile"),
        P("grp", None),
        P(None, "grp", "tile"),
        P(),
        P(),
        P(),
    )
    out_specs = (P("grp", "tile"), P(None, "grp", "tile"))
    return jax.shard_map(shards, mesh=mesh, in_specs=in_specs, out_specs=out_specs, check_vma=False)
```
